256 devices in a mesh: lev: 16 (over y, z_lo, core), lat: 16 (over x, z_hi).
Axes of the slice: x: 4, y: 4, z: 8 (z_hi: 4, z_lo: 2; z = z_hi * 2 + z_lo), core: 2. Of those that a mesh axis runs over, the one named last changes fastest.
Arguments:
- fields: bfloat16 [128, 768, 3072], P('lat', None, 'lev'), may hold values from -6 to 6
- level_group: int32 [128], replicated, may hold values from 0 to 2
- lat_start: int32 [128], replicated, may hold values from 0 to 115, as said below
- w_embed: bfloat16 [3072, 768], P('lev'), may hold values from -0.1875 to 0.1875
- group_bias: float32 [3, 768], replicated, may hold values from -4 to 4
- group_gain: float32 [3, 768], replicated, may hold values from 0.5 to 2
- norm_gain: float32 [768], replicated, may hold values from 0.1 to 1.9
- w_qkv: bfloat16 [768, 2304], replicated, may hold values from -3 to 3
- w_out: bfloat16 [768, 768], replicated, may hold values from -0.21875 to 0.21875
Outputs:
- encoded: bfloat16 [128, 768, 768], P('lat', 'lev')
The draws below stay inside these ranges and needn't reach their ends.
Inputs may be any that keep to these rules, and one draw needn't show every extreme that they name: lat_start[i] lies from i - 8 to i - 4, moved into 0 to 115 at the ends of the grid.
All inputs are finite; a program needn't handle non-finite values.
Results may differ from the reference program's by a relative error of at most 0.0025.
The reference program's roundings to bfloat16 on the way count: a program that leaves them out, or rounds other values in their place, can miss the bound.
Values may be sent and summed in bfloat16 or wider, within the bound.
No kernel may reach another device: no remote copies, remote signals or barrier semaphores. Data moves between devices by JAX's collectives and lax.ppermute only.
A program may use at most 256 MiB of HBM per device.

```python
import math
import jax
import jax.numpy as jnp
from jax import lax

D = 768
H = 12
DH = 64
L = 128
IN_LEV = 24
G = 3
WIN = 13
LAT_REACH = 8
LAT = 128
LON = 768


def draw_lat_start(key, part):
    lat_rows = jnp.arange(LAT, dtype=jnp.int32)
    jitter = jax.random.randint(key, (LAT,), 0, 2 * LAT_REACH - WIN + 2, dtype=jnp.int32)
    return jnp.clip(lat_rows - LAT_REACH + jitter, 0, LAT - WIN).astype(jnp.int32)


def draw_w_qkv(key, part):
    base_key = jax.random.fold_in(key, 0)
    matrix = jax.random.truncated_normal(base_key, -6.0, 6.0, (D, 3 * D), jnp.float32) * D ** (-0.5)
    return matrix.astype(jnp.bfloat16)


def set_ends(entries, own_key, smallest, largest):
    longest = entries.shape.index(max(entries.shape))
    spots = []
    for shift in (0, 1):
        where = [jax.random.randint(jax.random.fold_in(own_key, axis), (), 0, length) for axis, length in enumerate(entries.shape)]
        where[longest] = (where[longest] + shift) % entries.shape[longest]
        spots.append(tuple(where))
    return entries.at[spots[0]].set(smallest).at[spots[1]].set(largest)


def steps_of(stream_key, dims, pieces, low, top_value):
    def one(dim, blocks):
        steps = jax.random.uniform(jax.random.fold_in(jax.random.fold_in(stream_key, 6), dim), (blocks,), jnp.float32, low / len(pieces), top_value / len(pieces))
        return jnp.repeat(jnp.exp(steps), dims[dim] // blocks).reshape((-1,) + (1,) * (len(dims) - dim - 1))

    loudness = one(*pieces[0])
    for cut in pieces[1:]:
        loudness = loudness * one(*cut)
    return loudness


def gaussian(key, shape, deviation, most, pieces=(), kind=jnp.bfloat16):
    array = deviation * jax.random.normal(key, shape, jnp.float32)
    if pieces:
        array = array * steps_of(key, shape, pieces, -0.22, 0.18)
    return jnp.clip(array, -most, most).astype(kind)


def setup_inputs(seed: int = 0) -> dict:
    streams_of = jax.random.split(jax.random.key(seed), 10)
    fields = gaussian(streams_of[0], (LAT, LON, L * IN_LEV), 1.0, 6.0, ((0, 16), (2, 16)))
    level_group = set_ends(jax.random.randint(streams_of[1], (L,), 0, G), jax.random.fold_in(streams_of[1], 1), 0, G - 1).astype(jnp.int32)
    lat_start = draw_lat_start(jax.random.fold_in(streams_of[9], 71), 0)
    w_embed = gaussian(streams_of[3], (L * IN_LEV, D), (L * IN_LEV // G) ** -0.5, 0.1875, ((0, 16),))
    group_bias = gaussian(streams_of[4], (G, D), 1.0, 4.0, (), jnp.float32)
    group_gain = jnp.clip(jnp.exp(jax.random.uniform(streams_of[5], (G, D), jnp.float32, math.log(0.5), math.log(2.0))), 0.5, 2.0)
    norm_gain = jnp.clip(1.0 + 0.18 * jax.random.normal(streams_of[6], (D,), jnp.float32), 0.1, 1.9)
    w_qkv = draw_w_qkv(jax.random.fold_in(streams_of[9], 71), 0)
    w_out = gaussian(streams_of[8], (D, D), D ** -0.5, 0.21875)
    return {"fields": fields, "level_group": level_group, "lat_start": lat_start, "w_embed": w_embed, "group_bias": group_bias, "group_gain": group_gain, "norm_gain": norm_gain, "w_qkv": w_qkv, "w_out": w_out}


def grouped(weight_rows, row_groups, group_count):
    chosen = row_groups[:, None] == jnp.arange(group_count, dtype=jnp.int32)[None, :]
    stacked = jnp.where(chosen[:, :, None], weight_rows[:, None, :], jnp.zeros((), weight_rows.dtype))
    return stacked.reshape(weight_rows.shape[0], group_count * weight_rows.shape[1])

def reference(fields, level_group, lat_start, w_embed, group_bias, group_gain, norm_gain, w_qkv, w_out):
    row_groups = jnp.broadcast_to(level_group[:, None], (L, IN_LEV)).reshape(L * IN_LEV).astype(jnp.int32)
    w_grouped = grouped(w_embed, row_groups, G)

    def embed_line(lat_line):
        summed = jnp.dot(lat_line, w_grouped, preferred_element_type=jnp.float32).reshape(LON, G, D)
        activated = jax.nn.silu(summed + group_bias) * group_gain
        return lax.optimization_barrier(jnp.sum(activated, axis=1)).astype(jnp.bfloat16)
    embedded = lax.map(embed_line, fields)
    embed_wide = embedded.astype(jnp.float32)
    inv_rms = lax.rsqrt(lax.optimization_barrier(jnp.mean(embed_wide * embed_wide, axis=-1, keepdims=True)) + 1e-05)
    normed = (embed_wide * inv_rms * norm_gain).astype(jnp.bfloat16)

    def project_line(lat_line):
        return jnp.dot(lat_line, w_qkv, preferred_element_type=jnp.float32).astype(jnp.bfloat16)
    projected = lax.map(project_line, normed)
    queries = projected[:, :, :D].reshape(LAT, LON, H, DH)
    lon_reach = WIN // 2
    key_rows = projected[:, :, D:2 * D]
    value_rows = projected[:, :, 2 * D:]
    key_pad = jnp.concatenate([key_rows[:, LON - lon_reach:], key_rows, key_rows[:, :lon_reach]], axis=1)
    value_pad = jnp.concatenate([value_rows[:, LON - lon_reach:], value_rows, value_rows[:, :lon_reach]], axis=1)
    key_pad = key_pad.reshape(LAT, LON + 2 * lon_reach, H, DH)
    value_pad = value_pad.reshape(LAT, LON + 2 * lon_reach, H, DH)

    def attend(operands):
        query_line, band_first = operands
        key_band = lax.dynamic_slice_in_dim(key_pad, band_first.astype(jnp.int32), WIN, 0)
        value_band = lax.dynamic_slice_in_dim(value_pad, band_first.astype(jnp.int32), WIN, 0)
        key_window = jnp.stack([key_band[:, offset:offset + LON] for offset in range(WIN)], axis=1)
        value_window = jnp.stack([value_band[:, offset:offset + LON] for offset in range(WIN)], axis=1)
        key_window = key_window.reshape(WIN * WIN, LON, H, DH).astype(jnp.float32)
        value_window = value_window.reshape(WIN * WIN, LON, H, DH).astype(jnp.float32)
        scores = jnp.einsum('jhd,xjhd->jhx', query_line.astype(jnp.float32), key_window, precision=lax.Precision.HIGHEST) * DH ** (-0.5)
        row_max = lax.optimization_barrier(jnp.max(scores, axis=-1, keepdims=True))
        raised = jnp.exp(scores - row_max)
        weights = (raised / lax.optimization_barrier(jnp.sum(raised, axis=-1, keepdims=True))).astype(jnp.bfloat16)
        mixed = jnp.einsum('jhx,xjhd->jhd', weights.astype(jnp.float32), value_window, precision=lax.Precision.HIGHEST)
        return mixed.astype(jnp.bfloat16).reshape(LON, D)
    attended = lax.map(attend, (queries, lat_start))

    def finish_line(operands):
        embed_rows, attended_rows = operands
        return (embed_rows.astype(jnp.float32) + jnp.dot(attended_rows, w_out, preferred_element_type=jnp.float32)).astype(jnp.bfloat16)
    return lax.map(finish_line, (embedded, attended))
```

```python
import functools

import jax
import jax.numpy as jnp
from jax import lax
from jax.experimental import pallas as pl
from jax.experimental.pallas import tpu as pltpu
from jax.sharding import PartitionSpec as P

DH = 64
IN_LEV = 24
WIN = 13
LAT_REACH = 8
STRIP = 8
QCOLS = 16
KCOLS = QCOLS + 2 * STRIP
MASKED = -1e30


def params(mib):
    return pltpu.CompilerParams(vmem_limit_bytes=mib << 20)


def cost(flops, nbytes, trans=0):
    return pl.CostEstimate(flops=int(flops), bytes_accessed=int(nbytes), transcendentals=int(trans))


def pack_kernel(dests, lon_rows, x_ref, o_ref):
    rows, _, width = x_ref.shape
    tokens = rows * lon_rows
    half = tokens // 2
    for d in range(dests):
        x = x_ref[:, d * lon_rows:(d + 1) * lon_rows, :].reshape(tokens, width)
        o_ref[d, :tokens, :] = x[:, :128]
        tail = x[:, 128:]
        o_ref[d, tokens:, :] = jnp.concatenate([tail[:half], tail[half:]], axis=1)


def pack(fields, lev):
    rows, lon_all, width = fields.shape
    lon_rows = lon_all // lev
    tokens = rows * lon_rows
    dests = 4
    return pl.pallas_call(
        functools.partial(pack_kernel, dests, lon_rows),
        grid=(lev // dests,),
        in_specs=[pl.BlockSpec((rows, dests * lon_rows, width), lambda i: (0, i, 0))],
        out_specs=pl.BlockSpec((dests, tokens + tokens // 2, 128), lambda i: (i, 0, 0)),
        out_shape=jax.ShapeDtypeStruct((lev, tokens + tokens // 2, 128), fields.dtype),
        compiler_params=params(32),
        cost_estimate=cost(0, 2 * fields.size * 2),
        name="pack",
    )(fields)


def embed_kernel(sources, rows, x_ref, w_ref, pick_ref, bias_ref, gain_ref, norm_ref, emb_ref, normed_ref, acc_ref):
    groups = bias_ref.shape[0]
    width = w_ref.shape[1]
    tokens = acc_ref.shape[1]
    half = tokens // 2
    step = pl.program_id(0)
    main = [x_ref[s, :tokens, :] for s in range(sources)]
    tails = [x_ref[s, tokens:, :] for s in range(sources)]
    low = jnp.concatenate([t[:, :64] for t in tails], axis=1)
    high = jnp.concatenate([t[:, 64:] for t in tails], axis=1)
    x = jnp.concatenate(main + [jnp.concatenate([low, high], axis=0)], axis=1)
    w = jnp.concatenate(
        [w_ref[s * 192:s * 192 + 128, :] for s in range(sources)]
        + [w_ref[s * 192 + 128:(s + 1) * 192, :] for s in range(sources)],
        axis=0,
    )
    for g in range(groups):
        part = jnp.dot(x * pick_ref[0, g:g + 1, :], w, preferred_element_type=jnp.float32)

        @pl.when(step == 0)
        def _():
            acc_ref[g] = part

        @pl.when(step > 0)
        def _():
            acc_ref[g] += part

    @pl.when(step == pl.num_programs(0) - 1)
    def _():
        total = jnp.zeros((tokens, width), jnp.float32)
        for g in range(groups):
            v = acc_ref[g] + bias_ref[g:g + 1, :]
            total += v / (1.0 + jnp.exp(-v)) * gain_ref[g:g + 1, :]
        emb = total.astype(jnp.bfloat16)
        wide = emb.astype(jnp.float32)
        inv = lax.rsqrt(jnp.mean(wide * wide, axis=-1, keepdims=True) + 1e-05)
        emb_ref[...] = emb.reshape(emb_ref.shape)
        normed_ref[...] = (wide * inv * norm_ref[...]).astype(jnp.bfloat16).reshape(normed_ref.shape)


def embed(moved, w_all, level_group, bias, gain, norm_gain, rows):
    lev = moved.shape[0]
    tokens = moved.shape[1] * 2 // 3
    depth, width = w_all.shape
    per = depth // lev
    groups = bias.shape[0]
    sources = 4
    steps = lev // sources
    row_groups = jnp.repeat(level_group, IN_LEV).reshape(steps, sources, per)
    order = jnp.concatenate(
        [row_groups[:, :, :128].reshape(steps, -1), row_groups[:, :, 128:].reshape(steps, -1)], axis=1
    )
    pick = (order[:, None, :] == jnp.arange(groups, dtype=jnp.int32)[None, :, None]).astype(jnp.bfloat16)
    cols = tokens // rows
    whole = lambda i: (0, 0)
    return pl.pallas_call(
        functools.partial(embed_kernel, sources, rows),
        grid=(steps,),
        in_specs=[
            pl.BlockSpec((sources, tokens * 3 // 2, 128), lambda i: (i, 0, 0)),
            pl.BlockSpec((sources * per, width), lambda i: (i, 0)),
            pl.BlockSpec((1, groups, sources * per), lambda i: (i, 0, 0)),
            pl.BlockSpec((groups, width), whole),
            pl.BlockSpec((groups, width), whole),
            pl.BlockSpec((1, width), whole),
        ],
        out_specs=[pl.BlockSpec((rows, cols, width), lambda i: (0, 0, 0))] * 2,
        out_shape=[jax.ShapeDtypeStruct((rows, cols, width), jnp.bfloat16)] * 2,
        scratch_shapes=[pltpu.VMEM((groups, tokens, width), jnp.float32)],
        compiler_params=params(48),
        cost_estimate=cost(2 * tokens * depth * width * groups, depth * width * 2 + tokens * depth * 2),
        name="embed",
    )(moved, w_all, pick, bias, gain, norm_gain[None, :])


def project_kernel(x_ref, w_ref, q_ref, kv_ref):
    rows, cols, width = x_ref.shape
    x = x_ref[...].reshape(rows * cols, width)
    q = jnp.dot(x, w_ref[:, :width], preferred_element_type=jnp.float32).astype(jnp.bfloat16)
    q = (q * jnp.bfloat16(DH ** (-0.5))).reshape(rows, cols, width)
    for b in range(cols // QCOLS):
        q_ref[b] = q[:, b * QCOLS:(b + 1) * QCOLS, :].reshape(rows * QCOLS, width)
    kv = jnp.dot(x, w_ref[:, width:], preferred_element_type=jnp.float32).astype(jnp.bfloat16)
    kv_ref[...] = kv.reshape(kv_ref.shape)


def project(normed, w_qkv):
    rows, cols, width = normed.shape
    return pl.pallas_call(
        project_kernel,
        out_shape=[
            jax.ShapeDtypeStruct((cols // QCOLS, rows * QCOLS, width), jnp.bfloat16),
            jax.ShapeDtypeStruct((rows, cols, 2 * width), jnp.bfloat16),
        ],
        compiler_params=params(48),
        cost_estimate=cost(2 * normed.size * w_qkv.shape[1], w_qkv.size * 2 + normed.size * 8),
        name="project",
    )(normed, w_qkv)


def attend_kernel(q_ref, own_ref, low_ref, high_ref, left_ref, right_ref, mask_ref, wkv_ref, wout_ref, emb_ref, out_ref, kv_ref, att_ref):
    rows, cols, width = low_ref.shape
    blocks = q_ref.shape[0]
    queries = q_ref.shape[1]
    wkv = wkv_ref[...]

    def keys_values(x):
        n = x.shape[0] * x.shape[1]
        out = jnp.dot(x.reshape(n, width), wkv, preferred_element_type=jnp.float32).astype(jnp.bfloat16)
        return out.reshape(x.shape[0], x.shape[1], 2 * width)

    kv_ref[rows:2 * rows, STRIP:STRIP + cols, :] = own_ref[...]
    kv_ref[:rows, STRIP:STRIP + cols, :] = keys_values(low_ref[...])
    kv_ref[2 * rows:, STRIP:STRIP + cols, :] = keys_values(high_ref[...])
    kv_ref[:, :STRIP, :] = keys_values(left_ref[...])
    kv_ref[:, STRIP + cols:, :] = keys_values(right_ref[...])
    lane = lax.broadcasted_iota(jnp.int32, (queries, 128), 1)
    first = lane < DH

    def pair(p, carry):
        at = pl.multiple_of(p * 128, 128)
        at_v = pl.multiple_of(width + p * 128, 128)
        for b in range(blocks):
            q = q_ref[b, :, pl.ds(at, 128)]
            zero = jnp.zeros_like(q)
            qq = jnp.concatenate([jnp.where(first, q, zero), jnp.where(first, zero, q)], axis=0)
            k = kv_ref[:, b * QCOLS:b * QCOLS + KCOLS, pl.ds(at, 128)].reshape(3 * rows * KCOLS, 128)
            v = kv_ref[:, b * QCOLS:b * QCOLS + KCOLS, pl.ds(at_v, 128)].reshape(3 * rows * KCOLS, 128)
            s = lax.dot_general(qq, k, (((1,), (1,)), ((), ())), preferred_element_type=jnp.float32)
            s = s + mask_ref[...]
            top = jnp.max(s, axis=-1, keepdims=True)
            e = jnp.exp(s - top)
            weights = (e * (1.0 / jnp.sum(e, axis=-1, keepdims=True))).astype(jnp.bfloat16)
            o = jnp.dot(weights, v, preferred_element_type=jnp.float32)
            att_ref[b, :, pl.ds(at, 128)] = jnp.where(first, o[:queries], o[queries:]).astype(jnp.bfloat16)
        return carry

    lax.fori_loop(0, width // 128, pair, 0)
    for b in range(blocks):
        mixed = jnp.dot(att_ref[b], wout_ref[...], preferred_element_type=jnp.float32)
        here = slice(b * QCOLS, (b + 1) * QCOLS)
        wide = emb_ref[:, here, :].astype(jnp.float32)
        out_ref[:, here, :] = (wide + mixed.reshape(wide.shape)).astype(jnp.bfloat16)


def attend(q, own, low, high, left, right, mask, w_kv, w_out, emb):
    rows, cols, width = low.shape
    flops = 2 * 2 * rows * cols * width * 2 * width + 12 * 4 * rows * cols * 3 * rows * KCOLS * 64 * 4
    return pl.pallas_call(
        attend_kernel,
        out_shape=jax.ShapeDtypeStruct((rows, cols, width), jnp.bfloat16),
        scratch_shapes=[
            pltpu.VMEM((3 * rows, cols + 2 * STRIP, 2 * width), jnp.bfloat16),
            pltpu.VMEM(q.shape, jnp.bfloat16),
        ],
        compiler_params=params(56),
        cost_estimate=cost(flops, 12e6, 4e6),
        name="attend",
    )(q, own, low, high, left, right, mask, w_kv, w_out, emb)


def window_mask(lat_start, rows):
    first_row = lax.axis_index("lat") * rows
    start = lax.dynamic_slice_in_dim(lat_start, first_row, rows) - first_row + LAT_REACH
    key_row = jnp.arange(3 * rows, dtype=jnp.int32)
    row_ok = (key_row[None, :] >= start[:, None]) & (key_row[None, :] < start[:, None] + WIN)
    shift = jnp.arange(KCOLS, dtype=jnp.int32)[None, :] - jnp.arange(QCOLS, dtype=jnp.int32)[:, None]
    near = STRIP - WIN // 2
    col_ok = (shift >= near) & (shift < near + WIN)
    ok = row_ok[:, None, :, None] & col_ok[None, :, None, :]
    mask = jnp.where(ok, 0.0, MASKED).astype(jnp.float32).reshape(rows * QCOLS, 3 * rows * KCOLS)
    return jnp.concatenate([mask, mask], axis=0)


def per_device(
    fields, level_group, lat_start, w_embed, group_bias, group_gain, norm_gain, w_qkv, w_out
):
    rows = fields.shape[0]
    lev = lax.axis_size("lev")
    lat = lax.axis_size("lat")
    width = w_embed.shape[1]
    w_all = lax.all_gather(w_embed, "lev", axis=0, tiled=True)
    moved = lax.all_to_all(pack(fields, lev), "lev", split_axis=0, concat_axis=0, tiled=True)
    mask = window_mask(lat_start, rows)
    emb, normed = embed(moved, w_all, level_group, group_bias, group_gain, norm_gain, rows)
    up = [(i, i + 1) for i in range(lat - 1)]
    down = [(b, a) for a, b in up]
    low = lax.ppermute(normed, "lat", up)
    high = lax.ppermute(normed, "lat", down)
    q, own = project(normed, w_qkv)
    right_way = [(i, (i + 1) % lev) for i in range(lev)]
    left_way = [(b, a) for a, b in right_way]
    tall = [low, normed, high]
    left = lax.ppermute(jnp.concatenate([t[:, -STRIP:] for t in tall], axis=0), "lev", right_way)
    right = lax.ppermute(jnp.concatenate([t[:, :STRIP] for t in tall], axis=0), "lev", left_way)
    return attend(q, own, low, high, left, right, mask, w_qkv[:, width:], w_out, emb)


def solution(mesh):
    return jax.shard_map(
        per_device,
        mesh=mesh,
        in_specs=(P("lat", None, "lev"), P(), P(), P("lev", None), P(), P(), P(), P(), P()),
        out_specs=P("lat", "lev", None),
        check_vma=False,
    )
```

```python
import functools

import jax
import jax.numpy as jnp
from jax import lax
from jax.experimental import pallas as pl
from jax.experimental.pallas import tpu as pltpu
from jax.sharding import PartitionSpec as P

DH = 64
IN_LEV = 24
WIN = 13
LAT_REACH = 8
STRIP = 8
QCOLS = 16
KCOLS = QCOLS + 2 * STRIP
CHUNK = 4
SOURCES = 4
MASKED = -1e30


def params(mib):
    return pltpu.CompilerParams(vmem_limit_bytes=mib << 20)


def cost(flops, nbytes, trans=0):
    return pl.CostEstimate(flops=int(flops), bytes_accessed=int(nbytes), transcendentals=int(trans))


def smem():
    return pl.BlockSpec(memory_space=pltpu.SMEM)


def vmem():
    return pl.BlockSpec(memory_space=pltpu.VMEM)


def pack_kernel(x_ref, o_ref):
    rows, width, lon_all = x_ref.shape
    lev = o_ref.shape[0]
    cols = lon_all // lev
    tokens = rows * cols

    def put(block, first):
        turned = block.T.reshape(lev, cols, 128)
        o_ref[:, first:first + cols, :] = turned

    for r in range(rows):
        put(x_ref[r, :128, :], r * cols)
    for r in range(rows // 2):
        both = jnp.concatenate([x_ref[r, 128:, :], x_ref[r + rows // 2, 128:, :]], axis=0)
        put(both, tokens + r * cols)


def pack(turned, lev):
    rows, width, lon_all = turned.shape
    tokens = rows * lon_all // lev
    return pl.pallas_call(
        pack_kernel,
        out_shape=jax.ShapeDtypeStruct((lev, tokens + tokens // 2, 128), turned.dtype),
        compiler_params=params(60),
        cost_estimate=cost(0, 2 * turned.size * 2),
        name="pack",
    )(turned)


def embed_kernel(x_ref, w_hbm, pick_ref, bias_ref, gain_ref, norm_ref, emb_ref, normed_ref, xs_ref, sum_ref, w_ref, sem):
    groups, width = bias_ref.shape
    lev = x_ref.shape[0]
    parts, depth, part = w_ref.shape
    per = depth // lev
    tokens = xs_ref.shape[0] // groups
    span = SOURCES * per
    loads = [pltpu.make_async_copy(w_hbm.at[:, j * part:(j + 1) * part], w_ref.at[j], sem.at[j]) for j in range(parts)]
    for load in loads:
        load.start()

    for c in range(lev // SOURCES):
        here = range(c * SOURCES, (c + 1) * SOURCES)
        main = [x_ref[s, :tokens, :] for s in here]
        low = jnp.concatenate([x_ref[s, tokens:, :64] for s in here], axis=1)
        high = jnp.concatenate([x_ref[s, tokens:, 64:] for s in here], axis=1)
        x = jnp.concatenate(main + [jnp.concatenate([low, high], axis=0)], axis=1)
        for g in range(groups):
            xs_ref[g * tokens:(g + 1) * tokens, c * span:(c + 1) * span] = x * pick_ref[g:g + 1, c * span:(c + 1) * span]

    for j in range(parts):
        loads[j].wait()
        cols = slice(j * part, (j + 1) * part)
        acc = None
        for c in range(lev // SOURCES):
            here = range(c * SOURCES, (c + 1) * SOURCES)
            w = jnp.concatenate(
                [w_ref[j, s * per:s * per + 128, :] for s in here] + [w_ref[j, s * per + 128:(s + 1) * per, :] for s in here],
                axis=0,
            )
            term = jnp.dot(xs_ref[:, c * span:(c + 1) * span], w, preferred_element_type=jnp.float32)
            acc = term if acc is None else acc + term
        total = jnp.zeros((tokens, part), jnp.float32)
        for g in range(groups):
            v = acc[g * tokens:(g + 1) * tokens] + bias_ref[g:g + 1, cols]
            total += v / (1.0 + jnp.exp(-v)) * gain_ref[g:g + 1, cols]
        sum_ref[:, cols] = total

    emb = sum_ref[...].astype(jnp.bfloat16)
    wide = emb.astype(jnp.float32)
    inv = lax.rsqrt(jnp.mean(wide * wide, axis=-1, keepdims=True) + 1e-05)
    emb_ref[...] = emb.reshape(emb_ref.shape)
    normed_ref[...] = (wide * inv * norm_ref[...]).astype(jnp.bfloat16).reshape(normed_ref.shape)


def embed(moved, w_all, pick, bias, gain, norm_gain):
    tokens = moved.shape[1] * 2 // 3
    depth, width = w_all.shape
    groups = bias.shape[0]
    cols = tokens // CHUNK
    part = 256
    return pl.pallas_call(
        embed_kernel,
        in_specs=[vmem(), pl.BlockSpec(memory_space=pltpu.HBM)] + [vmem()] * 4,
        out_specs=[vmem()] * 2,
        out_shape=[jax.ShapeDtypeStruct((CHUNK, cols, width), jnp.bfloat16)] * 2,
        scratch_shapes=[
            pltpu.VMEM((groups * tokens, depth), jnp.bfloat16),
            pltpu.VMEM((tokens, width), jnp.float32),
            pltpu.VMEM((width // part, depth, part), jnp.bfloat16),
            pltpu.SemaphoreType.DMA((width // part,)),
        ],
        compiler_params=params(60),
        cost_estimate=cost(2 * tokens * depth * width * groups, depth * width * 2 + tokens * depth * 2),
        name="embed",
    )(moved, w_all, pick, bias, gain, norm_gain[None, :])


def picks(level_group, lev, groups):
    row_groups = jnp.repeat(level_group, IN_LEV).reshape(lev // SOURCES, SOURCES, -1)
    steps = row_groups.shape[0]
    order = jnp.concatenate(
        [row_groups[:, :, :128].reshape(steps, -1), row_groups[:, :, 128:].reshape(steps, -1)], axis=1
    ).reshape(-1)
    return (order[None, :] == jnp.arange(groups, dtype=jnp.int32)[:, None]).astype(jnp.bfloat16)


def keys_values(x, w):
    n = x.shape[0] * x.shape[1]
    out = jnp.dot(x.reshape(n, x.shape[2]), w, preferred_element_type=jnp.float32).astype(jnp.bfloat16)
    return out.reshape(x.shape[0], x.shape[1], w.shape[1])


def queries_of(x, w):
    rows, cols, width = x.shape
    q = jnp.dot(x.reshape(rows * cols, width), w, preferred_element_type=jnp.float32).astype(jnp.bfloat16)
    return (q * jnp.bfloat16(DH ** (-0.5))).reshape(rows, cols, width)


def project_kernel(own0_ref, own1_ref, low_ref, high_ref, w_ref, q_ref, own_kv_ref, low_kv_ref, high_kv_ref):
    rows, cols, width = low_ref.shape
    for c, ref in enumerate((own0_ref, own1_ref)):
        q = queries_of(ref[...], w_ref[:, :width])
        for b in range(cols // QCOLS):
            q_ref[b, c * rows * QCOLS:(c + 1) * rows * QCOLS, :] = q[:, b * QCOLS:(b + 1) * QCOLS, :].reshape(rows * QCOLS, width)
        own_kv_ref[c * rows:(c + 1) * rows] = keys_values(ref[...], w_ref[:, width:])
    low_kv_ref[...] = keys_values(low_ref[...], w_ref[:, width:])
    high_kv_ref[...] = keys_values(high_ref[...], w_ref[:, width:])


def project(own0, own1, low, high, w_qkv):
    rows, cols, width = low.shape
    kv = lambda n: jax.ShapeDtypeStruct((n, cols, 2 * width), jnp.bfloat16)
    return pl.pallas_call(
        project_kernel,
        out_shape=[jax.ShapeDtypeStruct((cols // QCOLS, 2 * rows * QCOLS, width), jnp.bfloat16), kv(2 * rows), kv(rows), kv(rows)],
        compiler_params=params(60),
        cost_estimate=cost(2 * low.size * 10 * width, w_qkv.size * 2 + low.size * 24),
        name="project",
    )(own0, own1, low, high, w_qkv)


def attend_kernel(start_ref, first_ref, q_ref, own_ref, low0_ref, high0_ref, low1_ref, high1_ref, left0_ref, right0_ref,
                  left1_ref, right1_ref, w_ref, wout_ref, emb0_ref, emb1_ref, out_ref, kv_ref, att_ref):
    rows, cols, width = out_ref.shape
    half = rows // 2
    blocks, queries, _ = q_ref.shape
    keys = 3 * rows * KCOLS
    wkv = w_ref[:, width:]
    inner = slice(STRIP, STRIP + cols)
    kv_ref[rows:2 * rows, inner, :] = own_ref[...]
    kv_ref[:half, inner, :] = low0_ref[...]
    kv_ref[2 * rows:2 * rows + half, inner, :] = high0_ref[...]
    kv_ref[half:rows, inner, :] = keys_values(low1_ref[...], wkv)
    kv_ref[2 * rows + half:, inner, :] = keys_values(high1_ref[...], wkv)
    for c, (left, right) in enumerate(((left0_ref, right0_ref), (left1_ref, right1_ref))):
        for side, at in ((left, slice(0, STRIP)), (right, slice(STRIP + cols, None))):
            strip = keys_values(side[...], wkv)
            for t in range(3):
                kv_ref[t * rows + c * half:t * rows + (c + 1) * half, at, :] = strip[t * half:(t + 1) * half]

    key = lax.broadcasted_iota(jnp.int32, (QCOLS, keys), 1)
    key_row = key // KCOLS
    shift = key % KCOLS - lax.broadcasted_iota(jnp.int32, (QCOLS, keys), 0)
    near = STRIP - WIN // 2
    col_ok = (shift >= near) & (shift < near + WIN)
    first_row = first_ref[0]
    bias = []
    for r in range(rows):
        start = start_ref[first_row + r] - first_row + LAT_REACH
        ok = col_ok & (key_row >= start) & (key_row < start + WIN)
        bias.append(jnp.where(ok, 0.0, MASKED))
    bias = jnp.concatenate(bias + bias, axis=0)

    lane = lax.broadcasted_iota(jnp.int32, (queries, 128), 1)
    is_first = lane < DH
    ones = jnp.ones((keys, 128), jnp.bfloat16)
    for p in range(width // 128):
        here = slice(p * 128, (p + 1) * 128)
        here_v = slice(width + p * 128, width + (p + 1) * 128)
        for b in range(blocks):
            band = slice(b * QCOLS, b * QCOLS + KCOLS)
            q = q_ref[b, :, here]
            zero = jnp.zeros_like(q)
            qq = jnp.concatenate([jnp.where(is_first, q, zero), jnp.where(is_first, zero, q)], axis=0)
            k = kv_ref[:, band, here].reshape(keys, 128)
            v = kv_ref[:, band, here_v].reshape(keys, 128)
            s = lax.dot_general(qq, k, (((1,), (1,)), ((), ())), preferred_element_type=jnp.float32) + bias
            e = jnp.exp(s - jnp.max(s, axis=-1, keepdims=True)).astype(jnp.bfloat16)
            o = jnp.dot(e, jnp.concatenate([v, ones], axis=1), preferred_element_type=jnp.float32)
            o = o[:, :128] / o[:, 128:]
            att_ref[b, :, here] = jnp.where(is_first, o[:queries], o[queries:]).astype(jnp.bfloat16)
    for b in range(blocks):
        mixed = jnp.dot(att_ref[b], wout_ref[...], preferred_element_type=jnp.float32)
        mixed = mixed.reshape(rows, QCOLS, width)
        here = slice(b * QCOLS, (b + 1) * QCOLS)
        for c, ref in enumerate((emb0_ref, emb1_ref)):
            wide = ref[:, here, :].astype(jnp.float32)
            out_ref[c * half:(c + 1) * half, here, :] = (wide + mixed[c * half:(c + 1) * half]).astype(jnp.bfloat16)


def attend(lat_start, first_row, q, own, low0, high0, low1, high1, sides, w_qkv, w_out, emb0, emb1):
    rows, cols, _ = own.shape
    width = w_out.shape[0]
    flops = 2 * 18 * rows * cols * width * width
    return pl.pallas_call(
        attend_kernel,
        in_specs=[smem(), smem()] + [vmem()] * 14,
        out_specs=vmem(),
        out_shape=jax.ShapeDtypeStruct((rows, cols, width), jnp.bfloat16),
        scratch_shapes=[
            pltpu.VMEM((3 * rows, cols + 2 * STRIP, 2 * width), jnp.bfloat16),
            pltpu.VMEM(q.shape, jnp.bfloat16),
        ],
        compiler_params=params(60),
        cost_estimate=cost(flops, 12e6, 4e6),
        name="attend",
    )(lat_start, first_row, q, own, low0, high0, low1, high1, *sides, w_qkv, w_out, emb0, emb1)


def per_device(
    fields, level_group, lat_start, w_embed, group_bias, group_gain, norm_gain, w_qkv, w_out
):
    rows = fields.shape[0]
    lev = lax.axis_size("lev")
    lat = lax.axis_size("lat")
    w_all = lax.all_gather(w_embed, "lev", axis=0, tiled=True)
    turned = jnp.transpose(fields, (0, 2, 1))
    pick = picks(level_group, lev, group_bias.shape[0])
    first_row = (lax.axis_index("lat") * rows).astype(jnp.int32).reshape(1)
    up = [(i, i + 1) for i in range(lat - 1)]
    down = [(b, a) for a, b in up]
    right_way = [(i, (i + 1) % lev) for i in range(lev)]
    left_way = [(b, a) for a, b in right_way]

    emb, normed, low, high, sides = [], [], [], [], []
    for c in range(rows // CHUNK):
        packed = pack(turned[c * CHUNK:(c + 1) * CHUNK], lev)
        moved = lax.all_to_all(packed, "lev", split_axis=0, concat_axis=0, tiled=True)
        e, n = embed(moved, w_all, pick, group_bias, group_gain, norm_gain)
        emb.append(e)
        normed.append(n)
        low.append(lax.ppermute(n, "lat", up))
        high.append(lax.ppermute(n, "lat", down))
    q, own_kv, low_kv, high_kv = project(normed[0], normed[1], low[0], high[0], w_qkv)
    low[1], high[1], q = lax.optimization_barrier((low[1], high[1], q))
    for c in range(rows // CHUNK):
        tall = [low[c], normed[c], high[c]]
        sides.append(lax.ppermute(jnp.concatenate([t[:, -STRIP:] for t in tall], axis=0), "lev", right_way))
        sides.append(lax.ppermute(jnp.concatenate([t[:, :STRIP] for t in tall], axis=0), "lev", left_way))
    return attend(lat_start, first_row, q, own_kv, low_kv, high_kv, low[1], high[1], sides, w_qkv, w_out, emb[0], emb[1])


def solution(mesh):
    return jax.shard_map(
        per_device,
        mesh=mesh,
        in_specs=(P("lat", None, "lev"), P(), P(), P("lev", None), P(), P(), P(), P(), P()),
        out_specs=P("lat", "lev", None),
        check_vma=False,
    )
```

```python
import functools

import jax
import jax.numpy as jnp
from jax import lax
from jax.experimental import pallas as pl
from jax.experimental.pallas import tpu as pltpu
from jax.sharding import PartitionSpec as P

DH = 64
IN_LEV = 24
WIN = 13
LAT_REACH = 8
STRIP = 8
QCOLS = 16
KCOLS = QCOLS + 2 * STRIP
CHUNK = 4
SOURCES = 4
MASKED = -1e30
LIMIT = 36


def params(mib):
    return pltpu.CompilerParams(vmem_limit_bytes=mib << 20)


def cost(flops, nbytes, trans=0):
    return pl.CostEstimate(flops=int(flops), bytes_accessed=int(nbytes), transcendentals=int(trans))


def smem():
    return pl.BlockSpec(memory_space=pltpu.SMEM)


def vmem():
    return pl.BlockSpec(memory_space=pltpu.VMEM)


def pack_kernel(x_ref, o_ref):
    rows, width, lon_all = x_ref.shape
    lev = o_ref.shape[0]
    cols = lon_all // lev
    tokens = rows * cols

    def put(block, first):
        turned = block.T.reshape(lev, cols, 128)
        o_ref[:, first:first + cols, :] = turned

    for r in range(rows):
        put(x_ref[r, :128, :], r * cols)
    for r in range(rows // 2):
        both = jnp.concatenate([x_ref[r, 128:, :], x_ref[r + rows // 2, 128:, :]], axis=0)
        put(both, tokens + r * cols)


def pack(turned, lev, chunk):
    _, width, lon_all = turned.shape
    tokens = CHUNK * lon_all // lev
    return pl.pallas_call(
        pack_kernel,
        grid=(1,),
        in_specs=[pl.BlockSpec((CHUNK, width, lon_all), lambda i: (chunk, 0, 0))],
        out_specs=pl.BlockSpec((lev, tokens + tokens // 2, 128), lambda i: (0, 0, 0)),
        out_shape=jax.ShapeDtypeStruct((lev, tokens + tokens // 2, 128), turned.dtype),
        compiler_params=params(60),
        cost_estimate=cost(0, 2 * turned.size),
        name="pack",
    )(turned)


def embed_kernel(x_ref, w_hbm, pick_ref, bias_ref, gain_ref, norm_ref, emb_ref, normed_ref, xs_ref, sum_ref, w_ref, sem):
    groups, width = bias_ref.shape
    lev = x_ref.shape[0]
    parts, depth, part = w_ref.shape
    per = depth // lev
    tokens = xs_ref.shape[0] // groups
    span = SOURCES * per
    loads = [pltpu.make_async_copy(w_hbm.at[:, j * part:(j + 1) * part], w_ref.at[j], sem.at[j]) for j in range(parts)]
    for load in loads:
        load.start()

    for c in range(lev // SOURCES):
        here = range(c * SOURCES, (c + 1) * SOURCES)
        main = [x_ref[s, :tokens, :] for s in here]
        low = jnp.concatenate([x_ref[s, tokens:, :64] for s in here], axis=1)
        high = jnp.concatenate([x_ref[s, tokens:, 64:] for s in here], axis=1)
        x = jnp.concatenate(main + [jnp.concatenate([low, high], axis=0)], axis=1)
        for g in range(groups):
            xs_ref[g * tokens:(g + 1) * tokens, c * span:(c + 1) * span] = x * pick_ref[g:g + 1, c * span:(c + 1) * span]

    for j in range(parts):
        loads[j].wait()
        cols = slice(j * part, (j + 1) * part)
        acc = None
        for c in range(lev // SOURCES):
            here = range(c * SOURCES, (c + 1) * SOURCES)
            w = jnp.concatenate(
                [w_ref[j, s * per:s * per + 128, :] for s in here] + [w_ref[j, s * per + 128:(s + 1) * per, :] for s in here],
                axis=0,
            )
            term = jnp.dot(xs_ref[:, c * span:(c + 1) * span], w, preferred_element_type=jnp.float32)
            acc = term if acc is None else acc + term
        total = jnp.zeros((tokens, part), jnp.float32)
        for g in range(groups):
            v = acc[g * tokens:(g + 1) * tokens] + bias_ref[g:g + 1, cols]
            total += v / (1.0 + jnp.exp(-v)) * gain_ref[g:g + 1, cols]
        sum_ref[:, cols] = total

    emb = sum_ref[...].astype(jnp.bfloat16)
    wide = emb.astype(jnp.float32)
    inv = lax.rsqrt(jnp.mean(wide * wide, axis=-1, keepdims=True) + 1e-05)
    emb_ref[...] = emb.reshape(emb_ref.shape)
    normed_ref[...] = (wide * inv * norm_ref[...]).astype(jnp.bfloat16).reshape(normed_ref.shape)


def embed(moved, w_all, pick, bias, gain, norm_gain):
    tokens = moved.shape[1] * 2 // 3
    depth, width = w_all.shape
    groups = bias.shape[0]
    cols = tokens // CHUNK
    part = 256
    return pl.pallas_call(
        embed_kernel,
        in_specs=[vmem(), pl.BlockSpec(memory_space=pltpu.HBM)] + [vmem()] * 4,
        out_specs=[vmem()] * 2,
        out_shape=[jax.ShapeDtypeStruct((CHUNK, cols, width), jnp.bfloat16)] * 2,
        scratch_shapes=[
            pltpu.VMEM((groups * tokens, depth), jnp.bfloat16),
            pltpu.VMEM((tokens, width), jnp.float32),
            pltpu.VMEM((width // part, depth, part), jnp.bfloat16),
            pltpu.SemaphoreType.DMA((width // part,)),
        ],
        compiler_params=params(60),
        cost_estimate=cost(2 * tokens * depth * width * groups, depth * width * 2 + tokens * depth * 2),
        name="embed",
    )(moved, w_all, pick, bias, gain, norm_gain[None, :])


def picks(level_group, lev, groups):
    row_groups = jnp.repeat(level_group, IN_LEV).reshape(lev // SOURCES, SOURCES, -1)
    steps = row_groups.shape[0]
    order = jnp.concatenate(
        [row_groups[:, :, :128].reshape(steps, -1), row_groups[:, :, 128:].reshape(steps, -1)], axis=1
    ).reshape(-1)
    return (order[None, :] == jnp.arange(groups, dtype=jnp.int32)[:, None]).astype(jnp.bfloat16)


def keys_values(x, w):
    n = x.shape[0] * x.shape[1]
    out = jnp.dot(x.reshape(n, x.shape[2]), w, preferred_element_type=jnp.float32).astype(jnp.bfloat16)
    return out.reshape(x.shape[0], x.shape[1], w.shape[1])


def queries_of(x, w):
    rows, cols, width = x.shape
    q = jnp.dot(x.reshape(rows * cols, width), w, preferred_element_type=jnp.float32).astype(jnp.bfloat16)
    return (q * jnp.bfloat16(DH ** (-0.5))).reshape(rows, cols, width)


def project_kernel(own0_ref, own1_ref, low_ref, high_ref, w_ref, q_ref, kv_ref):
    rows, cols, width = low_ref.shape
    inner = slice(STRIP, STRIP + cols)
    for c, ref in enumerate((own0_ref, own1_ref)):
        q = queries_of(ref[...], w_ref[:, :width])
        for b in range(cols // QCOLS):
            q_ref[b, c * rows * QCOLS:(c + 1) * rows * QCOLS, :] = q[:, b * QCOLS:(b + 1) * QCOLS, :].reshape(rows * QCOLS, width)
    for ref, at in ((own0_ref, 2), (own1_ref, 3), (low_ref, 0), (high_ref, 4)):
        kv_ref[at * rows:(at + 1) * rows, inner, :] = keys_values(ref[...], w_ref[:, width:])


def project(own0, own1, low, high, w_qkv):
    rows, cols, width = low.shape
    return pl.pallas_call(
        project_kernel,
        in_specs=[vmem()] * 5,
        out_specs=[vmem()] * 2,
        out_shape=[
            pltpu.VMEM((cols // QCOLS, 2 * rows * QCOLS, width), jnp.bfloat16),
            pltpu.VMEM((6 * rows, cols + 2 * STRIP, 2 * width), jnp.bfloat16),
        ],
        compiler_params=params(LIMIT),
        cost_estimate=cost(2 * low.size * 10 * width, w_qkv.size * 2 + low.size * 24),
        name="project",
    )(own0, own1, low, high, w_qkv)


def window_bias(start_ref, first_ref, rows):
    keys = 3 * rows * KCOLS
    key = lax.broadcasted_iota(jnp.int32, (QCOLS, keys), 1)
    key_row = key // KCOLS
    shift = key % KCOLS - lax.broadcasted_iota(jnp.int32, (QCOLS, keys), 0)
    near = STRIP - WIN // 2
    col_ok = (shift >= near) & (shift < near + WIN)
    first_row = first_ref[0]
    bias = []
    for r in range(rows):
        start = start_ref[first_row + r] - first_row + LAT_REACH
        ok = col_ok & (key_row >= start) & (key_row < start + WIN)
        bias.append(jnp.where(ok, 0.0, MASKED))
    return jnp.concatenate(bias + bias, axis=0)


def attend_block(b, bias, q_ref, kv_ref, att_ref):
    _, queries, width = q_ref.shape
    keys = bias.shape[1]
    lane = lax.broadcasted_iota(jnp.int32, (queries, 128), 1)
    is_first = lane < DH
    ones = jnp.ones((keys, 128), jnp.bfloat16)
    band = slice(b * QCOLS, b * QCOLS + KCOLS)
    for p in range(width // 128):
        here = slice(p * 128, (p + 1) * 128)
        here_v = slice(width + p * 128, width + (p + 1) * 128)
        q = q_ref[b, :, here]
        zero = jnp.zeros_like(q)
        qq = jnp.concatenate([jnp.where(is_first, q, zero), jnp.where(is_first, zero, q)], axis=0)
        k = kv_ref[:, band, here].reshape(keys, 128)
        v = kv_ref[:, band, here_v].reshape(keys, 128)
        s = lax.dot_general(qq, k, (((1,), (1,)), ((), ())), preferred_element_type=jnp.float32) + bias
        e = jnp.exp(s - jnp.max(s, axis=-1, keepdims=True)).astype(jnp.bfloat16)
        o = jnp.dot(e, jnp.concatenate([v, ones], axis=1), preferred_element_type=jnp.float32)
        o = o[:, :128] / o[:, 128:]
        att_ref[b, :, here] = jnp.where(is_first, o[:queries], o[queries:]).astype(jnp.bfloat16)


def finish_block(b, rows, att_ref, wout_ref, emb_refs, write):
    mixed = jnp.dot(att_ref[b], wout_ref[...], preferred_element_type=jnp.float32)
    mixed = mixed.reshape(rows, QCOLS, mixed.shape[1])
    half = rows // 2
    for c, ref in enumerate(emb_refs):
        wide = ref[:, b * QCOLS:(b + 1) * QCOLS, :].astype(jnp.float32)
        write(slice(c * half, (c + 1) * half), (wide + mixed[c * half:(c + 1) * half]).astype(jnp.bfloat16))


def middle_kernel(start_ref, first_ref, q_ref, _, low_ref, high_ref, left_ref, right_ref, w_ref, wout_ref, emb0_ref, emb1_ref,
                  kv_ref, out_ref, att_ref):
    half, cols, width = low_ref.shape
    rows = 2 * half
    wkv = w_ref[:, width:]
    inner = slice(STRIP, STRIP + cols)
    kv_ref[half:rows, inner, :] = keys_values(low_ref[...], wkv)
    kv_ref[2 * rows + half:, inner, :] = keys_values(high_ref[...], wkv)
    bias = window_bias(start_ref, first_ref, rows)
    attend_block(1, bias, q_ref, kv_ref, att_ref)

    def write(at, value):
        out_ref[at] = value

    finish_block(1, rows, att_ref, wout_ref, (emb0_ref, emb1_ref), write)
    for side, at in ((left_ref, slice(0, STRIP)), (right_ref, slice(STRIP + cols, None))):
        strip = keys_values(side[...], wkv)
        kv_ref[:half, at, :] = strip[:half]
        kv_ref[rows:2 * rows, at, :] = strip[half:3 * half]
        kv_ref[2 * rows:2 * rows + half, at, :] = strip[3 * half:]


def middle(lat_start, first_row, q, kv, low, high, left, right, w_qkv, w_out, emb0, emb1):
    half, cols, width = low.shape
    return pl.pallas_call(
        middle_kernel,
        in_specs=[smem(), smem()] + [vmem()] * 10,
        out_specs=[vmem()] * 2,
        out_shape=[pltpu.VMEM(kv.shape, kv.dtype), pltpu.VMEM((2 * half, QCOLS, width), jnp.bfloat16)],
        input_output_aliases={3: 0},
        scratch_shapes=[pltpu.VMEM(q.shape, jnp.bfloat16)],
        compiler_params=params(LIMIT),
        cost_estimate=cost(8e9, 10e6, 1e6),
        name="middle",
    )(lat_start, first_row, q, kv, low, high, left, right, w_qkv, w_out, emb0, emb1)


def sides_kernel(start_ref, first_ref, q_ref, _, left_ref, right_ref, w_ref, wout_ref, emb0_ref, emb1_ref, middle_ref,
                 out_ref, kv_ref, att_ref):
    rows, cols, width = out_ref.shape
    half = rows // 2
    blocks = q_ref.shape[0]
    wkv = w_ref[:, width:]
    for side, at in ((left_ref, slice(0, STRIP)), (right_ref, slice(STRIP + cols, None))):
        strip = keys_values(side[...], wkv)
        kv_ref[half:rows, at, :] = strip[:half]
        kv_ref[2 * rows + half:, at, :] = strip[half:]
    bias = window_bias(start_ref, first_ref, rows)
    out_ref[:, QCOLS:2 * QCOLS, :] = middle_ref[...]
    for b in (0, blocks - 1):
        attend_block(b, bias, q_ref, kv_ref, att_ref)

        def write(at, value):
            out_ref[at, b * QCOLS:(b + 1) * QCOLS, :] = value

        finish_block(b, rows, att_ref, wout_ref, (emb0_ref, emb1_ref), write)


def sides(lat_start, first_row, q, kv, left, right, w_qkv, w_out, emb0, emb1, centre):
    half, cols, width = emb0.shape
    return pl.pallas_call(
        sides_kernel,
        in_specs=[smem(), smem()] + [vmem()] * 9,
        out_specs=[vmem()] * 2,
        out_shape=[jax.ShapeDtypeStruct((2 * half, cols, width), jnp.bfloat16), pltpu.VMEM(kv.shape, kv.dtype)],
        input_output_aliases={3: 1},
        scratch_shapes=[pltpu.VMEM(q.shape, jnp.bfloat16)],
        compiler_params=params(LIMIT),
        cost_estimate=cost(9e9, 10e6, 2e6),
        name="sides",
    )(lat_start, first_row, q, kv, left, right, w_qkv, w_out, emb0, emb1, centre)[0]


def per_device(
    fields, level_group, lat_start, w_embed, group_bias, group_gain, norm_gain, w_qkv, w_out
):
    rows = fields.shape[0]
    lev = lax.axis_size("lev")
    lat = lax.axis_size("lat")
    w_all = lax.all_gather(w_embed, "lev", axis=0, tiled=True)
    turned = jnp.transpose(fields, (0, 2, 1))
    pick = picks(level_group, lev, group_bias.shape[0])
    first_row = (lax.axis_index("lat") * rows).astype(jnp.int32).reshape(1)
    up = [(i, i + 1) for i in range(lat - 1)]
    down = [(b, a) for a, b in up]
    right_way = [(i, (i + 1) % lev) for i in range(lev)]
    left_way = [(b, a) for a, b in right_way]

    emb, normed, low, high = [], [], [], []
    for c in range(rows // CHUNK):
        packed = pack(turned, lev, c)
        if c > 0:
            packed, w_all = lax.optimization_barrier((packed, w_all))
        moved = lax.all_to_all(packed, "lev", split_axis=0, concat_axis=0, tiled=True)
        e, n = embed(moved, w_all, pick, group_bias, group_gain, norm_gain)
        emb.append(e)
        normed.append(n)
        low.append(lax.ppermute(n, "lat", up))
        high.append(lax.ppermute(n, "lat", down))

    def strips(tall):
        left = lax.ppermute(jnp.concatenate([t[:, -STRIP:] for t in tall], axis=0), "lev", right_way)
        right = lax.ppermute(jnp.concatenate([t[:, :STRIP] for t in tall], axis=0), "lev", left_way)
        return left, right

    low[0], high[0], normed[1] = lax.optimization_barrier((low[0], high[0], normed[1]))
    left, right = strips([low[0], normed[0], normed[1], high[0]])
    q, kv = project(normed[0], normed[1], low[0], high[0], w_qkv)
    low[1], high[1], q = lax.optimization_barrier((low[1], high[1], q))
    last_left, last_right = strips([low[1], high[1]])
    kv, centre = middle(
        lat_start, first_row, q, kv, low[1], high[1], left, right, w_qkv, w_out, emb[0], emb[1]
    )
    return sides(lat_start, first_row, q, kv, last_left, last_right, w_qkv, w_out, emb[0], emb[1], centre)


def solution(mesh):
    return jax.shard_map(
        per_device,
        mesh=mesh,
        in_specs=(P("lat", None, "lev"), P(), P(), P("lev", None), P(), P(), P(), P(), P()),
        out_specs=P("lat", "lev", None),
        check_vma=False,
    )
```

```python
import functools

import jax
import jax.numpy as jnp
from jax import lax
from jax.experimental import pallas as pl
from jax.experimental.pallas import tpu as pltpu
from jax.sharding import PartitionSpec as P

DH = 64
IN_LEV = 24
WIN = 13
LAT_REACH = 8
STRIP = 8
QCOLS = 16
KCOLS = QCOLS + 2 * STRIP
PLANES = 4
CHUNK = 4
SOURCES = 4
MASKED = -1e30
PART = 256
EMBED_LIMIT = 50
LIMIT = 36


def params(mib):
    return pltpu.CompilerParams(vmem_limit_bytes=mib << 20)


def cost(flops, nbytes, trans=0):
    return pl.CostEstimate(flops=int(flops), bytes_accessed=int(nbytes), transcendentals=int(trans))


def smem():
    return pl.BlockSpec(memory_space=pltpu.SMEM)


def vmem():
    return pl.BlockSpec(memory_space=pltpu.VMEM)


def pack_kernel(x_ref, o_ref):
    rows, width, lon_all = x_ref.shape
    lev = o_ref.shape[0]
    cols = lon_all // lev
    tokens = rows * cols

    def put(block, first):
        turned = block.T.reshape(lev, cols, 128)
        o_ref[:, first:first + cols, :] = turned

    for r in range(rows):
        put(x_ref[r, :128, :], r * cols)
    for r in range(rows // 2):
        both = jnp.concatenate([x_ref[r, 128:, :], x_ref[r + rows // 2, 128:, :]], axis=0)
        put(both, tokens + r * cols)


def pack(turned, lev, chunk):
    _, width, lon_all = turned.shape
    tokens = CHUNK * lon_all // lev
    return pl.pallas_call(
        pack_kernel,
        grid=(1,),
        in_specs=[pl.BlockSpec((CHUNK, width, lon_all), lambda i: (chunk, 0, 0))],
        out_specs=pl.BlockSpec((lev, tokens + tokens // 2, 128), lambda i: (0, 0, 0)),
        out_shape=jax.ShapeDtypeStruct((lev, tokens + tokens // 2, 128), turned.dtype),
        compiler_params=params(60),
        cost_estimate=cost(0, 2 * turned.size),
        name="pack",
    )(turned)


def weight_rows(w_ref, s, first, last):
    size = w_ref.shape[2]
    out = []
    for quarter in range(w_ref.shape[1]):
        low, high = max(first - quarter * size, 0), min(last - quarter * size, size)
        if low < high:
            out.append((s, quarter, low, high))
    return out


def embed_body(x_ref, w_ref, pick_ref, bias_ref, gain_ref, norm_ref, emb_ref, normed_ref, xs_ref, sum_ref, before):
    groups, width = bias_ref.shape
    lev, quarters, size, _ = w_ref.shape
    per = quarters * size
    part = PART
    tokens = xs_ref.shape[0] // groups
    span = SOURCES * per

    for c in range(lev // SOURCES):
        here = range(c * SOURCES, (c + 1) * SOURCES)
        main = [x_ref[s, :tokens, :] for s in here]
        low = jnp.concatenate([x_ref[s, tokens:, :64] for s in here], axis=1)
        high = jnp.concatenate([x_ref[s, tokens:, 64:] for s in here], axis=1)
        x = jnp.concatenate(main + [jnp.concatenate([low, high], axis=0)], axis=1)
        for g in range(groups):
            xs_ref[g * tokens:(g + 1) * tokens, c * span:(c + 1) * span] = x * pick_ref[g:g + 1, c * span:(c + 1) * span]

    for j in range(width // part):
        before(j)
        cols = slice(j * part, (j + 1) * part)
        acc = None
        for c in range(lev // SOURCES):
            here = range(c * SOURCES, (c + 1) * SOURCES)
            rows = [r for s in here for r in weight_rows(w_ref, s, 0, 128)]
            rows += [r for s in here for r in weight_rows(w_ref, s, 128, per)]
            w = jnp.concatenate([w_ref[s, quarter, low:high, cols] for s, quarter, low, high in rows], axis=0)
            term = jnp.dot(xs_ref[:, c * span:(c + 1) * span], w, preferred_element_type=jnp.float32)
            acc = term if acc is None else acc + term
        total = jnp.zeros((tokens, part), jnp.float32)
        for g in range(groups):
            v = acc[g * tokens:(g + 1) * tokens] + bias_ref[g:g + 1, cols]
            total += v / (1.0 + jnp.exp(-v)) * gain_ref[g:g + 1, cols]
        sum_ref[:, cols] = total

    emb = sum_ref[...].astype(jnp.bfloat16)
    wide = emb.astype(jnp.float32)
    inv = lax.rsqrt(jnp.mean(wide * wide, axis=-1, keepdims=True) + 1e-05)
    emb_ref[...] = emb.reshape(emb_ref.shape)
    normed_ref[...] = (wide * inv * norm_ref[...]).astype(jnp.bfloat16).reshape(normed_ref.shape)


def embed_first_kernel(place_ref, x_ref, pick_ref, bias_ref, gain_ref, norm_ref, *refs):
    pieces, (emb_ref, normed_ref, kept_ref, xs_ref, sum_ref, w_ref, sem) = refs[:10], refs[10:]
    lev, quarters, _, width = w_ref.shape
    half = width // 2
    plane, core = place_ref[0], place_ref[1]
    loads = []
    for sibling in (0, 1):
        column = pl.multiple_of(lax.rem(core + sibling, 2) * half, 128)
        spots = ((0, 0, lev), (quarters - 1, 0, lev), (1, 0, lev), (2, 0, lev // 2), (2, lev // 2, lev))
        for n, (ahead, first, last) in enumerate(spots):
            quarter = lax.rem(plane + ahead, quarters)
            loads.append(
                pltpu.make_async_copy(
                    pieces[sibling * 5 + n],
                    w_ref.at[first:last, quarter, :, pl.ds(column, half)],
                    sem.at[sibling * 5 + n],
                )
            )
    for load in loads:
        load.start()
    keep = pltpu.make_async_copy(w_ref, kept_ref, sem.at[10])

    def before(j):
        if j == 0:
            for load in loads:
                load.wait()
            keep.start()

    embed_body(x_ref, w_ref, pick_ref, bias_ref, gain_ref, norm_ref, emb_ref, normed_ref, xs_ref, sum_ref, before)
    keep.wait()


def embed_next_kernel(x_ref, pick_ref, bias_ref, gain_ref, norm_ref, kept_ref, emb_ref, normed_ref, xs_ref, sum_ref, w_ref, sem):
    loads = []
    for j in range(w_ref.shape[3] // PART):
        cols = slice(j * PART, (j + 1) * PART)
        loads.append(pltpu.make_async_copy(kept_ref.at[:, :, :, cols], w_ref.at[:, :, :, cols], sem.at[j]))
        loads[j].start()
    embed_body(
        x_ref, w_ref, pick_ref, bias_ref, gain_ref, norm_ref, emb_ref, normed_ref, xs_ref, sum_ref, lambda j: loads[j].wait()
    )


def embed(moved, place, w_all, pick, bias, gain, norm_gain):
    lev = moved.shape[0]
    tokens = moved.shape[1] * 2 // 3
    groups, width = bias.shape
    depth = pick.shape[1]
    cols = tokens // CHUNK
    out_shape = [jax.ShapeDtypeStruct((CHUNK, cols, width), jnp.bfloat16)] * 2
    size = w_all[0].shape[-2]
    kept = jax.ShapeDtypeStruct((lev, depth // lev // size, size, width), jnp.bfloat16)
    scratch = [
        pltpu.VMEM((groups * tokens, depth), jnp.bfloat16),
        pltpu.VMEM((tokens, width), jnp.float32),
        pltpu.VMEM(kept.shape, kept.dtype),
    ]
    far = pl.BlockSpec(memory_space=pl.ANY)
    common = dict(
        compiler_params=params(EMBED_LIMIT),
        cost_estimate=cost(2 * tokens * depth * width * groups, depth * width * 2 + tokens * depth * 2),
    )
    shared = (moved, pick, bias, gain, norm_gain[None, :])
    if len(w_all) > 1:
        return pl.pallas_call(
            embed_first_kernel,
            in_specs=[smem()] + [vmem()] * 5 + [far] * 10,
            out_specs=[vmem()] * 2 + [far],
            out_shape=out_shape + [kept],
            scratch_shapes=scratch + [pltpu.SemaphoreType.DMA((11,))],
            name="embed_first",
            **common,
        )(place, *shared, *w_all)
    return (
        *pl.pallas_call(
            embed_next_kernel,
            in_specs=[vmem()] * 5 + [far],
            out_specs=[vmem()] * 2,
            out_shape=out_shape,
            scratch_shapes=scratch + [pltpu.SemaphoreType.DMA((width // PART,))],
            name="embed_next",
            **common,
        )(*shared, *w_all),
        w_all[0],
    )


def picks(level_group, lev, groups):
    row_groups = jnp.repeat(level_group, IN_LEV).reshape(lev // SOURCES, SOURCES, -1)
    steps = row_groups.shape[0]
    order = jnp.concatenate(
        [row_groups[:, :, :128].reshape(steps, -1), row_groups[:, :, 128:].reshape(steps, -1)], axis=1
    ).reshape(-1)
    return (order[None, :] == jnp.arange(groups, dtype=jnp.int32)[:, None]).astype(jnp.bfloat16)


def keys_values(x, w):
    n = x.shape[0] * x.shape[1]
    out = jnp.dot(x.reshape(n, x.shape[2]), w, preferred_element_type=jnp.float32).astype(jnp.bfloat16)
    return out.reshape(x.shape[0], x.shape[1], w.shape[1])


def queries_of(x, w):
    rows, cols, width = x.shape
    q = jnp.dot(x.reshape(rows * cols, width), w, preferred_element_type=jnp.float32).astype(jnp.bfloat16)
    return (q * jnp.bfloat16(DH ** (-0.5))).reshape(rows, cols, width)


def project_kernel(own0_ref, own1_ref, low_ref, high_ref, w_ref, q_ref, kv_ref):
    rows, cols, width = low_ref.shape
    inner = slice(STRIP, STRIP + cols)
    for c, ref in enumerate((own0_ref, own1_ref)):
        q = queries_of(ref[...], w_ref[:, :width])
        for b in range(cols // QCOLS):
            q_ref[b, c * rows * QCOLS:(c + 1) * rows * QCOLS, :] = q[:, b * QCOLS:(b + 1) * QCOLS, :].reshape(rows * QCOLS, width)
    for ref, at in ((own0_ref, 2), (own1_ref, 3), (low_ref, 0), (high_ref, 4)):
        kv_ref[at * rows:(at + 1) * rows, inner, :] = keys_values(ref[...], w_ref[:, width:])


def project(own0, own1, low, high, w_qkv):
    rows, cols, width = low.shape
    return pl.pallas_call(
        project_kernel,
        in_specs=[vmem()] * 5,
        out_specs=[vmem()] * 2,
        out_shape=[
            pltpu.VMEM((cols // QCOLS, 2 * rows * QCOLS, width), jnp.bfloat16),
            pltpu.VMEM((6 * rows, cols + 2 * STRIP, 2 * width), jnp.bfloat16),
        ],
        compiler_params=params(LIMIT),
        cost_estimate=cost(2 * low.size * 10 * width, w_qkv.size * 2 + low.size * 24),
        name="project",
    )(own0, own1, low, high, w_qkv)


def window_bias(start_ref, first_ref, rows):
    keys = 3 * rows * KCOLS
    key = lax.broadcasted_iota(jnp.int32, (QCOLS, keys), 1)
    key_row = key // KCOLS
    shift = key % KCOLS - lax.broadcasted_iota(jnp.int32, (QCOLS, keys), 0)
    near = STRIP - WIN // 2
    col_ok = (shift >= near) & (shift < near + WIN)
    first_row = first_ref[0]
    bias = []
    for r in range(rows):
        start = start_ref[first_row + r] - first_row + LAT_REACH
        ok = col_ok & (key_row >= start) & (key_row < start + WIN)
        bias.append(jnp.where(ok, 0.0, MASKED))
    return jnp.concatenate(bias + bias, axis=0)


def attend_block(b, bias, q_ref, kv_ref, att_ref):
    _, queries, width = q_ref.shape
    keys = bias.shape[1]
    lane = lax.broadcasted_iota(jnp.int32, (queries, 128), 1)
    is_first = lane < DH
    ones = jnp.ones((keys, 128), jnp.bfloat16)
    band = slice(b * QCOLS, b * QCOLS + KCOLS)
    for p in range(width // 128):
        here = slice(p * 128, (p + 1) * 128)
        here_v = slice(width + p * 128, width + (p + 1) * 128)
        q = q_ref[b, :, here]
        zero = jnp.zeros_like(q)
        qq = jnp.concatenate([jnp.where(is_first, q, zero), jnp.where(is_first, zero, q)], axis=0)
        k = kv_ref[:, band, here].reshape(keys, 128)
        v = kv_ref[:, band, here_v].reshape(keys, 128)
        s = lax.dot_general(qq, k, (((1,), (1,)), ((), ())), preferred_element_type=jnp.float32) + bias
        e = jnp.exp(s - jnp.max(s, axis=-1, keepdims=True)).astype(jnp.bfloat16)
        o = jnp.dot(e, jnp.concatenate([v, ones], axis=1), preferred_element_type=jnp.float32)
        o = o[:, :128] / o[:, 128:]
        att_ref[b, :, here] = jnp.where(is_first, o[:queries], o[queries:]).astype(jnp.bfloat16)


def finish_block(b, rows, att_ref, wout_ref, emb_refs, write):
    mixed = jnp.dot(att_ref[b], wout_ref[...], preferred_element_type=jnp.float32)
    mixed = mixed.reshape(rows, QCOLS, mixed.shape[1])
    half = rows // 2
    for c, ref in enumerate(emb_refs):
        wide = ref[:, b * QCOLS:(b + 1) * QCOLS, :].astype(jnp.float32)
        write(slice(c * half, (c + 1) * half), (wide + mixed[c * half:(c + 1) * half]).astype(jnp.bfloat16))


def middle_kernel(start_ref, first_ref, q_ref, _, low_ref, high_ref, left_ref, right_ref, w_ref, wout_ref, emb0_ref, emb1_ref,
                  kv_ref, out_ref, att_ref):
    half, cols, width = low_ref.shape
    rows = 2 * half
    wkv = w_ref[:, width:]
    inner = slice(STRIP, STRIP + cols)
    kv_ref[half:rows, inner, :] = keys_values(low_ref[...], wkv)
    kv_ref[2 * rows + half:, inner, :] = keys_values(high_ref[...], wkv)
    bias = window_bias(start_ref, first_ref, rows)
    attend_block(1, bias, q_ref, kv_ref, att_ref)

    def write(at, value):
        out_ref[at] = value

    finish_block(1, rows, att_ref, wout_ref, (emb0_ref, emb1_ref), write)
    for side, at in ((left_ref, slice(0, STRIP)), (right_ref, slice(STRIP + cols, None))):
        strip = keys_values(side[...], wkv)
        kv_ref[:half, at, :] = strip[:half]
        kv_ref[rows:2 * rows, at, :] = strip[half:3 * half]
        kv_ref[2 * rows:2 * rows + half, at, :] = strip[3 * half:]


def middle(lat_start, first_row, q, kv, low, high, left, right, w_qkv, w_out, emb0, emb1):
    half, cols, width = low.shape
    return pl.pallas_call(
        middle_kernel,
        in_specs=[smem(), smem()] + [vmem()] * 10,
        out_specs=[vmem()] * 2,
        out_shape=[pltpu.VMEM(kv.shape, kv.dtype), pltpu.VMEM((2 * half, QCOLS, width), jnp.bfloat16)],
        input_output_aliases={3: 0},
        scratch_shapes=[pltpu.VMEM(q.shape, jnp.bfloat16)],
        compiler_params=params(LIMIT),
        cost_estimate=cost(8e9, 10e6, 1e6),
        name="middle",
    )(lat_start, first_row, q, kv, low, high, left, right, w_qkv, w_out, emb0, emb1)


def sides_kernel(start_ref, first_ref, q_ref, _, left_ref, right_ref, w_ref, wout_ref, emb0_ref, emb1_ref, middle_ref,
                 out_ref, kv_ref, att_ref):
    rows, cols, width = out_ref.shape
    half = rows // 2
    blocks = q_ref.shape[0]
    wkv = w_ref[:, width:]
    for side, at in ((left_ref, slice(0, STRIP)), (right_ref, slice(STRIP + cols, None))):
        strip = keys_values(side[...], wkv)
        kv_ref[half:rows, at, :] = strip[:half]
        kv_ref[2 * rows + half:, at, :] = strip[half:]
    bias = window_bias(start_ref, first_ref, rows)
    out_ref[:, QCOLS:2 * QCOLS, :] = middle_ref[...]
    for b in (0, blocks - 1):
        attend_block(b, bias, q_ref, kv_ref, att_ref)

        def write(at, value):
            out_ref[at, b * QCOLS:(b + 1) * QCOLS, :] = value

        finish_block(b, rows, att_ref, wout_ref, (emb0_ref, emb1_ref), write)


def sides(lat_start, first_row, q, kv, left, right, w_qkv, w_out, emb0, emb1, centre):
    half, cols, width = emb0.shape
    return pl.pallas_call(
        sides_kernel,
        in_specs=[smem(), smem()] + [vmem()] * 9,
        out_specs=[vmem()] * 2,
        out_shape=[jax.ShapeDtypeStruct((2 * half, cols, width), jnp.bfloat16), pltpu.VMEM(kv.shape, kv.dtype)],
        input_output_aliases={3: 1},
        scratch_shapes=[pltpu.VMEM(q.shape, jnp.bfloat16)],
        compiler_params=params(LIMIT),
        cost_estimate=cost(9e9, 10e6, 2e6),
        name="sides",
    )(lat_start, first_row, q, kv, left, right, w_qkv, w_out, emb0, emb1, centre)[0]


def ring(count, stride, step):
    return [
        (base + i * stride, base + (i + step) % count * stride)
        for base in range(stride)
        for i in range(count)
    ]


def quarter_of_weights(w_embed, plane, lev):
    size, half = w_embed.shape[0] // PLANES, w_embed.shape[1] // 2
    mine = lax.dynamic_slice_in_dim(w_embed, plane * size, size, 0)
    both = jnp.stack([mine[:, :half], mine[:, half:]], axis=0)
    sent = jnp.broadcast_to(both[None], (lev // 2, 2, size, half)).reshape(lev, size, half)
    return lax.all_to_all(sent, "lev", split_axis=0, concat_axis=0, tiled=True)


def weight_pieces(own, lat):
    stride = lat // PLANES
    up, down = ring(PLANES, stride, 1), ring(PLANES, stride, -1)
    near = [lax.ppermute(own, "lat", up), lax.ppermute(own, "lat", down)]
    half = own.shape[0] // 2
    far = [lax.ppermute(near[0][:half], "lat", up), lax.ppermute(near[1][half:], "lat", down)]
    pieces = [own] + near + far
    swap = [(i, i ^ 1) for i in range(own.shape[0])]
    return pieces + [lax.ppermute(piece, "lev", swap) for piece in pieces]


def per_device(
    fields, level_group, lat_start, w_embed, group_bias, group_gain, norm_gain, w_qkv, w_out
):
    rows = fields.shape[0]
    lev = lax.axis_size("lev")
    lat = lax.axis_size("lat")
    plane = lax.axis_index("lat") // (lat // PLANES)
    place = jnp.stack([plane, lax.axis_index("lev") % 2]).astype(jnp.int32)
    own = quarter_of_weights(w_embed, plane, lev)
    turned = jnp.transpose(fields, (0, 2, 1))
    pick = picks(level_group, lev, group_bias.shape[0])
    first_row = (lax.axis_index("lat") * rows).astype(jnp.int32).reshape(1)
    up = [(i, i + 1) for i in range(lat - 1)]
    down = [(b, a) for a, b in up]
    right_way = [(i, (i + 1) % lev) for i in range(lev)]
    left_way = [(b, a) for a, b in right_way]

    later, own, pick, place = lax.optimization_barrier((turned, own, pick, place))
    packed = [pack(later if c == 0 else turned, lev, c) for c in range(rows // CHUNK)]
    w_all = weight_pieces(own, lat)
    emb, normed, low, high = [], [], [], []
    for c in range(rows // CHUNK):
        if c > 0:
            packed[c] = held
        moved = lax.all_to_all(packed[c], "lev", split_axis=0, concat_axis=0, tiled=True)
        if c == 0:
            held, *w_all[1:8] = lax.optimization_barrier((packed[1], *w_all[1:8]))
        e, n, kept = embed(moved, place, w_all, pick, group_bias, group_gain, norm_gain)
        w_all = [kept]
        emb.append(e)
        normed.append(n)
        low.append(lax.ppermute(n, "lat", up))
        high.append(lax.ppermute(n, "lat", down))

    def strips(tall):
        left = lax.ppermute(jnp.concatenate([t[:, -STRIP:] for t in tall], axis=0), "lev", right_way)
        right = lax.ppermute(jnp.concatenate([t[:, :STRIP] for t in tall], axis=0), "lev", left_way)
        return left, right

    low[0], high[0], normed[1] = lax.optimization_barrier((low[0], high[0], normed[1]))
    left, right = strips([low[0], normed[0], normed[1], high[0]])
    q, kv = project(normed[0], normed[1], low[0], high[0], w_qkv)
    low[1], high[1], q = lax.optimization_barrier((low[1], high[1], q))
    last_left, last_right = strips([low[1], high[1]])
    kv, centre = middle(
        lat_start, first_row, q, kv, low[1], high[1], left, right, w_qkv, w_out, emb[0], emb[1]
    )
    return sides(lat_start, first_row, q, kv, last_left, last_right, w_qkv, w_out, emb[0], emb[1], centre)


def solution(mesh):
    return jax.shard_map(
        per_device,
        mesh=mesh,
        in_specs=(P("lat", None, "lev"), P(), P(), P("lev", None), P(), P(), P(), P(), P()),
        out_specs=P("lat", "lev", None),
        check_vma=False,
    )
```

```python
import functools

import jax
import jax.numpy as jnp
from jax import lax
from jax.experimental import pallas as pl
from jax.experimental.pallas import tpu as pltpu
from jax.sharding import PartitionSpec as P

DH = 64
IN_LEV = 24
WIN = 13
LAT_REACH = 8
STRIP = 8
QCOLS = 16
KCOLS = QCOLS + 2 * STRIP
PLANES = 4
CHUNK = 4
SOURCES = 4
MASKED = -1e30
PART = 256
PACK_FLOPS = (0, 18e9)
EMBED_LIMIT = 56
LIMIT = 36


def params(mib):
    return pltpu.CompilerParams(vmem_limit_bytes=mib << 20)


def cost(flops, nbytes, trans=0):
    return pl.CostEstimate(flops=int(flops), bytes_accessed=int(nbytes), transcendentals=int(trans))


def smem():
    return pl.BlockSpec(memory_space=pltpu.SMEM)


def vmem():
    return pl.BlockSpec(memory_space=pltpu.VMEM)


def pack_kernel(x_ref, o_ref):
    rows, width, lon_all = x_ref.shape
    lev = o_ref.shape[0]
    cols = lon_all // lev
    tokens = rows * cols

    def put(block, first):
        turned = block.T.reshape(lev, cols, 128)
        o_ref[:, first:first + cols, :] = turned

    for r in range(rows):
        put(x_ref[r, :128, :], r * cols)
    for r in range(rows // 2):
        both = jnp.concatenate([x_ref[r, 128:, :], x_ref[r + rows // 2, 128:, :]], axis=0)
        put(both, tokens + r * cols)


def pack(turned, lev, chunk):
    _, width, lon_all = turned.shape
    tokens = CHUNK * lon_all // lev
    return pl.pallas_call(
        pack_kernel,
        grid=(1,),
        in_specs=[pl.BlockSpec((CHUNK, width, lon_all), lambda i: (chunk, 0, 0))],
        out_specs=pl.BlockSpec((lev, tokens + tokens // 2, 128), lambda i: (0, 0, 0)),
        out_shape=jax.ShapeDtypeStruct((lev, tokens + tokens // 2, 128), turned.dtype),
        compiler_params=params(60),
        cost_estimate=cost(PACK_FLOPS[chunk], 2 * turned.size),
        name="pack",
    )(turned)


def weight_rows(w_ref, s, first, last):
    size = w_ref.shape[2]
    out = []
    for quarter in range(w_ref.shape[1]):
        low, high = max(first - quarter * size, 0), min(last - quarter * size, size)
        if low < high:
            out.append((s, quarter, low, high))
    return out


def embed_body(x_ref, w_ref, pick_ref, bias_ref, gain_ref, norm_ref, emb_ref, normed_ref, xs_ref, sum_ref, before):
    groups, width = bias_ref.shape
    lev, quarters, size, _ = w_ref.shape
    per = quarters * size
    part = PART
    tokens = xs_ref.shape[0] // groups
    span = SOURCES * per

    for c in range(lev // SOURCES):
        here = range(c * SOURCES, (c + 1) * SOURCES)
        main = [x_ref[s, :tokens, :] for s in here]
        low = jnp.concatenate([x_ref[s, tokens:, :64] for s in here], axis=1)
        high = jnp.concatenate([x_ref[s, tokens:, 64:] for s in here], axis=1)
        x = jnp.concatenate(main + [jnp.concatenate([low, high], axis=0)], axis=1)
        for g in range(groups):
            xs_ref[g * tokens:(g + 1) * tokens, c * span:(c + 1) * span] = x * pick_ref[g:g + 1, c * span:(c + 1) * span]

    for j in range(width // part):
        before(j)
        cols = slice(j * part, (j + 1) * part)
        acc = None
        for c in range(lev // SOURCES):
            here = range(c * SOURCES, (c + 1) * SOURCES)
            rows = [r for s in here for r in weight_rows(w_ref, s, 0, 128)]
            rows += [r for s in here for r in weight_rows(w_ref, s, 128, per)]
            w = jnp.concatenate([w_ref[s, quarter, low:high, cols] for s, quarter, low, high in rows], axis=0)
            term = jnp.dot(xs_ref[:, c * span:(c + 1) * span], w, preferred_element_type=jnp.float32)
            acc = term if acc is None else acc + term
        total = jnp.zeros((tokens, part), jnp.float32)
        for g in range(groups):
            v = acc[g * tokens:(g + 1) * tokens] + bias_ref[g:g + 1, cols]
            total += v / (1.0 + jnp.exp(-v)) * gain_ref[g:g + 1, cols]
        sum_ref[:, cols] = total

    emb = sum_ref[...].astype(jnp.bfloat16)
    wide = emb.astype(jnp.float32)
    inv = lax.rsqrt(jnp.mean(wide * wide, axis=-1, keepdims=True) + 1e-05)
    emb_ref[...] = emb.reshape(emb_ref.shape)
    normed_ref[...] = (wide * inv * norm_ref[...]).astype(jnp.bfloat16).reshape(normed_ref.shape)


def embed_first_kernel(place_ref, x_ref, pick_ref, bias_ref, gain_ref, norm_ref, *refs):
    pieces, (emb_ref, normed_ref, kept_ref, xs_ref, sum_ref, w_ref, sem) = refs[:10], refs[10:]
    lev, quarters, _, width = w_ref.shape
    half = width // 2
    plane, core = place_ref[0], place_ref[1]
    loads = []
    for sibling in (0, 1):
        column = pl.multiple_of(lax.rem(core + sibling, 2) * half, 128)
        spots = ((0, 0, lev), (quarters - 1, 0, lev), (1, 0, lev), (2, 0, lev // 2), (2, lev // 2, lev))
        for n, (ahead, first, last) in enumerate(spots):
            quarter = lax.rem(plane + ahead, quarters)
            loads.append(
                pltpu.make_async_copy(
                    pieces[sibling * 5 + n],
                    w_ref.at[first:last, quarter, :, pl.ds(column, half)],
                    sem.at[sibling * 5 + n],
                )
            )
    for load in loads:
        load.start()
    keep = pltpu.make_async_copy(w_ref, kept_ref, sem.at[10])

    def before(j):
        if j == 0:
            for load in loads:
                load.wait()
            keep.start()

    embed_body(x_ref, w_ref, pick_ref, bias_ref, gain_ref, norm_ref, emb_ref, normed_ref, xs_ref, sum_ref, before)
    keep.wait()


def embed_next_kernel(x_ref, pick_ref, bias_ref, gain_ref, norm_ref, kept_ref, emb_ref, normed_ref, xs_ref, sum_ref, w_ref, sem):
    loads = []
    for j in range(w_ref.shape[3] // PART):
        cols = slice(j * PART, (j + 1) * PART)
        loads.append(pltpu.make_async_copy(kept_ref.at[:, :, :, cols], w_ref.at[:, :, :, cols], sem.at[j]))
        loads[j].start()
    embed_body(
        x_ref, w_ref, pick_ref, bias_ref, gain_ref, norm_ref, emb_ref, normed_ref, xs_ref, sum_ref, lambda j: loads[j].wait()
    )


def embed(moved, place, w_all, pick, bias, gain, norm_gain):
    lev = moved.shape[0]
    tokens = moved.shape[1] * 2 // 3
    groups, width = bias.shape
    depth = pick.shape[1]
    cols = tokens // CHUNK
    out_shape = [jax.ShapeDtypeStruct((CHUNK, cols, width), jnp.bfloat16)] * 2
    size = w_all[0].shape[-2]
    kept = jax.ShapeDtypeStruct((lev, depth // lev // size, size, width), jnp.bfloat16)
    scratch = [
        pltpu.VMEM((groups * tokens, depth), jnp.bfloat16),
        pltpu.VMEM((tokens, width), jnp.float32),
        pltpu.VMEM(kept.shape, kept.dtype),
    ]
    far = pl.BlockSpec(memory_space=pl.ANY)
    common = dict(
        compiler_params=params(EMBED_LIMIT),
        cost_estimate=cost(2 * tokens * depth * width * groups, depth * width * 2 + tokens * depth * 2),
    )
    shared = (moved, pick, bias, gain, norm_gain[None, :])
    if len(w_all) > 1:
        return pl.pallas_call(
            embed_first_kernel,
            in_specs=[smem()] + [vmem()] * 5 + [far] * 10,
            out_specs=[vmem()] * 2 + [far],
            out_shape=out_shape + [kept],
            scratch_shapes=scratch + [pltpu.SemaphoreType.DMA((11,))],
            name="embed_first",
            **common,
        )(place, *shared, *w_all)
    return (
        *pl.pallas_call(
            embed_next_kernel,
            in_specs=[vmem()] * 5 + [far],
            out_specs=[vmem()] * 2,
            out_shape=out_shape,
            scratch_shapes=scratch + [pltpu.SemaphoreType.DMA((width // PART,))],
            name="embed_next",
            **common,
        )(*shared, *w_all),
        w_all[0],
    )


def picks(level_group, lev, groups):
    row_groups = jnp.repeat(level_group, IN_LEV).reshape(lev // SOURCES, SOURCES, -1)
    steps = row_groups.shape[0]
    order = jnp.concatenate(
        [row_groups[:, :, :128].reshape(steps, -1), row_groups[:, :, 128:].reshape(steps, -1)], axis=1
    ).reshape(-1)
    return (order[None, :] == jnp.arange(groups, dtype=jnp.int32)[:, None]).astype(jnp.bfloat16)


def keys_values(x, w):
    n = x.shape[0] * x.shape[1]
    out = jnp.dot(x.reshape(n, x.shape[2]), w, preferred_element_type=jnp.float32).astype(jnp.bfloat16)
    return out.reshape(x.shape[0], x.shape[1], w.shape[1])


def queries_of(x, w):
    rows, cols, width = x.shape
    q = jnp.dot(x.reshape(rows * cols, width), w, preferred_element_type=jnp.float32).astype(jnp.bfloat16)
    return (q * jnp.bfloat16(DH ** (-0.5))).reshape(rows, cols, width)


def project_kernel(own0_ref, own1_ref, low_ref, high_ref, w_ref, q_ref, kv_ref):
    rows, cols, width = low_ref.shape
    inner = slice(STRIP, STRIP + cols)
    for c, ref in enumerate((own0_ref, own1_ref)):
        q = queries_of(ref[...], w_ref[:, :width])
        for b in range(cols // QCOLS):
            q_ref[b, c * rows * QCOLS:(c + 1) * rows * QCOLS, :] = q[:, b * QCOLS:(b + 1) * QCOLS, :].reshape(rows * QCOLS, width)
    for ref, at in ((own0_ref, 2), (own1_ref, 3), (low_ref, 0), (high_ref, 4)):
        kv_ref[at * rows:(at + 1) * rows, inner, :] = keys_values(ref[...], w_ref[:, width:])


def project(own0, own1, low, high, w_qkv):
    rows, cols, width = low.shape
    return pl.pallas_call(
        project_kernel,
        in_specs=[vmem()] * 5,
        out_specs=[vmem()] * 2,
        out_shape=[
            pltpu.VMEM((cols // QCOLS, 2 * rows * QCOLS, width), jnp.bfloat16),
            pltpu.VMEM((6 * rows, cols + 2 * STRIP, 2 * width), jnp.bfloat16),
        ],
        compiler_params=params(LIMIT),
        cost_estimate=cost(2 * low.size * 10 * width, w_qkv.size * 2 + low.size * 24),
        name="project",
    )(own0, own1, low, high, w_qkv)


def window_bias(start_ref, first_ref, rows):
    keys = 3 * rows * KCOLS
    key = lax.broadcasted_iota(jnp.int32, (QCOLS, keys), 1)
    key_row = key // KCOLS
    shift = key % KCOLS - lax.broadcasted_iota(jnp.int32, (QCOLS, keys), 0)
    near = STRIP - WIN // 2
    col_ok = (shift >= near) & (shift < near + WIN)
    first_row = first_ref[0]
    bias = []
    for r in range(rows):
        start = start_ref[first_row + r] - first_row + LAT_REACH
        ok = col_ok & (key_row >= start) & (key_row < start + WIN)
        bias.append(jnp.where(ok, 0.0, MASKED))
    return jnp.concatenate(bias + bias, axis=0)


def attend_block(b, bias, q_ref, kv_ref, att_ref):
    _, queries, width = q_ref.shape
    keys = bias.shape[1]
    lane = lax.broadcasted_iota(jnp.int32, (queries, 128), 1)
    is_first = lane < DH
    ones = jnp.ones((keys, 128), jnp.bfloat16)
    band = slice(b * QCOLS, b * QCOLS + KCOLS)
    for p in range(width // 128):
        here = slice(p * 128, (p + 1) * 128)
        here_v = slice(width + p * 128, width + (p + 1) * 128)
        q = q_ref[b, :, here]
        zero = jnp.zeros_like(q)
        qq = jnp.concatenate([jnp.where(is_first, q, zero), jnp.where(is_first, zero, q)], axis=0)
        k = kv_ref[:, band, here].reshape(keys, 128)
        v = kv_ref[:, band, here_v].reshape(keys, 128)
        s = lax.dot_general(qq, k, (((1,), (1,)), ((), ())), preferred_element_type=jnp.float32) + bias
        e = jnp.exp(s - jnp.max(s, axis=-1, keepdims=True)).astype(jnp.bfloat16)
        o = jnp.dot(e, jnp.concatenate([v, ones], axis=1), preferred_element_type=jnp.float32)
        o = o[:, :128] / o[:, 128:]
        att_ref[b, :, here] = jnp.where(is_first, o[:queries], o[queries:]).astype(jnp.bfloat16)


def finish_block(b, rows, att_ref, wout_ref, emb_refs, write):
    mixed = jnp.dot(att_ref[b], wout_ref[...], preferred_element_type=jnp.float32)
    mixed = mixed.reshape(rows, QCOLS, mixed.shape[1])
    half = rows // 2
    for c, ref in enumerate(emb_refs):
        wide = ref[:, b * QCOLS:(b + 1) * QCOLS, :].astype(jnp.float32)
        write(slice(c * half, (c + 1) * half), (wide + mixed[c * half:(c + 1) * half]).astype(jnp.bfloat16))


def middle_kernel(start_ref, first_ref, q_ref, _, low_ref, high_ref, left_ref, right_ref, w_ref, wout_ref, emb0_ref, emb1_ref,
                  kv_ref, out_ref, att_ref):
    half, cols, width = low_ref.shape
    rows = 2 * half
    wkv = w_ref[:, width:]
    inner = slice(STRIP, STRIP + cols)
    kv_ref[half:rows, inner, :] = keys_values(low_ref[...], wkv)
    kv_ref[2 * rows + half:, inner, :] = keys_values(high_ref[...], wkv)
    bias = window_bias(start_ref, first_ref, rows)
    attend_block(1, bias, q_ref, kv_ref, att_ref)

    def write(at, value):
        out_ref[at] = value

    finish_block(1, rows, att_ref, wout_ref, (emb0_ref, emb1_ref), write)
    for side, at in ((left_ref, slice(0, STRIP)), (right_ref, slice(STRIP + cols, None))):
        strip = keys_values(side[...], wkv)
        kv_ref[:half, at, :] = strip[:half]
        kv_ref[rows:2 * rows, at, :] = strip[half:3 * half]
        kv_ref[2 * rows:2 * rows + half, at, :] = strip[3 * half:]


def middle(lat_start, first_row, q, kv, low, high, left, right, w_qkv, w_out, emb0, emb1):
    half, cols, width = low.shape
    return pl.pallas_call(
        middle_kernel,
        in_specs=[smem(), smem()] + [vmem()] * 10,
        out_specs=[vmem()] * 2,
        out_shape=[pltpu.VMEM(kv.shape, kv.dtype), pltpu.VMEM((2 * half, QCOLS, width), jnp.bfloat16)],
        input_output_aliases={3: 0},
        scratch_shapes=[pltpu.VMEM(q.shape, jnp.bfloat16)],
        compiler_params=params(LIMIT),
        cost_estimate=cost(8e9, 10e6, 1e6),
        name="middle",
    )(lat_start, first_row, q, kv, low, high, left, right, w_qkv, w_out, emb0, emb1)


def sides_kernel(start_ref, first_ref, q_ref, _, left_ref, right_ref, w_ref, wout_ref, emb0_ref, emb1_ref, middle_ref,
                 out_ref, kv_ref, att_ref):
    rows, cols, width = out_ref.shape
    half = rows // 2
    blocks = q_ref.shape[0]
    wkv = w_ref[:, width:]
    for side, at in ((left_ref, slice(0, STRIP)), (right_ref, slice(STRIP + cols, None))):
        strip = keys_values(side[...], wkv)
        kv_ref[half:rows, at, :] = strip[:half]
        kv_ref[2 * rows + half:, at, :] = strip[half:]
    bias = window_bias(start_ref, first_ref, rows)
    out_ref[:, QCOLS:2 * QCOLS, :] = middle_ref[...]
    for b in (0, blocks - 1):
        attend_block(b, bias, q_ref, kv_ref, att_ref)

        def write(at, value):
            out_ref[at, b * QCOLS:(b + 1) * QCOLS, :] = value

        finish_block(b, rows, att_ref, wout_ref, (emb0_ref, emb1_ref), write)


def sides(lat_start, first_row, q, kv, left, right, w_qkv, w_out, emb0, emb1, centre):
    half, cols, width = emb0.shape
    return pl.pallas_call(
        sides_kernel,
        in_specs=[smem(), smem()] + [vmem()] * 9,
        out_specs=[vmem()] * 2,
        out_shape=[jax.ShapeDtypeStruct((2 * half, cols, width), jnp.bfloat16), pltpu.VMEM(kv.shape, kv.dtype)],
        input_output_aliases={3: 1},
        scratch_shapes=[pltpu.VMEM(q.shape, jnp.bfloat16)],
        compiler_params=params(LIMIT),
        cost_estimate=cost(9e9, 10e6, 2e6),
        name="sides",
    )(lat_start, first_row, q, kv, left, right, w_qkv, w_out, emb0, emb1, centre)[0]


def ring(count, stride, step):
    return [
        (base + i * stride, base + (i + step) % count * stride)
        for base in range(stride)
        for i in range(count)
    ]


def quarter_of_weights(w_embed, plane, lev):
    size, half = w_embed.shape[0] // PLANES, w_embed.shape[1] // 2
    mine = lax.dynamic_slice_in_dim(w_embed, plane * size, size, 0)
    both = jnp.stack([mine[:, :half], mine[:, half:]], axis=0)
    sent = jnp.broadcast_to(both[None], (lev // 2, 2, size, half)).reshape(lev, size, half)
    return lax.all_to_all(sent, "lev", split_axis=0, concat_axis=0, tiled=True)


def weight_pieces(own, lat):
    stride = lat // PLANES
    up, down = ring(PLANES, stride, 1), ring(PLANES, stride, -1)
    near = [lax.ppermute(own, "lat", up), lax.ppermute(own, "lat", down)]
    half = own.shape[0] // 2
    far = [lax.ppermute(near[0][:half], "lat", up), lax.ppermute(near[1][half:], "lat", down)]
    pieces = [own] + near + far
    swap = [(i, i ^ 1) for i in range(own.shape[0])]
    return pieces + [lax.ppermute(piece, "lev", swap) for piece in pieces]


def per_device(
    fields, level_group, lat_start, w_embed, group_bias, group_gain, norm_gain, w_qkv, w_out
):
    rows = fields.shape[0]
    lev = lax.axis_size("lev")
    lat = lax.axis_size("lat")
    plane = lax.axis_index("lat") // (lat // PLANES)
    place = jnp.stack([plane, lax.axis_index("lev") % 2]).astype(jnp.int32)
    own = quarter_of_weights(w_embed, plane, lev)
    turned = jnp.transpose(fields, (0, 2, 1))
    pick = picks(level_group, lev, group_bias.shape[0])
    first_row = (lax.axis_index("lat") * rows).astype(jnp.int32).reshape(1)
    up = [(i, i + 1) for i in range(lat - 1)]
    down = [(b, a) for a, b in up]
    right_way = [(i, (i + 1) % lev) for i in range(lev)]
    left_way = [(b, a) for a, b in right_way]

    later, own, pick, place = lax.optimization_barrier((turned, own, pick, place))
    packed = [pack(later if c == 0 else turned, lev, c) for c in range(rows // CHUNK)]
    w_all = weight_pieces(own, lat)
    emb, normed, low, high = [], [], [], []
    for c in range(rows // CHUNK):
        if c > 0:
            packed[c] = held
        moved = lax.all_to_all(packed[c], "lev", split_axis=0, concat_axis=0, tiled=True)
        if c == 0:
            held, *w_all = lax.optimization_barrier((packed[1], *w_all))
        e, n, kept = embed(moved, place, w_all, pick, group_bias, group_gain, norm_gain)
        w_all = [kept]
        emb.append(e)
        normed.append(n)
        low.append(lax.ppermute(n, "lat", up))
        high.append(lax.ppermute(n, "lat", down))

    def strips(tall):
        left = lax.ppermute(jnp.concatenate([t[:, -STRIP:] for t in tall], axis=0), "lev", right_way)
        right = lax.ppermute(jnp.concatenate([t[:, :STRIP] for t in tall], axis=0), "lev", left_way)
        return left, right

    low[0], high[0], normed[1] = lax.optimization_barrier((low[0], high[0], normed[1]))
    left, right = strips([low[0], normed[0], normed[1], high[0]])
    q, kv = project(normed[0], normed[1], low[0], high[0], w_qkv)
    low[1], high[1], q = lax.optimization_barrier((low[1], high[1], q))
    last_left, last_right = strips([low[1], high[1]])
    kv, centre = middle(
        lat_start, first_row, q, kv, low[1], high[1], left, right, w_qkv, w_out, emb[0], emb[1]
    )
    return sides(lat_start, first_row, q, kv, last_left, last_right, w_qkv, w_out, emb[0], emb[1], centre)


def solution(mesh):
    return jax.shard_map(
        per_device,
        mesh=mesh,
        in_specs=(P("lat", None, "lev"), P(), P(), P("lev", None), P(), P(), P(), P(), P()),
        out_specs=P("lat", "lev", None),
        check_vma=False,
    )
```

```python
import functools

import jax
import jax.numpy as jnp
from jax import lax
from jax.experimental import pallas as pl
from jax.experimental.pallas import tpu as pltpu
from jax.sharding import PartitionSpec as P

DH = 64
IN_LEV = 24
WIN = 13
LAT_REACH = 8
STRIP = 8
QCOLS = 16
KCOLS = QCOLS + 2 * STRIP
PLANES = 4
CHUNK = 4
SOURCES = 4
MASKED = -1e30
PART = 256
SPLIT_FLOPS = 18e9
FIRST_LIMIT = 56
NEXT_LIMIT = 50
LIMIT = 36


def params(mib):
    return pltpu.CompilerParams(vmem_limit_bytes=mib << 20)


def cost(flops, nbytes, trans=0):
    return pl.CostEstimate(flops=int(flops), bytes_accessed=int(nbytes), transcendentals=int(trans))


def smem():
    return pl.BlockSpec(memory_space=pltpu.SMEM)


def vmem():
    return pl.BlockSpec(memory_space=pltpu.VMEM)


def pack_kernel(x_ref, o_ref):
    rows, width, lon_all = x_ref.shape
    lev = o_ref.shape[0]
    cols = lon_all // lev
    tokens = rows * cols

    def put(block, first):
        turned = block.T.reshape(lev, cols, 128)
        o_ref[:, first:first + cols, :] = turned

    for r in range(rows):
        put(x_ref[r, :128, :], r * cols)
    for r in range(rows // 2):
        both = jnp.concatenate([x_ref[r, 128:, :], x_ref[r + rows // 2, 128:, :]], axis=0)
        put(both, tokens + r * cols)


def pack(turned, lev, chunk):
    _, width, lon_all = turned.shape
    tokens = CHUNK * lon_all // lev
    return pl.pallas_call(
        pack_kernel,
        grid=(1,),
        in_specs=[pl.BlockSpec((CHUNK, width, lon_all), lambda i: (chunk, 0, 0))],
        out_specs=pl.BlockSpec((lev, tokens + tokens // 2, 128), lambda i: (0, 0, 0)),
        out_shape=jax.ShapeDtypeStruct((lev, tokens + tokens // 2, 128), turned.dtype),
        compiler_params=params(60),
        cost_estimate=cost(0, 2 * turned.size),
        name="pack",
    )(turned)


def weight_rows(w_ref, s, first, last):
    size = w_ref.shape[2]
    out = []
    for quarter in range(w_ref.shape[1]):
        low, high = max(first - quarter * size, 0), min(last - quarter * size, size)
        if low < high:
            out.append((s, quarter, low, high))
    return out


def embed_body(x_ref, w_ref, pick_ref, bias_ref, gain_ref, norm_ref, emb_ref, normed_ref, xs_ref, sum_ref, before):
    groups, width = bias_ref.shape
    lev, quarters, size, _ = w_ref.shape
    per = quarters * size
    part = PART
    tokens = xs_ref.shape[0] // groups
    span = SOURCES * per

    for c in range(lev // SOURCES):
        here = range(c * SOURCES, (c + 1) * SOURCES)
        main = [x_ref[s, :tokens, :] for s in here]
        low = jnp.concatenate([x_ref[s, tokens:, :64] for s in here], axis=1)
        high = jnp.concatenate([x_ref[s, tokens:, 64:] for s in here], axis=1)
        x = jnp.concatenate(main + [jnp.concatenate([low, high], axis=0)], axis=1)
        for g in range(groups):
            xs_ref[g * tokens:(g + 1) * tokens, c * span:(c + 1) * span] = x * pick_ref[g:g + 1, c * span:(c + 1) * span]

    for j in range(width // part):
        before(j)
        cols = slice(j * part, (j + 1) * part)
        acc = None
        for c in range(lev // SOURCES):
            here = range(c * SOURCES, (c + 1) * SOURCES)
            rows = [r for s in here for r in weight_rows(w_ref, s, 0, 128)]
            rows += [r for s in here for r in weight_rows(w_ref, s, 128, per)]
            w = jnp.concatenate([w_ref[s, quarter, low:high, cols] for s, quarter, low, high in rows], axis=0)
            term = jnp.dot(xs_ref[:, c * span:(c + 1) * span], w, preferred_element_type=jnp.float32)
            acc = term if acc is None else acc + term
        total = jnp.zeros((tokens, part), jnp.float32)
        for g in range(groups):
            v = acc[g * tokens:(g + 1) * tokens] + bias_ref[g:g + 1, cols]
            total += v / (1.0 + jnp.exp(-v)) * gain_ref[g:g + 1, cols]
        sum_ref[:, cols] = total

    emb = sum_ref[...].astype(jnp.bfloat16)
    wide = emb.astype(jnp.float32)
    inv = lax.rsqrt(jnp.mean(wide * wide, axis=-1, keepdims=True) + 1e-05)
    emb_ref[...] = emb.reshape(emb_ref.shape)
    normed_ref[...] = (wide * inv * norm_ref[...]).astype(jnp.bfloat16).reshape(normed_ref.shape)


def embed_first_kernel(place_ref, x_ref, pick_ref, bias_ref, gain_ref, norm_ref, *refs):
    pieces, (emb_ref, normed_ref, kept_ref, xs_ref, sum_ref, w_ref, sem) = refs[:10], refs[10:]
    lev, quarters, _, width = w_ref.shape
    half = width // 2
    plane, core = place_ref[0], place_ref[1]
    loads = []
    for sibling in (0, 1):
        column = pl.multiple_of(lax.rem(core + sibling, 2) * half, 128)
        spots = ((0, 0, lev), (quarters - 1, 0, lev), (1, 0, lev), (2, 0, lev // 2), (2, lev // 2, lev))
        for n, (ahead, first, last) in enumerate(spots):
            quarter = lax.rem(plane + ahead, quarters)
            loads.append(
                pltpu.make_async_copy(
                    pieces[sibling * 5 + n],
                    w_ref.at[first:last, quarter, :, pl.ds(column, half)],
                    sem.at[sibling * 5 + n],
                )
            )
    for load in loads:
        load.start()
    keep = pltpu.make_async_copy(w_ref, kept_ref, sem.at[10])

    def before(j):
        if j == 0:
            for load in loads:
                load.wait()
            keep.start()

    embed_body(x_ref, w_ref, pick_ref, bias_ref, gain_ref, norm_ref, emb_ref, normed_ref, xs_ref, sum_ref, before)
    keep.wait()


def embed_next_kernel(x_ref, pick_ref, bias_ref, gain_ref, norm_ref, kept_ref, emb_ref, normed_ref, xs_ref, sum_ref, w_ref, sem):
    loads = []
    for j in range(w_ref.shape[3] // PART):
        cols = slice(j * PART, (j + 1) * PART)
        loads.append(pltpu.make_async_copy(kept_ref.at[:, :, :, cols], w_ref.at[:, :, :, cols], sem.at[j]))
        loads[j].start()
    embed_body(
        x_ref, w_ref, pick_ref, bias_ref, gain_ref, norm_ref, emb_ref, normed_ref, xs_ref, sum_ref, lambda j: loads[j].wait()
    )


def embed(moved, place, w_all, pick, bias, gain, norm_gain):
    lev = moved.shape[0]
    tokens = moved.shape[1] * 2 // 3
    groups, width = bias.shape
    depth = pick.shape[1]
    cols = tokens // CHUNK
    out_shape = [jax.ShapeDtypeStruct((CHUNK, cols, width), jnp.bfloat16)] * 2
    size = w_all[0].shape[-2]
    kept = jax.ShapeDtypeStruct((lev, depth // lev // size, size, width), jnp.bfloat16)
    scratch = [
        pltpu.VMEM((groups * tokens, depth), jnp.bfloat16),
        pltpu.VMEM((tokens, width), jnp.float32),
        pltpu.VMEM(kept.shape, kept.dtype),
    ]
    far = pl.BlockSpec(memory_space=pl.ANY)
    common = dict(
        compiler_params=params(FIRST_LIMIT if len(w_all) > 1 else NEXT_LIMIT),
        cost_estimate=cost(2 * tokens * depth * width * groups, depth * width * 2 + tokens * depth * 2),
    )
    shared = (moved, pick, bias, gain, norm_gain)
    if len(w_all) > 1:
        return pl.pallas_call(
            embed_first_kernel,
            in_specs=[smem()] + [vmem()] * 5 + [far] * 10,
            out_specs=[vmem()] * 2 + [far],
            out_shape=out_shape + [kept],
            scratch_shapes=scratch + [pltpu.SemaphoreType.DMA((11,))],
            name="embed_first",
            **common,
        )(place, *shared, *w_all)
    return (
        *pl.pallas_call(
            embed_next_kernel,
            in_specs=[vmem()] * 5 + [far],
            out_specs=[vmem()] * 2,
            out_shape=out_shape,
            scratch_shapes=scratch + [pltpu.SemaphoreType.DMA((width // PART,))],
            name="embed_next",
            **common,
        )(*shared, *w_all),
        w_all[0],
    )


def picks(level_group, lev, groups):
    row_groups = jnp.repeat(level_group, IN_LEV).reshape(lev // SOURCES, SOURCES, -1)
    steps = row_groups.shape[0]
    order = jnp.concatenate(
        [row_groups[:, :, :128].reshape(steps, -1), row_groups[:, :, 128:].reshape(steps, -1)], axis=1
    ).reshape(-1)
    return (order[None, :] == jnp.arange(groups, dtype=jnp.int32)[:, None]).astype(jnp.bfloat16)


def keys_values(x, w):
    n = x.shape[0] * x.shape[1]
    out = jnp.dot(x.reshape(n, x.shape[2]), w, preferred_element_type=jnp.float32).astype(jnp.bfloat16)
    return out.reshape(x.shape[0], x.shape[1], w.shape[1])


def queries_of(x, w):
    rows, cols, width = x.shape
    q = jnp.dot(x.reshape(rows * cols, width), w, preferred_element_type=jnp.float32).astype(jnp.bfloat16)
    return (q * jnp.bfloat16(DH ** (-0.5))).reshape(rows, cols, width)


def project_kernel(own0_ref, own1_ref, low_ref, high_ref, w_ref, q_ref, kv_ref):
    rows, cols, width = low_ref.shape
    inner = slice(STRIP, STRIP + cols)
    for c, ref in enumerate((own0_ref, own1_ref)):
        q = queries_of(ref[...], w_ref[:, :width])
        for b in range(cols // QCOLS):
            q_ref[b, c * rows * QCOLS:(c + 1) * rows * QCOLS, :] = q[:, b * QCOLS:(b + 1) * QCOLS, :].reshape(rows * QCOLS, width)
    for ref, at in ((own0_ref, 2), (own1_ref, 3), (low_ref, 0), (high_ref, 4)):
        kv_ref[at * rows:(at + 1) * rows, inner, :] = keys_values(ref[...], w_ref[:, width:])


def project(own0, own1, low, high, w_qkv):
    rows, cols, width = low.shape
    return pl.pallas_call(
        project_kernel,
        in_specs=[vmem()] * 5,
        out_specs=[vmem()] * 2,
        out_shape=[
            pltpu.VMEM((cols // QCOLS, 2 * rows * QCOLS, width), jnp.bfloat16),
            pltpu.VMEM((6 * rows, cols + 2 * STRIP, 2 * width), jnp.bfloat16),
        ],
        compiler_params=params(LIMIT),
        cost_estimate=cost(2 * low.size * 10 * width, w_qkv.size * 2 + low.size * 24),
        name="project",
    )(own0, own1, low, high, w_qkv)


def window_bias(start_ref, first_ref, rows):
    keys = 3 * rows * KCOLS
    key = lax.broadcasted_iota(jnp.int32, (QCOLS, keys), 1)
    key_row = key // KCOLS
    shift = key % KCOLS - lax.broadcasted_iota(jnp.int32, (QCOLS, keys), 0)
    near = STRIP - WIN // 2
    col_ok = (shift >= near) & (shift < near + WIN)
    first_row = first_ref[0]
    bias = []
    for r in range(rows):
        start = start_ref[first_row + r] - first_row + LAT_REACH
        ok = col_ok & (key_row >= start) & (key_row < start + WIN)
        bias.append(jnp.where(ok, 0.0, MASKED))
    return jnp.concatenate(bias + bias, axis=0)


def attend_block(b, bias, q_ref, kv_ref, att_ref):
    _, queries, width = q_ref.shape
    keys = bias.shape[1]
    lane = lax.broadcasted_iota(jnp.int32, (queries, 128), 1)
    is_first = lane < DH
    ones = jnp.ones((keys, 128), jnp.bfloat16)
    band = slice(b * QCOLS, b * QCOLS + KCOLS)
    for p in range(width // 128):
        here = slice(p * 128, (p + 1) * 128)
        here_v = slice(width + p * 128, width + (p + 1) * 128)
        q = q_ref[b, :, here]
        zero = jnp.zeros_like(q)
        qq = jnp.concatenate([jnp.where(is_first, q, zero), jnp.where(is_first, zero, q)], axis=0)
        k = kv_ref[:, band, here].reshape(keys, 128)
        v = kv_ref[:, band, here_v].reshape(keys, 128)
        s = lax.dot_general(qq, k, (((1,), (1,)), ((), ())), preferred_element_type=jnp.float32) + bias
        e = jnp.exp(s - jnp.max(s, axis=-1, keepdims=True)).astype(jnp.bfloat16)
        o = jnp.dot(e, jnp.concatenate([v, ones], axis=1), preferred_element_type=jnp.float32)
        o = o[:, :128] / o[:, 128:]
        att_ref[b, :, here] = jnp.where(is_first, o[:queries], o[queries:]).astype(jnp.bfloat16)


def finish_block(b, rows, att_ref, wout_ref, emb_refs, write):
    mixed = jnp.dot(att_ref[b], wout_ref[...], preferred_element_type=jnp.float32)
    mixed = mixed.reshape(rows, QCOLS, mixed.shape[1])
    half = rows // 2
    for c, ref in enumerate(emb_refs):
        wide = ref[:, b * QCOLS:(b + 1) * QCOLS, :].astype(jnp.float32)
        write(slice(c * half, (c + 1) * half), (wide + mixed[c * half:(c + 1) * half]).astype(jnp.bfloat16))


def middle_kernel(start_ref, first_ref, q_ref, _, low_ref, high_ref, left_ref, right_ref, w_ref, wout_ref, emb0_ref, emb1_ref,
                  kv_ref, out_ref, att_ref):
    half, cols, width = low_ref.shape
    rows = 2 * half
    wkv = w_ref[:, width:]
    inner = slice(STRIP, STRIP + cols)
    kv_ref[half:rows, inner, :] = keys_values(low_ref[...], wkv)
    kv_ref[2 * rows + half:, inner, :] = keys_values(high_ref[...], wkv)
    bias = window_bias(start_ref, first_ref, rows)
    attend_block(1, bias, q_ref, kv_ref, att_ref)

    def write(at, value):
        out_ref[at] = value

    finish_block(1, rows, att_ref, wout_ref, (emb0_ref, emb1_ref), write)
    for side, at in ((left_ref, slice(0, STRIP)), (right_ref, slice(STRIP + cols, None))):
        strip = keys_values(side[...], wkv)
        kv_ref[:half, at, :] = strip[:half]
        kv_ref[rows:2 * rows, at, :] = strip[half:3 * half]
        kv_ref[2 * rows:2 * rows + half, at, :] = strip[3 * half:]


def middle(lat_start, first_row, q, kv, low, high, left, right, w_qkv, w_out, emb0, emb1):
    half, cols, width = low.shape
    return pl.pallas_call(
        middle_kernel,
        in_specs=[smem(), smem()] + [vmem()] * 10,
        out_specs=[vmem()] * 2,
        out_shape=[pltpu.VMEM(kv.shape, kv.dtype), pltpu.VMEM((2 * half, QCOLS, width), jnp.bfloat16)],
        input_output_aliases={3: 0},
        scratch_shapes=[pltpu.VMEM(q.shape, jnp.bfloat16)],
        compiler_params=params(LIMIT),
        cost_estimate=cost(8e9, 10e6, 1e6),
        name="middle",
    )(lat_start, first_row, q, kv, low, high, left, right, w_qkv, w_out, emb0, emb1)


def sides_kernel(start_ref, first_ref, q_ref, _, left_ref, right_ref, w_ref, wout_ref, emb0_ref, emb1_ref, middle_ref,
                 out_ref, kv_ref, att_ref):
    rows, cols, width = out_ref.shape
    half = rows // 2
    blocks = q_ref.shape[0]
    wkv = w_ref[:, width:]
    for side, at in ((left_ref, slice(0, STRIP)), (right_ref, slice(STRIP + cols, None))):
        strip = keys_values(side[...], wkv)
        kv_ref[half:rows, at, :] = strip[:half]
        kv_ref[2 * rows + half:, at, :] = strip[half:]
    bias = window_bias(start_ref, first_ref, rows)
    out_ref[:, QCOLS:2 * QCOLS, :] = middle_ref[...]
    for b in (0, blocks - 1):
        attend_block(b, bias, q_ref, kv_ref, att_ref)

        def write(at, value):
            out_ref[at, b * QCOLS:(b + 1) * QCOLS, :] = value

        finish_block(b, rows, att_ref, wout_ref, (emb0_ref, emb1_ref), write)


def sides(lat_start, first_row, q, kv, left, right, w_qkv, w_out, emb0, emb1, centre):
    half, cols, width = emb0.shape
    return pl.pallas_call(
        sides_kernel,
        in_specs=[smem(), smem()] + [vmem()] * 9,
        out_specs=[vmem()] * 2,
        out_shape=[jax.ShapeDtypeStruct((2 * half, cols, width), jnp.bfloat16), pltpu.VMEM(kv.shape, kv.dtype)],
        input_output_aliases={3: 1},
        scratch_shapes=[pltpu.VMEM(q.shape, jnp.bfloat16)],
        compiler_params=params(LIMIT),
        cost_estimate=cost(9e9, 10e6, 2e6),
        name="sides",
    )(lat_start, first_row, q, kv, left, right, w_qkv, w_out, emb0, emb1, centre)[0]


def ring(count, stride, step):
    return [
        (base + i * stride, base + (i + step) % count * stride)
        for base in range(stride)
        for i in range(count)
    ]


def quarter_of_weights(w_embed, plane, lev):
    size, half = w_embed.shape[0] // PLANES, w_embed.shape[1] // 2
    mine = lax.dynamic_slice_in_dim(w_embed, plane * size, size, 0)
    both = jnp.stack([mine[:, :half], mine[:, half:]], axis=0)
    sent = jnp.broadcast_to(both[None], (lev // 2, 2, size, half)).reshape(lev, size, half)
    return lax.all_to_all(sent, "lev", split_axis=0, concat_axis=0, tiled=True)


def split_kernel(up_ref, down_ref, first_ref, second_ref):
    first_ref[...] = up_ref[...]
    second_ref[...] = down_ref[...]


def split(from_up, from_down):
    lev, size, half = from_up.shape
    block = (lev // 2, size, half)
    return pl.pallas_call(
        split_kernel,
        grid=(1,),
        in_specs=[pl.BlockSpec(block, lambda i: (0, 0, 0)), pl.BlockSpec(block, lambda i: (1, 0, 0))],
        out_specs=[pl.BlockSpec(block, lambda i: (0, 0, 0))] * 2,
        out_shape=[jax.ShapeDtypeStruct(block, from_up.dtype)] * 2,
        compiler_params=params(LIMIT),
        cost_estimate=cost(SPLIT_FLOPS, 4 * from_up.size),
        name="split",
    )(from_up, from_down)


def weight_pieces(own, lat):
    stride = lat // PLANES
    up, down = ring(PLANES, stride, 1), ring(PLANES, stride, -1)
    near = [lax.ppermute(own, "lat", up), lax.ppermute(own, "lat", down)]
    first, second = split(*near)
    far = [lax.ppermute(first, "lat", up), lax.ppermute(second, "lat", down)]
    pieces = [own] + near + far
    swap = [(i, i ^ 1) for i in range(own.shape[0])]
    return pieces + [lax.ppermute(piece, "lev", swap) for piece in pieces]


def per_device(
    fields, level_group, lat_start, w_embed, group_bias, group_gain, norm_gain, w_qkv, w_out
):
    rows = fields.shape[0]
    lev = lax.axis_size("lev")
    lat = lax.axis_size("lat")
    plane = lax.axis_index("lat") // (lat // PLANES)
    place = jnp.stack([plane, lax.axis_index("lev") % 2]).astype(jnp.int32)
    own = quarter_of_weights(w_embed, plane, lev)
    turned = jnp.transpose(fields, (0, 2, 1))
    pick = picks(level_group, lev, group_bias.shape[0])
    first_row = (lax.axis_index("lat") * rows).astype(jnp.int32).reshape(1)
    up = [(i, i + 1) for i in range(lat - 1)]
    down = [(b, a) for a, b in up]
    right_way = [(i, (i + 1) % lev) for i in range(lev)]
    left_way = [(b, a) for a, b in right_way]

    packed = [pack(turned, lev, c) for c in range(rows // CHUNK)]
    norm_gain = norm_gain[None, :]
    *packed, own, pick, place, norm_gain = lax.optimization_barrier((*packed, own, pick, place, norm_gain))
    w_all = weight_pieces(own, lat)
    emb, normed, low, high = [], [], [], []
    for c in range(rows // CHUNK):
        if c > 0:
            packed[c] = held
        moved = lax.all_to_all(packed[c], "lev", split_axis=0, concat_axis=0, tiled=True)
        if c == 0:
            held, *w_all[1:8] = lax.optimization_barrier((packed[1], *w_all[1:8]))
        e, n, kept = embed(moved, place, w_all, pick, group_bias, group_gain, norm_gain)
        w_all = [kept]
        emb.append(e)
        normed.append(n)
        low.append(lax.ppermute(n, "lat", up))
        high.append(lax.ppermute(n, "lat", down))

    def strips(tall):
        left = lax.ppermute(jnp.concatenate([t[:, -STRIP:] for t in tall], axis=0), "lev", right_way)
        right = lax.ppermute(jnp.concatenate([t[:, :STRIP] for t in tall], axis=0), "lev", left_way)
        return left, right

    low[0], high[0], normed[1] = lax.optimization_barrier((low[0], high[0], normed[1]))
    left, right = strips([low[0], normed[0], normed[1], high[0]])
    q, kv = project(normed[0], normed[1], low[0], high[0], w_qkv)
    low[1], high[1], q = lax.optimization_barrier((low[1], high[1], q))
    last_left, last_right = strips([low[1], high[1]])
    kv, centre = middle(
        lat_start, first_row, q, kv, low[1], high[1], left, right, w_qkv, w_out, emb[0], emb[1]
    )
    return sides(lat_start, first_row, q, kv, last_left, last_right, w_qkv, w_out, emb[0], emb[1], centre)


def solution(mesh):
    return jax.shard_map(
        per_device,
        mesh=mesh,
        in_specs=(P("lat", None, "lev"), P(), P(), P("lev", None), P(), P(), P(), P(), P()),
        out_specs=P("lat", "lev", None),
        check_vma=False,
    )
```

```python
import functools

import jax
import jax.numpy as jnp
from jax import lax
from jax.experimental import pallas as pl
from jax.experimental.pallas import tpu as pltpu
from jax.sharding import PartitionSpec as P

DH = 64
IN_LEV = 24
WIN = 13
LAT_REACH = 8
STRIP = 8
QCOLS = 16
KCOLS = QCOLS + 2 * STRIP
PLANES = 4
CHUNK = 4
SOURCES = 4
MASKED = -1e30
PART = 256
SPLIT_FLOPS = 18e9
FIRST_LIMIT = 56
NEXT_LIMIT = 50
LIMIT = 36


def params(mib):
    return pltpu.CompilerParams(vmem_limit_bytes=mib << 20)


def cost(flops, nbytes, trans=0):
    return pl.CostEstimate(flops=int(flops), bytes_accessed=int(nbytes), transcendentals=int(trans))


def smem():
    return pl.BlockSpec(memory_space=pltpu.SMEM)


def vmem():
    return pl.BlockSpec(memory_space=pltpu.VMEM)


def pack_kernel(x_ref, o_ref):
    rows, width, lon_all = x_ref.shape
    lev = o_ref.shape[0]
    cols = lon_all // lev
    tokens = rows * cols

    def put(block, first):
        turned = block.T.reshape(lev, cols, 128)
        o_ref[:, first:first + cols, :] = turned

    for r in range(rows):
        put(x_ref[r, :128, :], r * cols)
    for r in range(rows // 2):
        both = jnp.concatenate([x_ref[r, 128:, :], x_ref[r + rows // 2, 128:, :]], axis=0)
        put(both, tokens + r * cols)


def pack(turned, lev, chunk):
    _, width, lon_all = turned.shape
    tokens = CHUNK * lon_all // lev
    return pl.pallas_call(
        pack_kernel,
        grid=(1,),
        in_specs=[pl.BlockSpec((CHUNK, width, lon_all), lambda i: (chunk, 0, 0))],
        out_specs=pl.BlockSpec((lev, tokens + tokens // 2, 128), lambda i: (0, 0, 0)),
        out_shape=jax.ShapeDtypeStruct((lev, tokens + tokens // 2, 128), turned.dtype),
        compiler_params=params(60),
        cost_estimate=cost(0, 2 * turned.size),
        name="pack",
    )(turned)


def weight_rows(w_ref, s, first, last):
    size = w_ref.shape[2]
    out = []
    for quarter in range(w_ref.shape[1]):
        low, high = max(first - quarter * size, 0), min(last - quarter * size, size)
        if low < high:
            out.append((s, quarter, low, high))
    return out


def embed_body(x_ref, w_ref, pick_ref, bias_ref, gain_ref, norm_ref, emb_ref, normed_ref, xs_ref, sum_ref, before):
    groups, width = bias_ref.shape
    lev, quarters, size, _ = w_ref.shape
    per = quarters * size
    part = PART
    tokens = xs_ref.shape[0] // groups
    span = SOURCES * per

    for c in range(lev // SOURCES):
        here = range(c * SOURCES, (c + 1) * SOURCES)
        main = [x_ref[s, :tokens, :] for s in here]
        low = jnp.concatenate([x_ref[s, tokens:, :64] for s in here], axis=1)
        high = jnp.concatenate([x_ref[s, tokens:, 64:] for s in here], axis=1)
        x = jnp.concatenate(main + [jnp.concatenate([low, high], axis=0)], axis=1)
        for g in range(groups):
            xs_ref[g * tokens:(g + 1) * tokens, c * span:(c + 1) * span] = x * pick_ref[g:g + 1, c * span:(c + 1) * span]

    for j in range(width // part):
        before(j)
        cols = slice(j * part, (j + 1) * part)
        acc = None
        for c in range(lev // SOURCES):
            here = range(c * SOURCES, (c + 1) * SOURCES)
            rows = [r for s in here for r in weight_rows(w_ref, s, 0, 128)]
            rows += [r for s in here for r in weight_rows(w_ref, s, 128, per)]
            w = jnp.concatenate([w_ref[s, quarter, low:high, cols] for s, quarter, low, high in rows], axis=0)
            term = jnp.dot(xs_ref[:, c * span:(c + 1) * span], w, preferred_element_type=jnp.float32)
            acc = term if acc is None else acc + term
        total = jnp.zeros((tokens, part), jnp.float32)
        for g in range(groups):
            v = acc[g * tokens:(g + 1) * tokens] + bias_ref[g:g + 1, cols]
            total += v / (1.0 + jnp.exp(-v)) * gain_ref[g:g + 1, cols]
        sum_ref[:, cols] = total

    emb = sum_ref[...].astype(jnp.bfloat16)
    wide = emb.astype(jnp.float32)
    inv = lax.rsqrt(jnp.mean(wide * wide, axis=-1, keepdims=True) + 1e-05)
    emb_ref[...] = emb.reshape(emb_ref.shape)
    normed_ref[...] = (wide * inv * norm_ref[...]).astype(jnp.bfloat16).reshape(normed_ref.shape)


def embed_first_kernel(place_ref, x_ref, pick_ref, bias_ref, gain_ref, norm_ref, *refs):
    pieces, (emb_ref, normed_ref, kept_ref, xs_ref, sum_ref, w_ref, sem) = refs[:10], refs[10:]
    lev, quarters, _, width = w_ref.shape
    half = width // 2
    plane, core = place_ref[0], place_ref[1]
    loads = []
    for sibling in (0, 1):
        column = pl.multiple_of(lax.rem(core + sibling, 2) * half, 128)
        spots = ((0, 0, lev), (quarters - 1, 0, lev), (1, 0, lev), (2, 0, lev // 2), (2, lev // 2, lev))
        for n, (ahead, first, last) in enumerate(spots):
            quarter = lax.rem(plane + ahead, quarters)
            loads.append(
                pltpu.make_async_copy(
                    pieces[sibling * 5 + n],
                    w_ref.at[first:last, quarter, :, pl.ds(column, half)],
                    sem.at[sibling * 5 + n],
                )
            )
    for load in loads:
        load.start()
    keep = pltpu.make_async_copy(w_ref, kept_ref, sem.at[10])

    def before(j):
        if j == 0:
            for load in loads:
                load.wait()
            keep.start()

    embed_body(x_ref, w_ref, pick_ref, bias_ref, gain_ref, norm_ref, emb_ref, normed_ref, xs_ref, sum_ref, before)
    keep.wait()


def embed_next_kernel(x_ref, pick_ref, bias_ref, gain_ref, norm_ref, kept_ref, emb_ref, normed_ref, xs_ref, sum_ref, w_ref, sem):
    loads = []
    for j in range(w_ref.shape[3] // PART):
        cols = slice(j * PART, (j + 1) * PART)
        loads.append(pltpu.make_async_copy(kept_ref.at[:, :, :, cols], w_ref.at[:, :, :, cols], sem.at[j]))
        loads[j].start()
    embed_body(
        x_ref, w_ref, pick_ref, bias_ref, gain_ref, norm_ref, emb_ref, normed_ref, xs_ref, sum_ref, lambda j: loads[j].wait()
    )


def embed(moved, place, w_all, pick, bias, gain, norm_gain):
    lev = moved.shape[0]
    tokens = moved.shape[1] * 2 // 3
    groups, width = bias.shape
    depth = pick.shape[1]
    cols = tokens // CHUNK
    out_shape = [jax.ShapeDtypeStruct((CHUNK, cols, width), jnp.bfloat16)] * 2
    size = w_all[0].shape[-2]
    kept = jax.ShapeDtypeStruct((lev, depth // lev // size, size, width), jnp.bfloat16)
    scratch = [
        pltpu.VMEM((groups * tokens, depth), jnp.bfloat16),
        pltpu.VMEM((tokens, width), jnp.float32),
        pltpu.VMEM(kept.shape, kept.dtype),
    ]
    far = pl.BlockSpec(memory_space=pl.ANY)
    common = dict(
        compiler_params=params(FIRST_LIMIT if len(w_all) > 1 else NEXT_LIMIT),
        cost_estimate=cost(2 * tokens * depth * width * groups, depth * width * 2 + tokens * depth * 2),
    )
    shared = (moved, pick, bias, gain, norm_gain)
    if len(w_all) > 1:
        return pl.pallas_call(
            embed_first_kernel,
            in_specs=[smem()] + [vmem()] * 5 + [far] * 10,
            out_specs=[vmem()] * 2 + [far],
            out_shape=out_shape + [kept],
            scratch_shapes=scratch + [pltpu.SemaphoreType.DMA((11,))],
            name="embed_first",
            **common,
        )(place, *shared, *w_all)
    return (
        *pl.pallas_call(
            embed_next_kernel,
            in_specs=[vmem()] * 5 + [far],
            out_specs=[vmem()] * 2,
            out_shape=out_shape,
            scratch_shapes=scratch + [pltpu.SemaphoreType.DMA((width // PART,))],
            name="embed_next",
            **common,
        )(*shared, *w_all),
        w_all[0],
    )


def picks(level_group, lev, groups):
    row_groups = jnp.repeat(level_group, IN_LEV).reshape(lev // SOURCES, SOURCES, -1)
    steps = row_groups.shape[0]
    order = jnp.concatenate(
        [row_groups[:, :, :128].reshape(steps, -1), row_groups[:, :, 128:].reshape(steps, -1)], axis=1
    ).reshape(-1)
    return (order[None, :] == jnp.arange(groups, dtype=jnp.int32)[:, None]).astype(jnp.bfloat16)


def keys_values(x, w):
    n = x.shape[0] * x.shape[1]
    out = jnp.dot(x.reshape(n, x.shape[2]), w, preferred_element_type=jnp.float32).astype(jnp.bfloat16)
    return out.reshape(x.shape[0], x.shape[1], w.shape[1])


def queries_of(x, w):
    rows, cols, width = x.shape
    q = jnp.dot(x.reshape(rows * cols, width), w, preferred_element_type=jnp.float32).astype(jnp.bfloat16)
    return (q * jnp.bfloat16(DH ** (-0.5))).reshape(rows, cols, width)


def project_kernel(own0_ref, own1_ref, low_ref, high_ref, w_ref, q_ref, kv_ref):
    rows, cols, width = low_ref.shape
    inner = slice(STRIP, STRIP + cols)
    for c, ref in enumerate((own0_ref, own1_ref)):
        q = queries_of(ref[...], w_ref[:, :width])
        for b in range(cols // QCOLS):
            q_ref[b, c * rows * QCOLS:(c + 1) * rows * QCOLS, :] = q[:, b * QCOLS:(b + 1) * QCOLS, :].reshape(rows * QCOLS, width)
    for ref, at in ((own0_ref, 2), (own1_ref, 3), (low_ref, 0), (high_ref, 4)):
        kv_ref[at * rows:(at + 1) * rows, inner, :] = keys_values(ref[...], w_ref[:, width:])


def project(own0, own1, low, high, w_qkv):
    rows, cols, width = low.shape
    return pl.pallas_call(
        project_kernel,
        in_specs=[vmem()] * 5,
        out_specs=[vmem()] * 2,
        out_shape=[
            pltpu.VMEM((cols // QCOLS, 2 * rows * QCOLS, width), jnp.bfloat16),
            pltpu.VMEM((6 * rows, cols + 2 * STRIP, 2 * width), jnp.bfloat16),
        ],
        compiler_params=params(LIMIT),
        cost_estimate=cost(2 * low.size * 10 * width, w_qkv.size * 2 + low.size * 24),
        name="project",
    )(own0, own1, low, high, w_qkv)


def window_bias(start_ref, first_ref, rows):
    keys = 3 * rows * KCOLS
    key = lax.broadcasted_iota(jnp.int32, (QCOLS, keys), 1)
    key_row = key // KCOLS
    shift = key % KCOLS - lax.broadcasted_iota(jnp.int32, (QCOLS, keys), 0)
    near = STRIP - WIN // 2
    col_ok = (shift >= near) & (shift < near + WIN)
    first_row = first_ref[0]
    bias = []
    for r in range(rows):
        start = start_ref[first_row + r] - first_row + LAT_REACH
        ok = col_ok & (key_row >= start) & (key_row < start + WIN)
        bias.append(jnp.where(ok, 0.0, MASKED))
    return jnp.concatenate(bias + bias, axis=0)


def attend_block(b, bias, q_ref, kv_ref, att_ref):
    _, queries, width = q_ref.shape
    keys = bias.shape[1]
    lane = lax.broadcasted_iota(jnp.int32, (queries, 128), 1)
    is_first = lane < DH
    ones = jnp.ones((keys, 128), jnp.bfloat16)
    band = slice(b * QCOLS, b * QCOLS + KCOLS)
    for p in range(width // 128):
        here = slice(p * 128, (p + 1) * 128)
        here_v = slice(width + p * 128, width + (p + 1) * 128)
        q = q_ref[b, :, here]
        zero = jnp.zeros_like(q)
        qq = jnp.concatenate([jnp.where(is_first, q, zero), jnp.where(is_first, zero, q)], axis=0)
        k = kv_ref[:, band, here].reshape(keys, 128)
        v = kv_ref[:, band, here_v].reshape(keys, 128)
        s = lax.dot_general(qq, k, (((1,), (1,)), ((), ())), preferred_element_type=jnp.float32) + bias
        e = jnp.exp(s - jnp.max(s, axis=-1, keepdims=True)).astype(jnp.bfloat16)
        o = jnp.dot(e, jnp.concatenate([v, ones], axis=1), preferred_element_type=jnp.float32)
        o = o[:, :128] / o[:, 128:]
        att_ref[b, :, here] = jnp.where(is_first, o[:queries], o[queries:]).astype(jnp.bfloat16)


def finish_block(b, rows, att_ref, wout_ref, emb_refs, write):
    mixed = jnp.dot(att_ref[b], wout_ref[...], preferred_element_type=jnp.float32)
    mixed = mixed.reshape(rows, QCOLS, mixed.shape[1])
    half = rows // 2
    for c, ref in enumerate(emb_refs):
        wide = ref[:, b * QCOLS:(b + 1) * QCOLS, :].astype(jnp.float32)
        write(slice(c * half, (c + 1) * half), (wide + mixed[c * half:(c + 1) * half]).astype(jnp.bfloat16))


def middle_kernel(start_ref, first_ref, q_ref, _, low_ref, high_ref, left_ref, right_ref, w_ref, wout_ref, emb0_ref, emb1_ref,
                  kv_ref, out_ref, att_ref):
    half, cols, width = low_ref.shape
    rows = 2 * half
    wkv = w_ref[:, width:]
    inner = slice(STRIP, STRIP + cols)
    kv_ref[half:rows, inner, :] = keys_values(low_ref[...], wkv)
    kv_ref[2 * rows + half:, inner, :] = keys_values(high_ref[...], wkv)
    bias = window_bias(start_ref, first_ref, rows)
    attend_block(1, bias, q_ref, kv_ref, att_ref)

    def write(at, value):
        out_ref[at] = value

    finish_block(1, rows, att_ref, wout_ref, (emb0_ref, emb1_ref), write)
    for side, at in ((left_ref, slice(0, STRIP)), (right_ref, slice(STRIP + cols, None))):
        strip = keys_values(side[...], wkv)
        kv_ref[:half, at, :] = strip[:half]
        kv_ref[rows:2 * rows, at, :] = strip[half:3 * half]
        kv_ref[2 * rows:2 * rows + half, at, :] = strip[3 * half:]


def middle(lat_start, first_row, q, kv, low, high, left, right, w_qkv, w_out, emb0, emb1):
    half, cols, width = low.shape
    return pl.pallas_call(
        middle_kernel,
        in_specs=[smem(), smem()] + [vmem()] * 10,
        out_specs=[vmem()] * 2,
        out_shape=[pltpu.VMEM(kv.shape, kv.dtype), pltpu.VMEM((2 * half, QCOLS, width), jnp.bfloat16)],
        input_output_aliases={3: 0},
        scratch_shapes=[pltpu.VMEM(q.shape, jnp.bfloat16)],
        compiler_params=params(LIMIT),
        cost_estimate=cost(8e9, 10e6, 1e6),
        name="middle",
    )(lat_start, first_row, q, kv, low, high, left, right, w_qkv, w_out, emb0, emb1)


def sides_kernel(start_ref, first_ref, q_ref, _, left_ref, right_ref, w_ref, wout_ref, emb0_ref, emb1_ref, middle_ref,
                 out_ref, kv_ref, att_ref):
    rows, cols, width = out_ref.shape
    half = rows // 2
    blocks = q_ref.shape[0]
    wkv = w_ref[:, width:]
    for side, at in ((left_ref, slice(0, STRIP)), (right_ref, slice(STRIP + cols, None))):
        strip = keys_values(side[...], wkv)
        kv_ref[half:rows, at, :] = strip[:half]
        kv_ref[2 * rows + half:, at, :] = strip[half:]
    bias = window_bias(start_ref, first_ref, rows)
    out_ref[:, QCOLS:2 * QCOLS, :] = middle_ref[...]
    for b in (0, blocks - 1):
        attend_block(b, bias, q_ref, kv_ref, att_ref)

        def write(at, value):
            out_ref[at, b * QCOLS:(b + 1) * QCOLS, :] = value

        finish_block(b, rows, att_ref, wout_ref, (emb0_ref, emb1_ref), write)


def sides(lat_start, first_row, q, kv, left, right, w_qkv, w_out, emb0, emb1, centre):
    half, cols, width = emb0.shape
    return pl.pallas_call(
        sides_kernel,
        in_specs=[smem(), smem()] + [vmem()] * 9,
        out_specs=[vmem()] * 2,
        out_shape=[jax.ShapeDtypeStruct((2 * half, cols, width), jnp.bfloat16), pltpu.VMEM(kv.shape, kv.dtype)],
        input_output_aliases={3: 1},
        scratch_shapes=[pltpu.VMEM(q.shape, jnp.bfloat16)],
        compiler_params=params(LIMIT),
        cost_estimate=cost(9e9, 10e6, 2e6),
        name="sides",
    )(lat_start, first_row, q, kv, left, right, w_qkv, w_out, emb0, emb1, centre)[0]


def ring(count, stride, step):
    return [
        (base + i * stride, base + (i + step) % count * stride)
        for base in range(stride)
        for i in range(count)
    ]


def quarter_of_weights(w_embed, plane, lev):
    size, half = w_embed.shape[0] // PLANES, w_embed.shape[1] // 2
    mine = lax.dynamic_slice_in_dim(w_embed, plane * size, size, 0)
    both = jnp.stack([mine[:, :half], mine[:, half:]], axis=0)
    sent = jnp.broadcast_to(both[None], (lev // 2, 2, size, half)).reshape(lev, size, half)
    return lax.all_to_all(sent, "lev", split_axis=0, concat_axis=0, tiled=True)


def split_kernel(up_ref, down_ref, first_ref, second_ref):
    first_ref[...] = up_ref[...]
    second_ref[...] = down_ref[...]


def split(from_up, from_down):
    lev, size, half = from_up.shape
    block = (lev // 2, size, half)
    return pl.pallas_call(
        split_kernel,
        grid=(1,),
        in_specs=[pl.BlockSpec(block, lambda i: (0, 0, 0)), pl.BlockSpec(block, lambda i: (1, 0, 0))],
        out_specs=[pl.BlockSpec(block, lambda i: (0, 0, 0))] * 2,
        out_shape=[jax.ShapeDtypeStruct(block, from_up.dtype)] * 2,
        compiler_params=params(LIMIT),
        cost_estimate=cost(SPLIT_FLOPS, 4 * from_up.size),
        name="split",
    )(from_up, from_down)


def weight_pieces(own, lat):
    stride = lat // PLANES
    up, down = ring(PLANES, stride, 1), ring(PLANES, stride, -1)
    near = [lax.ppermute(own, "lat", up), lax.ppermute(own, "lat", down)]
    first, second = split(*near)
    far = [lax.ppermute(first, "lat", up), lax.ppermute(second, "lat", down)]
    pieces = [own] + near + far
    swap = [(i, i ^ 1) for i in range(own.shape[0])]
    return pieces + [lax.ppermute(piece, "lev", swap) for piece in pieces]


def per_device(
    fields, level_group, lat_start, w_embed, group_bias, group_gain, norm_gain, w_qkv, w_out
):
    rows = fields.shape[0]
    lev = lax.axis_size("lev")
    lat = lax.axis_size("lat")
    plane = lax.axis_index("lat") // (lat // PLANES)
    place = jnp.stack([plane, lax.axis_index("lev") % 2]).astype(jnp.int32)
    own = quarter_of_weights(w_embed, plane, lev)
    turned = jnp.transpose(fields, (0, 2, 1))
    pick = picks(level_group, lev, group_bias.shape[0])
    first_row = (lax.axis_index("lat") * rows).astype(jnp.int32).reshape(1)
    up = [(i, i + 1) for i in range(lat - 1)]
    down = [(b, a) for a, b in up]
    right_way = [(i, (i + 1) % lev) for i in range(lev)]
    left_way = [(b, a) for a, b in right_way]

    packed = [pack(turned, lev, c) for c in range(rows // CHUNK)]
    norm_gain = norm_gain[None, :]
    *packed, own, pick, place, norm_gain = lax.optimization_barrier((*packed, own, pick, place, norm_gain))
    w_all = weight_pieces(own, lat)
    emb, normed, low, high = [], [], [], []
    for c in range(rows // CHUNK):
        if c > 0:
            packed[c] = held
        moved = lax.all_to_all(packed[c], "lev", split_axis=0, concat_axis=0, tiled=True)
        if c == 0:
            held, *w_all = lax.optimization_barrier((packed[1], *w_all))
        e, n, kept = embed(moved, place, w_all, pick, group_bias, group_gain, norm_gain)
        w_all = [kept]
        emb.append(e)
        normed.append(n)
        if c % 2 == 0:
            low.append(lax.ppermute(n, "lat", up))
            high.append(lax.ppermute(n, "lat", down))
        else:
            high.append(lax.ppermute(n, "lat", down))
            low.append(lax.ppermute(n, "lat", up))

    def strips(tall):
        left = lax.ppermute(jnp.concatenate([t[:, -STRIP:] for t in tall], axis=0), "lev", right_way)
        right = lax.ppermute(jnp.concatenate([t[:, :STRIP] for t in tall], axis=0), "lev", left_way)
        return left, right

    low[0], high[0], normed[1] = lax.optimization_barrier((low[0], high[0], normed[1]))
    left, right = strips([low[0], normed[0], normed[1], high[0]])
    q, kv = project(normed[0], normed[1], low[0], high[0], w_qkv)
    high[1], low[1], q = lax.optimization_barrier((high[1], low[1], q))
    last_left, last_right = strips([low[1], high[1]])
    kv, centre = middle(
        lat_start, first_row, q, kv, low[1], high[1], left, right, w_qkv, w_out, emb[0], emb[1]
    )
    return sides(lat_start, first_row, q, kv, last_left, last_right, w_qkv, w_out, emb[0], emb[1], centre)


def solution(mesh):
    return jax.shard_map(
        per_device,
        mesh=mesh,
        in_specs=(P("lat", None, "lev"), P(), P(), P("lev", None), P(), P(), P(), P(), P()),
        out_specs=P("lat", "lev", None),
        check_vma=False,
    )
```

```python
import functools

import jax
import jax.numpy as jnp
from jax import lax
from jax.experimental import pallas as pl
from jax.experimental.pallas import tpu as pltpu
from jax.sharding import PartitionSpec as P

DH = 64
IN_LEV = 24
WIN = 13
LAT_REACH = 8
STRIP = 8
QCOLS = 16
KCOLS = QCOLS + 2 * STRIP
PLANES = 4
CHUNK = 4
SOURCES = 4
MASKED = -1e30
PART = 256
SPLIT_FLOPS = 18e9
FIRST_FLOPS = 16e9
FIRST_LIMIT = 56
NEXT_LIMIT = 50
LIMIT = 36


def params(mib):
    return pltpu.CompilerParams(vmem_limit_bytes=mib << 20)


def cost(flops, nbytes, trans=0):
    return pl.CostEstimate(flops=int(flops), bytes_accessed=int(nbytes), transcendentals=int(trans))


def smem():
    return pl.BlockSpec(memory_space=pltpu.SMEM)


def vmem():
    return pl.BlockSpec(memory_space=pltpu.VMEM)


def pack_kernel(x_ref, o_ref):
    rows, width, lon_all = x_ref.shape
    lev = o_ref.shape[0]
    cols = lon_all // lev
    tokens = rows * cols

    def put(block, first):
        turned = block.T.reshape(lev, cols, 128)
        o_ref[:, first:first + cols, :] = turned

    for r in range(rows):
        put(x_ref[r, :128, :], r * cols)
    for r in range(rows // 2):
        both = jnp.concatenate([x_ref[r, 128:, :], x_ref[r + rows // 2, 128:, :]], axis=0)
        put(both, tokens + r * cols)


def pack(turned, lev, chunk):
    _, width, lon_all = turned.shape
    tokens = CHUNK * lon_all // lev
    return pl.pallas_call(
        pack_kernel,
        grid=(1,),
        in_specs=[pl.BlockSpec((CHUNK, width, lon_all), lambda i: (chunk, 0, 0))],
        out_specs=pl.BlockSpec((lev, tokens + tokens // 2, 128), lambda i: (0, 0, 0)),
        out_shape=jax.ShapeDtypeStruct((lev, tokens + tokens // 2, 128), turned.dtype),
        compiler_params=params(60),
        cost_estimate=cost(0, 2 * turned.size),
        name="pack",
    )(turned)


def weight_rows(w_ref, s, first, last):
    size = w_ref.shape[2]
    out = []
    for quarter in range(w_ref.shape[1]):
        low, high = max(first - quarter * size, 0), min(last - quarter * size, size)
        if low < high:
            out.append((s, quarter, low, high))
    return out


def embed_body(x_ref, w_ref, pick_ref, bias_ref, gain_ref, norm_ref, emb_ref, normed_ref, xs_ref, sum_ref, before):
    groups, width = bias_ref.shape
    lev, quarters, size, _ = w_ref.shape
    per = quarters * size
    part = PART
    tokens = xs_ref.shape[0] // groups
    span = SOURCES * per

    for c in range(lev // SOURCES):
        here = range(c * SOURCES, (c + 1) * SOURCES)
        main = [x_ref[s, :tokens, :] for s in here]
        low = jnp.concatenate([x_ref[s, tokens:, :64] for s in here], axis=1)
        high = jnp.concatenate([x_ref[s, tokens:, 64:] for s in here], axis=1)
        x = jnp.concatenate(main + [jnp.concatenate([low, high], axis=0)], axis=1)
        for g in range(groups):
            xs_ref[g * tokens:(g + 1) * tokens, c * span:(c + 1) * span] = x * pick_ref[g:g + 1, c * span:(c + 1) * span]

    for j in range(width // part):
        before(j)
        cols = slice(j * part, (j + 1) * part)
        acc = None
        for c in range(lev // SOURCES):
            here = range(c * SOURCES, (c + 1) * SOURCES)
            rows = [r for s in here for r in weight_rows(w_ref, s, 0, 128)]
            rows += [r for s in here for r in weight_rows(w_ref, s, 128, per)]
            w = jnp.concatenate([w_ref[s, quarter, low:high, cols] for s, quarter, low, high in rows], axis=0)
            term = jnp.dot(xs_ref[:, c * span:(c + 1) * span], w, preferred_element_type=jnp.float32)
            acc = term if acc is None else acc + term
        total = jnp.zeros((tokens, part), jnp.float32)
        for g in range(groups):
            v = acc[g * tokens:(g + 1) * tokens] + bias_ref[g:g + 1, cols]
            total += v / (1.0 + jnp.exp(-v)) * gain_ref[g:g + 1, cols]
        sum_ref[:, cols] = total

    emb = sum_ref[...].astype(jnp.bfloat16)
    wide = emb.astype(jnp.float32)
    inv = lax.rsqrt(jnp.mean(wide * wide, axis=-1, keepdims=True) + 1e-05)
    emb_ref[...] = emb.reshape(emb_ref.shape)
    normed_ref[...] = (wide * inv * norm_ref[...]).astype(jnp.bfloat16).reshape(normed_ref.shape)


def embed_first_kernel(place_ref, x_ref, pick_ref, bias_ref, gain_ref, norm_ref, *refs):
    pieces, (emb_ref, normed_ref, kept_ref, xs_ref, sum_ref, w_ref, sem) = refs[:10], refs[10:]
    lev, quarters, _, width = w_ref.shape
    half = width // 2
    plane, core = place_ref[0], place_ref[1]
    loads = []
    for sibling in (0, 1):
        column = pl.multiple_of(lax.rem(core + sibling, 2) * half, 128)
        spots = ((0, 0, lev), (quarters - 1, 0, lev), (1, 0, lev), (2, 0, lev // 2), (2, lev // 2, lev))
        for n, (ahead, first, last) in enumerate(spots):
            quarter = lax.rem(plane + ahead, quarters)
            loads.append(
                pltpu.make_async_copy(
                    pieces[sibling * 5 + n],
                    w_ref.at[first:last, quarter, :, pl.ds(column, half)],
                    sem.at[sibling * 5 + n],
                )
            )
    for load in loads:
        load.start()
    keep = pltpu.make_async_copy(w_ref, kept_ref, sem.at[10])

    def before(j):
        if j == 0:
            for load in loads:
                load.wait()
            keep.start()

    embed_body(x_ref, w_ref, pick_ref, bias_ref, gain_ref, norm_ref, emb_ref, normed_ref, xs_ref, sum_ref, before)
    keep.wait()


def embed_next_kernel(x_ref, pick_ref, bias_ref, gain_ref, norm_ref, kept_ref, emb_ref, normed_ref, xs_ref, sum_ref, w_ref, sem):
    loads = []
    for j in range(w_ref.shape[3] // PART):
        cols = slice(j * PART, (j + 1) * PART)
        loads.append(pltpu.make_async_copy(kept_ref.at[:, :, :, cols], w_ref.at[:, :, :, cols], sem.at[j]))
        loads[j].start()
    embed_body(
        x_ref, w_ref, pick_ref, bias_ref, gain_ref, norm_ref, emb_ref, normed_ref, xs_ref, sum_ref, lambda j: loads[j].wait()
    )


def embed(moved, place, w_all, pick, bias, gain, norm_gain):
    lev = moved.shape[0]
    tokens = moved.shape[1] * 2 // 3
    groups, width = bias.shape
    depth = pick.shape[1]
    cols = tokens // CHUNK
    out_shape = [jax.ShapeDtypeStruct((CHUNK, cols, width), jnp.bfloat16)] * 2
    size = w_all[0].shape[-2]
    kept = jax.ShapeDtypeStruct((lev, depth // lev // size, size, width), jnp.bfloat16)
    scratch = [
        pltpu.VMEM((groups * tokens, depth), jnp.bfloat16),
        pltpu.VMEM((tokens, width), jnp.float32),
        pltpu.VMEM(kept.shape, kept.dtype),
    ]
    far = pl.BlockSpec(memory_space=pl.ANY)
    common = dict(
        compiler_params=params(FIRST_LIMIT if len(w_all) > 1 else NEXT_LIMIT),
        cost_estimate=cost(FIRST_FLOPS if len(w_all) > 1 else 2 * tokens * depth * width * groups, depth * width * 2 + tokens * depth * 2),
    )
    shared = (moved, pick, bias, gain, norm_gain)
    if len(w_all) > 1:
        return pl.pallas_call(
            embed_first_kernel,
            in_specs=[smem()] + [vmem()] * 5 + [far] * 10,
            out_specs=[vmem()] * 2 + [far],
            out_shape=out_shape + [kept],
            scratch_shapes=scratch + [pltpu.SemaphoreType.DMA((11,))],
            name="embed_first",
            **common,
        )(place, *shared, *w_all)
    return (
        *pl.pallas_call(
            embed_next_kernel,
            in_specs=[vmem()] * 5 + [far],
            out_specs=[vmem()] * 2,
            out_shape=out_shape,
            scratch_shapes=scratch + [pltpu.SemaphoreType.DMA((width // PART,))],
            name="embed_next",
            **common,
        )(*shared, *w_all),
        w_all[0],
    )


def picks(level_group, lev, groups):
    row_groups = jnp.repeat(level_group, IN_LEV).reshape(lev // SOURCES, SOURCES, -1)
    steps = row_groups.shape[0]
    order = jnp.concatenate(
        [row_groups[:, :, :128].reshape(steps, -1), row_groups[:, :, 128:].reshape(steps, -1)], axis=1
    ).reshape(-1)
    return (order[None, :] == jnp.arange(groups, dtype=jnp.int32)[:, None]).astype(jnp.bfloat16)


def keys_values(x, w):
    n = x.shape[0] * x.shape[1]
    out = jnp.dot(x.reshape(n, x.shape[2]), w, preferred_element_type=jnp.float32).astype(jnp.bfloat16)
    return out.reshape(x.shape[0], x.shape[1], w.shape[1])


def queries_of(x, w):
    rows, cols, width = x.shape
    q = jnp.dot(x.reshape(rows * cols, width), w, preferred_element_type=jnp.float32).astype(jnp.bfloat16)
    return (q * jnp.bfloat16(DH ** (-0.5))).reshape(rows, cols, width)


def project_kernel(own0_ref, own1_ref, low_ref, high_ref, w_ref, q_ref, kv_ref):
    rows, cols, width = low_ref.shape
    inner = slice(STRIP, STRIP + cols)
    for c, ref in enumerate((own0_ref, own1_ref)):
        q = queries_of(ref[...], w_ref[:, :width])
        for b in range(cols // QCOLS):
            q_ref[b, c * rows * QCOLS:(c + 1) * rows * QCOLS, :] = q[:, b * QCOLS:(b + 1) * QCOLS, :].reshape(rows * QCOLS, width)
    for ref, at in ((own0_ref, 2), (own1_ref, 3), (low_ref, 0), (high_ref, 4)):
        kv_ref[at * rows:(at + 1) * rows, inner, :] = keys_values(ref[...], w_ref[:, width:])


def project(own0, own1, low, high, w_qkv):
    rows, cols, width = low.shape
    return pl.pallas_call(
        project_kernel,
        in_specs=[vmem()] * 5,
        out_specs=[vmem()] * 2,
        out_shape=[
            pltpu.VMEM((cols // QCOLS, 2 * rows * QCOLS, width), jnp.bfloat16),
            pltpu.VMEM((6 * rows, cols + 2 * STRIP, 2 * width), jnp.bfloat16),
        ],
        compiler_params=params(LIMIT),
        cost_estimate=cost(2 * low.size * 10 * width, w_qkv.size * 2 + low.size * 24),
        name="project",
    )(own0, own1, low, high, w_qkv)


def window_bias(start_ref, first_ref, rows):
    keys = 3 * rows * KCOLS
    key = lax.broadcasted_iota(jnp.int32, (QCOLS, keys), 1)
    key_row = key // KCOLS
    shift = key % KCOLS - lax.broadcasted_iota(jnp.int32, (QCOLS, keys), 0)
    near = STRIP - WIN // 2
    col_ok = (shift >= near) & (shift < near + WIN)
    first_row = first_ref[0]
    bias = []
    for r in range(rows):
        start = start_ref[first_row + r] - first_row + LAT_REACH
        ok = col_ok & (key_row >= start) & (key_row < start + WIN)
        bias.append(jnp.where(ok, 0.0, MASKED))
    return jnp.concatenate(bias + bias, axis=0)


def attend_block(b, bias, q_ref, kv_ref, att_ref):
    _, queries, width = q_ref.shape
    keys = bias.shape[1]
    lane = lax.broadcasted_iota(jnp.int32, (queries, 128), 1)
    is_first = lane < DH
    ones = jnp.ones((keys, 128), jnp.bfloat16)
    band = slice(b * QCOLS, b * QCOLS + KCOLS)
    for p in range(width // 128):
        here = slice(p * 128, (p + 1) * 128)
        here_v = slice(width + p * 128, width + (p + 1) * 128)
        q = q_ref[b, :, here]
        zero = jnp.zeros_like(q)
        qq = jnp.concatenate([jnp.where(is_first, q, zero), jnp.where(is_first, zero, q)], axis=0)
        k = kv_ref[:, band, here].reshape(keys, 128)
        v = kv_ref[:, band, here_v].reshape(keys, 128)
        s = lax.dot_general(qq, k, (((1,), (1,)), ((), ())), preferred_element_type=jnp.float32) + bias
        e = jnp.exp(s - jnp.max(s, axis=-1, keepdims=True)).astype(jnp.bfloat16)
        o = jnp.dot(e, jnp.concatenate([v, ones], axis=1), preferred_element_type=jnp.float32)
        o = o[:, :128] / o[:, 128:]
        att_ref[b, :, here] = jnp.where(is_first, o[:queries], o[queries:]).astype(jnp.bfloat16)


def finish_block(b, rows, att_ref, wout_ref, emb_refs, write):
    mixed = jnp.dot(att_ref[b], wout_ref[...], preferred_element_type=jnp.float32)
    mixed = mixed.reshape(rows, QCOLS, mixed.shape[1])
    half = rows // 2
    for c, ref in enumerate(emb_refs):
        wide = ref[:, b * QCOLS:(b + 1) * QCOLS, :].astype(jnp.float32)
        write(slice(c * half, (c + 1) * half), (wide + mixed[c * half:(c + 1) * half]).astype(jnp.bfloat16))


def middle_kernel(start_ref, first_ref, q_ref, _, low_ref, high_ref, left_ref, right_ref, w_ref, wout_ref, emb0_ref, emb1_ref,
                  kv_ref, out_ref, att_ref):
    half, cols, width = low_ref.shape
    rows = 2 * half
    wkv = w_ref[:, width:]
    inner = slice(STRIP, STRIP + cols)
    kv_ref[half:rows, inner, :] = keys_values(low_ref[...], wkv)
    kv_ref[2 * rows + half:, inner, :] = keys_values(high_ref[...], wkv)
    bias = window_bias(start_ref, first_ref, rows)
    attend_block(1, bias, q_ref, kv_ref, att_ref)

    def write(at, value):
        out_ref[at] = value

    finish_block(1, rows, att_ref, wout_ref, (emb0_ref, emb1_ref), write)
    for side, at in ((left_ref, slice(0, STRIP)), (right_ref, slice(STRIP + cols, None))):
        strip = keys_values(side[...], wkv)
        kv_ref[:half, at, :] = strip[:half]
        kv_ref[rows:2 * rows, at, :] = strip[half:3 * half]
        kv_ref[2 * rows:2 * rows + half, at, :] = strip[3 * half:]


def middle(lat_start, first_row, q, kv, low, high, left, right, w_qkv, w_out, emb0, emb1):
    half, cols, width = low.shape
    return pl.pallas_call(
        middle_kernel,
        in_specs=[smem(), smem()] + [vmem()] * 10,
        out_specs=[vmem()] * 2,
        out_shape=[pltpu.VMEM(kv.shape, kv.dtype), pltpu.VMEM((2 * half, QCOLS, width), jnp.bfloat16)],
        input_output_aliases={3: 0},
        scratch_shapes=[pltpu.VMEM(q.shape, jnp.bfloat16)],
        compiler_params=params(LIMIT),
        cost_estimate=cost(8e9, 10e6, 1e6),
        name="middle",
    )(lat_start, first_row, q, kv, low, high, left, right, w_qkv, w_out, emb0, emb1)


def sides_kernel(start_ref, first_ref, q_ref, _, left_ref, right_ref, w_ref, wout_ref, emb0_ref, emb1_ref, middle_ref,
                 out_ref, kv_ref, att_ref):
    rows, cols, width = out_ref.shape
    half = rows // 2
    blocks = q_ref.shape[0]
    wkv = w_ref[:, width:]
    for side, at in ((left_ref, slice(0, STRIP)), (right_ref, slice(STRIP + cols, None))):
        strip = keys_values(side[...], wkv)
        kv_ref[half:rows, at, :] = strip[:half]
        kv_ref[2 * rows + half:, at, :] = strip[half:]
    bias = window_bias(start_ref, first_ref, rows)
    out_ref[:, QCOLS:2 * QCOLS, :] = middle_ref[...]
    for b in (0, blocks - 1):
        attend_block(b, bias, q_ref, kv_ref, att_ref)

        def write(at, value):
            out_ref[at, b * QCOLS:(b + 1) * QCOLS, :] = value

        finish_block(b, rows, att_ref, wout_ref, (emb0_ref, emb1_ref), write)


def sides(lat_start, first_row, q, kv, left, right, w_qkv, w_out, emb0, emb1, centre):
    half, cols, width = emb0.shape
    return pl.pallas_call(
        sides_kernel,
        in_specs=[smem(), smem()] + [vmem()] * 9,
        out_specs=[vmem()] * 2,
        out_shape=[jax.ShapeDtypeStruct((2 * half, cols, width), jnp.bfloat16), pltpu.VMEM(kv.shape, kv.dtype)],
        input_output_aliases={3: 1},
        scratch_shapes=[pltpu.VMEM(q.shape, jnp.bfloat16)],
        compiler_params=params(LIMIT),
        cost_estimate=cost(9e9, 10e6, 2e6),
        name="sides",
    )(lat_start, first_row, q, kv, left, right, w_qkv, w_out, emb0, emb1, centre)[0]


def ring(count, stride, step):
    return [
        (base + i * stride, base + (i + step) % count * stride)
        for base in range(stride)
        for i in range(count)
    ]


def quarter_of_weights(w_embed, plane, lev):
    size, half = w_embed.shape[0] // PLANES, w_embed.shape[1] // 2
    mine = lax.dynamic_slice_in_dim(w_embed, plane * size, size, 0)
    both = jnp.stack([mine[:, :half], mine[:, half:]], axis=0)
    sent = jnp.broadcast_to(both[None], (lev // 2, 2, size, half)).reshape(lev, size, half)
    return lax.all_to_all(sent, "lev", split_axis=0, concat_axis=0, tiled=True)


def split_kernel(up_ref, down_ref, first_ref, second_ref):
    first_ref[...] = up_ref[...]
    second_ref[...] = down_ref[...]


def split(from_up, from_down):
    lev, size, half = from_up.shape
    block = (lev // 2, size, half)
    return pl.pallas_call(
        split_kernel,
        grid=(1,),
        in_specs=[pl.BlockSpec(block, lambda i: (0, 0, 0)), pl.BlockSpec(block, lambda i: (1, 0, 0))],
        out_specs=[pl.BlockSpec(block, lambda i: (0, 0, 0))] * 2,
        out_shape=[jax.ShapeDtypeStruct(block, from_up.dtype)] * 2,
        compiler_params=params(LIMIT),
        cost_estimate=cost(SPLIT_FLOPS, 4 * from_up.size),
        name="split",
    )(from_up, from_down)


def weight_pieces(own, lat):
    stride = lat // PLANES
    up, down = ring(PLANES, stride, 1), ring(PLANES, stride, -1)
    near = [lax.ppermute(own, "lat", up), lax.ppermute(own, "lat", down)]
    first, second = split(*near)
    far = [lax.ppermute(first, "lat", up), lax.ppermute(second, "lat", down)]
    pieces = [own] + near + far
    swap = [(i, i ^ 1) for i in range(own.shape[0])]
    return pieces + [lax.ppermute(piece, "lev", swap) for piece in pieces]


def per_device(
    fields, level_group, lat_start, w_embed, group_bias, group_gain, norm_gain, w_qkv, w_out
):
    rows = fields.shape[0]
    lev = lax.axis_size("lev")
    lat = lax.axis_size("lat")
    plane = lax.axis_index("lat") // (lat // PLANES)
    place = jnp.stack([plane, lax.axis_index("lev") % 2]).astype(jnp.int32)
    own = quarter_of_weights(w_embed, plane, lev)
    turned = jnp.transpose(fields, (0, 2, 1))
    pick = picks(level_group, lev, group_bias.shape[0])
    first_row = (lax.axis_index("lat") * rows).astype(jnp.int32).reshape(1)
    up = [(i, i + 1) for i in range(lat - 1)]
    down = [(b, a) for a, b in up]
    right_way = [(i, (i + 1) % lev) for i in range(lev)]
    left_way = [(b, a) for a, b in right_way]

    packed = [pack(turned, lev, c) for c in range(rows // CHUNK)]
    norm_gain = norm_gain[None, :]
    *packed, own, pick, place, norm_gain = lax.optimization_barrier((*packed, own, pick, place, norm_gain))
    w_all = weight_pieces(own, lat)
    emb, normed, low, high = [], [], [], []
    for c in range(rows // CHUNK):
        if c > 0:
            packed[c] = held
        moved = lax.all_to_all(packed[c], "lev", split_axis=0, concat_axis=0, tiled=True)
        if c == 0:
            held, *w_all[5:8] = lax.optimization_barrier((packed[1], *w_all[5:8]))
        e, n, kept = embed(moved, place, w_all, pick, group_bias, group_gain, norm_gain)
        w_all = [kept]
        emb.append(e)
        normed.append(n)
        if c % 2 == 0:
            low.append(lax.ppermute(n, "lat", up))
            high.append(lax.ppermute(n, "lat", down))
        else:
            high.append(lax.ppermute(n, "lat", down))
            low.append(lax.ppermute(n, "lat", up))

    def strips(tall):
        left = lax.ppermute(jnp.concatenate([t[:, -STRIP:] for t in tall], axis=0), "lev", right_way)
        right = lax.ppermute(jnp.concatenate([t[:, :STRIP] for t in tall], axis=0), "lev", left_way)
        return left, right

    low[0], high[0], normed[1] = lax.optimization_barrier((low[0], high[0], normed[1]))
    left, right = strips([low[0], normed[0], normed[1], high[0]])
    q, kv = project(normed[0], normed[1], low[0], high[0], w_qkv)
    high[1], low[1], q = lax.optimization_barrier((high[1], low[1], q))
    last_left, last_right = strips([low[1], high[1]])
    kv, centre = middle(
        lat_start, first_row, q, kv, low[1], high[1], left, right, w_qkv, w_out, emb[0], emb[1]
    )
    return sides(lat_start, first_row, q, kv, last_left, last_right, w_qkv, w_out, emb[0], emb[1], centre)


def solution(mesh):
    return jax.shard_map(
        per_device,
        mesh=mesh,
        in_specs=(P("lat", None, "lev"), P(), P(), P("lev", None), P(), P(), P(), P(), P()),
        out_specs=P("lat", "lev", None),
        check_vma=False,
    )
```

```python
import functools

import jax
import jax.numpy as jnp
from jax import lax
from jax.experimental import pallas as pl
from jax.experimental.pallas import tpu as pltpu
from jax.sharding import PartitionSpec as P

DH = 64
IN_LEV = 24
WIN = 13
LAT_REACH = 8
STRIP = 8
QCOLS = 16
KCOLS = QCOLS + 2 * STRIP
PLANES = 4
CHUNK = 4
SOURCES = 4
MASKED = -1e30
PART = 256
SPLIT_FLOPS = 18e9
FIRST_FLOPS = 16e9
FIRST_LIMIT = 56
NEXT_LIMIT = 50
LIMIT = 36


def params(mib):
    return pltpu.CompilerParams(vmem_limit_bytes=mib << 20)


def cost(flops, nbytes, trans=0):
    return pl.CostEstimate(flops=int(flops), bytes_accessed=int(nbytes), transcendentals=int(trans))


def smem():
    return pl.BlockSpec(memory_space=pltpu.SMEM)


def vmem():
    return pl.BlockSpec(memory_space=pltpu.VMEM)


def pack_kernel(x_ref, o_ref):
    rows, width, lon_all = x_ref.shape
    lev = o_ref.shape[0]
    cols = lon_all // lev
    tokens = rows * cols

    def put(block, first):
        turned = block.T.reshape(lev, cols, 128)
        o_ref[:, first:first + cols, :] = turned

    for r in range(rows):
        put(x_ref[r, :128, :], r * cols)
    for r in range(rows // 2):
        both = jnp.concatenate([x_ref[r, 128:, :], x_ref[r + rows // 2, 128:, :]], axis=0)
        put(both, tokens + r * cols)


def pack(turned, lev, chunk):
    _, width, lon_all = turned.shape
    tokens = CHUNK * lon_all // lev
    return pl.pallas_call(
        pack_kernel,
        grid=(1,),
        in_specs=[pl.BlockSpec((CHUNK, width, lon_all), lambda i: (chunk, 0, 0))],
        out_specs=pl.BlockSpec((lev, tokens + tokens // 2, 128), lambda i: (0, 0, 0)),
        out_shape=jax.ShapeDtypeStruct((lev, tokens + tokens // 2, 128), turned.dtype),
        compiler_params=params(60),
        cost_estimate=cost(0, 2 * turned.size),
        name="pack",
    )(turned)


def weight_rows(w_ref, s, first, last):
    size = w_ref.shape[2]
    out = []
    for quarter in range(w_ref.shape[1]):
        low, high = max(first - quarter * size, 0), min(last - quarter * size, size)
        if low < high:
            out.append((s, quarter, low, high))
    return out


def embed_body(x_ref, w_ref, pick_ref, bias_ref, gain_ref, norm_ref, emb_ref, normed_ref, xs_ref, sum_ref, before):
    groups, width = bias_ref.shape
    lev, quarters, size, _ = w_ref.shape
    per = quarters * size
    part = PART
    tokens = xs_ref.shape[0] // groups
    span = SOURCES * per

    for c in range(lev // SOURCES):
        here = range(c * SOURCES, (c + 1) * SOURCES)
        main = [x_ref[s, :tokens, :] for s in here]
        low = jnp.concatenate([x_ref[s, tokens:, :64] for s in here], axis=1)
        high = jnp.concatenate([x_ref[s, tokens:, 64:] for s in here], axis=1)
        x = jnp.concatenate(main + [jnp.concatenate([low, high], axis=0)], axis=1)
        for g in range(groups):
            xs_ref[g * tokens:(g + 1) * tokens, c * span:(c + 1) * span] = x * pick_ref[g:g + 1, c * span:(c + 1) * span]

    for j in range(width // part):
        before(j)
        cols = slice(j * part, (j + 1) * part)
        acc = None
        for c in range(lev // SOURCES):
            here = range(c * SOURCES, (c + 1) * SOURCES)
            rows = [r for s in here for r in weight_rows(w_ref, s, 0, 128)]
            rows += [r for s in here for r in weight_rows(w_ref, s, 128, per)]
            w = jnp.concatenate([w_ref[s, quarter, low:high, cols] for s, quarter, low, high in rows], axis=0)
            term = jnp.dot(xs_ref[:, c * span:(c + 1) * span], w, preferred_element_type=jnp.float32)
            acc = term if acc is None else acc + term
        total = jnp.zeros((tokens, part), jnp.float32)
        for g in range(groups):
            v = acc[g * tokens:(g + 1) * tokens] + bias_ref[g:g + 1, cols]
            total += v / (1.0 + jnp.exp(-v)) * gain_ref[g:g + 1, cols]
        sum_ref[:, cols] = total

    emb = sum_ref[...].astype(jnp.bfloat16)
    wide = emb.astype(jnp.float32)
    inv = lax.rsqrt(jnp.mean(wide * wide, axis=-1, keepdims=True) + 1e-05)
    emb_ref[...] = emb.reshape(emb_ref.shape)
    normed_ref[...] = (wide * inv * norm_ref[...]).astype(jnp.bfloat16).reshape(normed_ref.shape)


def embed_first_kernel(place_ref, x_ref, pick_ref, bias_ref, gain_ref, norm_ref, *refs):
    pieces, (emb_ref, normed_ref, kept_ref, xs_ref, sum_ref, w_ref, sem) = refs[:10], refs[10:]
    lev, quarters, _, width = w_ref.shape
    half = width // 2
    plane, core = place_ref[0], place_ref[1]
    spots = ((0, 0, lev), (quarters - 1, 0, lev), (1, 0, lev), (2, 0, lev // 2), (2, lev // 2, lev))

    def loads(side, sibling):
        out = []
        for n, (ahead, first, last) in enumerate(spots):
            spot = w_ref.at[first:last, lax.rem(plane + ahead, quarters), :, side * half:(side + 1) * half]
            out.append(pltpu.make_async_copy(pieces[sibling * 5 + n], spot, sem.at[side * 5 + n]))
        return out

    for own_side in (0, 1):

        @pl.when(core == own_side)
        def _():
            for side in (0, 1):
                for load in loads(side, 0 if side == own_side else 1):
                    load.start()

    keep = pltpu.make_async_copy(w_ref, kept_ref, sem.at[10])

    def before(j):
        if j < 2:
            for load in loads(j, j):
                load.wait()
        if j == 1:
            keep.start()

    embed_body(x_ref, w_ref, pick_ref, bias_ref, gain_ref, norm_ref, emb_ref, normed_ref, xs_ref, sum_ref, before)
    keep.wait()


def embed_next_kernel(x_ref, pick_ref, bias_ref, gain_ref, norm_ref, kept_ref, emb_ref, normed_ref, xs_ref, sum_ref, w_ref, sem):
    loads = []
    for j in range(w_ref.shape[3] // PART):
        cols = slice(j * PART, (j + 1) * PART)
        loads.append(pltpu.make_async_copy(kept_ref.at[:, :, :, cols], w_ref.at[:, :, :, cols], sem.at[j]))
        loads[j].start()
    embed_body(
        x_ref, w_ref, pick_ref, bias_ref, gain_ref, norm_ref, emb_ref, normed_ref, xs_ref, sum_ref, lambda j: loads[j].wait()
    )


def embed(moved, place, w_all, pick, bias, gain, norm_gain):
    lev = moved.shape[0]
    tokens = moved.shape[1] * 2 // 3
    groups, width = bias.shape
    depth = pick.shape[1]
    cols = tokens // CHUNK
    out_shape = [jax.ShapeDtypeStruct((CHUNK, cols, width), jnp.bfloat16)] * 2
    size = w_all[0].shape[-2]
    kept = jax.ShapeDtypeStruct((lev, depth // lev // size, size, width), jnp.bfloat16)
    scratch = [
        pltpu.VMEM((groups * tokens, depth), jnp.bfloat16),
        pltpu.VMEM((tokens, width), jnp.float32),
        pltpu.VMEM(kept.shape, kept.dtype),
    ]
    far = pl.BlockSpec(memory_space=pl.ANY)
    common = dict(
        compiler_params=params(FIRST_LIMIT if len(w_all) > 1 else NEXT_LIMIT),
        cost_estimate=cost(FIRST_FLOPS if len(w_all) > 1 else 2 * tokens * depth * width * groups, depth * width * 2 + tokens * depth * 2),
    )
    shared = (moved, pick, bias, gain, norm_gain)
    if len(w_all) > 1:
        return pl.pallas_call(
            embed_first_kernel,
            in_specs=[smem()] + [vmem()] * 5 + [far] * 10,
            out_specs=[vmem()] * 2 + [far],
            out_shape=out_shape + [kept],
            scratch_shapes=scratch + [pltpu.SemaphoreType.DMA((11,))],
            name="embed_first",
            **common,
        )(place, *shared, *w_all)
    return (
        *pl.pallas_call(
            embed_next_kernel,
            in_specs=[vmem()] * 5 + [far],
            out_specs=[vmem()] * 2,
            out_shape=out_shape,
            scratch_shapes=scratch + [pltpu.SemaphoreType.DMA((width // PART,))],
            name="embed_next",
            **common,
        )(*shared, *w_all),
        w_all[0],
    )


def picks(level_group, lev, groups):
    row_groups = jnp.repeat(level_group, IN_LEV).reshape(lev // SOURCES, SOURCES, -1)
    steps = row_groups.shape[0]
    order = jnp.concatenate(
        [row_groups[:, :, :128].reshape(steps, -1), row_groups[:, :, 128:].reshape(steps, -1)], axis=1
    ).reshape(-1)
    return (order[None, :] == jnp.arange(groups, dtype=jnp.int32)[:, None]).astype(jnp.bfloat16)


def keys_values(x, w):
    n = x.shape[0] * x.shape[1]
    out = jnp.dot(x.reshape(n, x.shape[2]), w, preferred_element_type=jnp.float32).astype(jnp.bfloat16)
    return out.reshape(x.shape[0], x.shape[1], w.shape[1])


def queries_of(x, w):
    rows, cols, width = x.shape
    q = jnp.dot(x.reshape(rows * cols, width), w, preferred_element_type=jnp.float32).astype(jnp.bfloat16)
    return (q * jnp.bfloat16(DH ** (-0.5))).reshape(rows, cols, width)


def project_kernel(own0_ref, own1_ref, low_ref, high_ref, w_ref, q_ref, kv_ref):
    rows, cols, width = low_ref.shape
    inner = slice(STRIP, STRIP + cols)
    for c, ref in enumerate((own0_ref, own1_ref)):
        q = queries_of(ref[...], w_ref[:, :width])
        for b in range(cols // QCOLS):
            q_ref[b, c * rows * QCOLS:(c + 1) * rows * QCOLS, :] = q[:, b * QCOLS:(b + 1) * QCOLS, :].reshape(rows * QCOLS, width)
    for ref, at in ((own0_ref, 2), (own1_ref, 3), (low_ref, 0), (high_ref, 4)):
        kv_ref[at * rows:(at + 1) * rows, inner, :] = keys_values(ref[...], w_ref[:, width:])


def project(own0, own1, low, high, w_qkv):
    rows, cols, width = low.shape
    return pl.pallas_call(
        project_kernel,
        in_specs=[vmem()] * 5,
        out_specs=[vmem()] * 2,
        out_shape=[
            pltpu.VMEM((cols // QCOLS, 2 * rows * QCOLS, width), jnp.bfloat16),
            pltpu.VMEM((6 * rows, cols + 2 * STRIP, 2 * width), jnp.bfloat16),
        ],
        compiler_params=params(LIMIT),
        cost_estimate=cost(2 * low.size * 10 * width, w_qkv.size * 2 + low.size * 24),
        name="project",
    )(own0, own1, low, high, w_qkv)


def window_bias(start_ref, first_ref, rows):
    keys = 3 * rows * KCOLS
    key = lax.broadcasted_iota(jnp.int32, (QCOLS, keys), 1)
    key_row = key // KCOLS
    shift = key % KCOLS - lax.broadcasted_iota(jnp.int32, (QCOLS, keys), 0)
    near = STRIP - WIN // 2
    col_ok = (shift >= near) & (shift < near + WIN)
    first_row = first_ref[0]
    bias = []
    for r in range(rows):
        start = start_ref[first_row + r] - first_row + LAT_REACH
        ok = col_ok & (key_row >= start) & (key_row < start + WIN)
        bias.append(jnp.where(ok, 0.0, MASKED))
    return jnp.concatenate(bias + bias, axis=0)


def attend_block(b, bias, q_ref, kv_ref, att_ref):
    _, queries, width = q_ref.shape
    keys = bias.shape[1]
    lane = lax.broadcasted_iota(jnp.int32, (queries, 128), 1)
    is_first = lane < DH
    ones = jnp.ones((keys, 128), jnp.bfloat16)
    band = slice(b * QCOLS, b * QCOLS + KCOLS)
    for p in range(width // 128):
        here = slice(p * 128, (p + 1) * 128)
        here_v = slice(width + p * 128, width + (p + 1) * 128)
        q = q_ref[b, :, here]
        zero = jnp.zeros_like(q)
        qq = jnp.concatenate([jnp.where(is_first, q, zero), jnp.where(is_first, zero, q)], axis=0)
        k = kv_ref[:, band, here].reshape(keys, 128)
        v = kv_ref[:, band, here_v].reshape(keys, 128)
        s = lax.dot_general(qq, k, (((1,), (1,)), ((), ())), preferred_element_type=jnp.float32) + bias
        e = jnp.exp(s - jnp.max(s, axis=-1, keepdims=True)).astype(jnp.bfloat16)
        o = jnp.dot(e, jnp.concatenate([v, ones], axis=1), preferred_element_type=jnp.float32)
        o = o[:, :128] / o[:, 128:]
        att_ref[b, :, here] = jnp.where(is_first, o[:queries], o[queries:]).astype(jnp.bfloat16)


def finish_block(b, rows, att_ref, wout_ref, emb_refs, write):
    mixed = jnp.dot(att_ref[b], wout_ref[...], preferred_element_type=jnp.float32)
    mixed = mixed.reshape(rows, QCOLS, mixed.shape[1])
    half = rows // 2
    for c, ref in enumerate(emb_refs):
        wide = ref[:, b * QCOLS:(b + 1) * QCOLS, :].astype(jnp.float32)
        write(slice(c * half, (c + 1) * half), (wide + mixed[c * half:(c + 1) * half]).astype(jnp.bfloat16))


def middle_kernel(start_ref, first_ref, q_ref, _, low_ref, high_ref, left_ref, right_ref, w_ref, wout_ref, emb0_ref, emb1_ref,
                  kv_ref, out_ref, att_ref):
    half, cols, width = low_ref.shape
    rows = 2 * half
    wkv = w_ref[:, width:]
    inner = slice(STRIP, STRIP + cols)
    kv_ref[half:rows, inner, :] = keys_values(low_ref[...], wkv)
    kv_ref[2 * rows + half:, inner, :] = keys_values(high_ref[...], wkv)
    bias = window_bias(start_ref, first_ref, rows)
    attend_block(1, bias, q_ref, kv_ref, att_ref)

    def write(at, value):
        out_ref[at] = value

    finish_block(1, rows, att_ref, wout_ref, (emb0_ref, emb1_ref), write)
    for side, at in ((left_ref, slice(0, STRIP)), (right_ref, slice(STRIP + cols, None))):
        strip = keys_values(side[...], wkv)
        kv_ref[:half, at, :] = strip[:half]
        kv_ref[rows:2 * rows, at, :] = strip[half:3 * half]
        kv_ref[2 * rows:2 * rows + half, at, :] = strip[3 * half:]


def middle(lat_start, first_row, q, kv, low, high, left, right, w_qkv, w_out, emb0, emb1):
    half, cols, width = low.shape
    return pl.pallas_call(
        middle_kernel,
        in_specs=[smem(), smem()] + [vmem()] * 10,
        out_specs=[vmem()] * 2,
        out_shape=[pltpu.VMEM(kv.shape, kv.dtype), pltpu.VMEM((2 * half, QCOLS, width), jnp.bfloat16)],
        input_output_aliases={3: 0},
        scratch_shapes=[pltpu.VMEM(q.shape, jnp.bfloat16)],
        compiler_params=params(LIMIT),
        cost_estimate=cost(8e9, 10e6, 1e6),
        name="middle",
    )(lat_start, first_row, q, kv, low, high, left, right, w_qkv, w_out, emb0, emb1)


def sides_kernel(start_ref, first_ref, q_ref, _, left_ref, right_ref, w_ref, wout_ref, emb0_ref, emb1_ref, middle_ref,
                 out_ref, kv_ref, att_ref):
    rows, cols, width = out_ref.shape
    half = rows // 2
    blocks = q_ref.shape[0]
    wkv = w_ref[:, width:]
    for side, at in ((left_ref, slice(0, STRIP)), (right_ref, slice(STRIP + cols, None))):
        strip = keys_values(side[...], wkv)
        kv_ref[half:rows, at, :] = strip[:half]
        kv_ref[2 * rows + half:, at, :] = strip[half:]
    bias = window_bias(start_ref, first_ref, rows)
    out_ref[:, QCOLS:2 * QCOLS, :] = middle_ref[...]
    for b in (0, blocks - 1):
        attend_block(b, bias, q_ref, kv_ref, att_ref)

        def write(at, value):
            out_ref[at, b * QCOLS:(b + 1) * QCOLS, :] = value

        finish_block(b, rows, att_ref, wout_ref, (emb0_ref, emb1_ref), write)


def sides(lat_start, first_row, q, kv, left, right, w_qkv, w_out, emb0, emb1, centre):
    half, cols, width = emb0.shape
    return pl.pallas_call(
        sides_kernel,
        in_specs=[smem(), smem()] + [vmem()] * 9,
        out_specs=[vmem()] * 2,
        out_shape=[jax.ShapeDtypeStruct((2 * half, cols, width), jnp.bfloat16), pltpu.VMEM(kv.shape, kv.dtype)],
        input_output_aliases={3: 1},
        scratch_shapes=[pltpu.VMEM(q.shape, jnp.bfloat16)],
        compiler_params=params(LIMIT),
        cost_estimate=cost(9e9, 10e6, 2e6),
        name="sides",
    )(lat_start, first_row, q, kv, left, right, w_qkv, w_out, emb0, emb1, centre)[0]


def ring(count, stride, step):
    return [
        (base + i * stride, base + (i + step) % count * stride)
        for base in range(stride)
        for i in range(count)
    ]


def spread_kernel(plane_ref, w_ref, o_ref):
    half = o_ref.shape[2]
    for core in (0, 1):
        mine = w_ref[:, core * half:(core + 1) * half]
        for chip in range(o_ref.shape[0] // 2):
            o_ref[2 * chip + core] = mine


def quarter_of_weights(w_embed, place, lev):
    size, width = w_embed.shape[0] // PLANES, w_embed.shape[1]
    sent = pl.pallas_call(
        spread_kernel,
        grid_spec=pltpu.PrefetchScalarGridSpec(
            num_scalar_prefetch=1,
            grid=(1,),
            in_specs=[pl.BlockSpec((size, width), lambda i, plane: (plane[0], 0))],
            out_specs=pl.BlockSpec((lev, size, width // 2), lambda i, plane: (0, 0, 0)),
        ),
        out_shape=jax.ShapeDtypeStruct((lev, size, width // 2), w_embed.dtype),
        compiler_params=params(60),
        name="spread",
    )(place, w_embed)
    return lax.all_to_all(sent, "lev", split_axis=0, concat_axis=0, tiled=True)


def split_kernel(up_ref, down_ref, first_ref, second_ref):
    first_ref[...] = up_ref[...]
    second_ref[...] = down_ref[...]


def split(from_up, from_down):
    lev, size, half = from_up.shape
    block = (lev // 2, size, half)
    return pl.pallas_call(
        split_kernel,
        grid=(1,),
        in_specs=[pl.BlockSpec(block, lambda i: (0, 0, 0)), pl.BlockSpec(block, lambda i: (1, 0, 0))],
        out_specs=[pl.BlockSpec(block, lambda i: (0, 0, 0))] * 2,
        out_shape=[jax.ShapeDtypeStruct(block, from_up.dtype)] * 2,
        compiler_params=params(LIMIT),
        cost_estimate=cost(SPLIT_FLOPS, 4 * from_up.size),
        name="split",
    )(from_up, from_down)


def weight_pieces(own, lat):
    stride = lat // PLANES
    up, down = ring(PLANES, stride, 1), ring(PLANES, stride, -1)
    near = [lax.ppermute(own, "lat", up), lax.ppermute(own, "lat", down)]
    first, second = split(*near)
    far = [lax.ppermute(first, "lat", up), lax.ppermute(second, "lat", down)]
    pieces = [own] + near + far
    swap = [(i, i ^ 1) for i in range(own.shape[0])]
    return pieces + [lax.ppermute(piece, "lev", swap) for piece in pieces]


def per_device(
    fields, level_group, lat_start, w_embed, group_bias, group_gain, norm_gain, w_qkv, w_out
):
    rows = fields.shape[0]
    lev = lax.axis_size("lev")
    lat = lax.axis_size("lat")
    plane = lax.axis_index("lat") // (lat // PLANES)
    place = jnp.stack([plane, lax.axis_index("lev") % 2]).astype(jnp.int32)
    own = quarter_of_weights(w_embed, plane.astype(jnp.int32).reshape(1), lev)
    turned = jnp.transpose(fields, (0, 2, 1))
    pick = picks(level_group, lev, group_bias.shape[0])
    first_row = (lax.axis_index("lat") * rows).astype(jnp.int32).reshape(1)
    up = [(i, i + 1) for i in range(lat - 1)]
    down = [(b, a) for a, b in up]
    right_way = [(i, (i + 1) % lev) for i in range(lev)]
    left_way = [(b, a) for a, b in right_way]

    packed = [pack(turned, lev, c) for c in range(rows // CHUNK)]
    norm_gain = norm_gain[None, :]
    *packed, own, pick, place, norm_gain = lax.optimization_barrier((*packed, own, pick, place, norm_gain))
    w_all = weight_pieces(own, lat)
    emb, normed, low, high = [], [], [], []
    for c in range(rows // CHUNK):
        if c > 0:
            packed[c] = held
        moved = lax.all_to_all(packed[c], "lev", split_axis=0, concat_axis=0, tiled=True)
        if c == 0:
            held, *w_all[5:8] = lax.optimization_barrier((packed[1], *w_all[5:8]))
        e, n, kept = embed(moved, place, w_all, pick, group_bias, group_gain, norm_gain)
        w_all = [kept]
        emb.append(e)
        normed.append(n)
        if c % 2 == 0:
            low.append(lax.ppermute(n, "lat", up))
            high.append(lax.ppermute(n, "lat", down))
        else:
            high.append(lax.ppermute(n, "lat", down))
            low.append(lax.ppermute(n, "lat", up))

    def strips(tall):
        left = lax.ppermute(jnp.concatenate([t[:, -STRIP:] for t in tall], axis=0), "lev", right_way)
        right = lax.ppermute(jnp.concatenate([t[:, :STRIP] for t in tall], axis=0), "lev", left_way)
        return left, right

    low[0], high[0], normed[1] = lax.optimization_barrier((low[0], high[0], normed[1]))
    left, right = strips([low[0], normed[0], normed[1], high[0]])
    q, kv = project(normed[0], normed[1], low[0], high[0], w_qkv)
    high[1], low[1], q = lax.optimization_barrier((high[1], low[1], q))
    last_left, last_right = strips([low[1], high[1]])
    kv, centre = middle(
        lat_start, first_row, q, kv, low[1], high[1], left, right, w_qkv, w_out, emb[0], emb[1]
    )
    return sides(lat_start, first_row, q, kv, last_left, last_right, w_qkv, w_out, emb[0], emb[1], centre)


def solution(mesh):
    return jax.shard_map(
        per_device,
        mesh=mesh,
        in_specs=(P("lat", None, "lev"), P(), P(), P("lev", None), P(), P(), P(), P(), P()),
        out_specs=P("lat", "lev", None),
        check_vma=False,
    )
```

```python
import functools

import jax
import jax.numpy as jnp
from jax import lax
from jax.experimental import pallas as pl
from jax.experimental.pallas import tpu as pltpu
from jax.sharding import PartitionSpec as P

DH = 64
IN_LEV = 24
WIN = 13
LAT_REACH = 8
STRIP = 8
QCOLS = 16
KCOLS = QCOLS + 2 * STRIP
PLANES = 4
CHUNK = 4
SOURCES = 4
MASKED = -1e30
PART = 256
SPLIT_FLOPS = 18e9
FIRST_FLOPS = 16e9
FIRST_LIMIT = 56
NEXT_LIMIT = 50
LIMIT = 36


def params(mib):
    return pltpu.CompilerParams(vmem_limit_bytes=mib << 20)


def cost(flops, nbytes, trans=0):
    return pl.CostEstimate(flops=int(flops), bytes_accessed=int(nbytes), transcendentals=int(trans))


def smem():
    return pl.BlockSpec(memory_space=pltpu.SMEM)


def vmem():
    return pl.BlockSpec(memory_space=pltpu.VMEM)


def pack_kernel(x_ref, o_ref):
    rows, width, lon_all = x_ref.shape
    lev = o_ref.shape[0]
    cols = lon_all // lev
    tokens = rows * cols

    def put(block, first):
        turned = block.T.reshape(lev, cols, 128)
        o_ref[:, first:first + cols, :] = turned

    for r in range(rows):
        put(x_ref[r, :128, :], r * cols)
    for r in range(rows // 2):
        both = jnp.concatenate([x_ref[r, 128:, :], x_ref[r + rows // 2, 128:, :]], axis=0)
        put(both, tokens + r * cols)


def pack(turned, lev, chunk):
    _, width, lon_all = turned.shape
    tokens = CHUNK * lon_all // lev
    return pl.pallas_call(
        pack_kernel,
        grid=(1,),
        in_specs=[pl.BlockSpec((CHUNK, width, lon_all), lambda i: (chunk, 0, 0))],
        out_specs=pl.BlockSpec((lev, tokens + tokens // 2, 128), lambda i: (0, 0, 0)),
        out_shape=jax.ShapeDtypeStruct((lev, tokens + tokens // 2, 128), turned.dtype),
        compiler_params=params(60),
        cost_estimate=cost(0, 2 * turned.size),
        name="pack",
    )(turned)


def weight_rows(w_ref, s, first, last):
    size = w_ref.shape[2]
    out = []
    for quarter in range(w_ref.shape[1]):
        low, high = max(first - quarter * size, 0), min(last - quarter * size, size)
        if low < high:
            out.append((s, quarter, low, high))
    return out


def embed_body(x_ref, w_ref, pick_ref, bias_ref, gain_ref, norm_ref, emb_ref, normed_ref, xs_ref, sum_ref, before):
    groups, width = bias_ref.shape
    lev, quarters, size, _ = w_ref.shape
    per = quarters * size
    part = PART
    tokens = xs_ref.shape[0] // groups
    span = SOURCES * per

    for c in range(lev // SOURCES):
        here = range(c * SOURCES, (c + 1) * SOURCES)
        main = [x_ref[s, :tokens, :] for s in here]
        low = jnp.concatenate([x_ref[s, tokens:, :64] for s in here], axis=1)
        high = jnp.concatenate([x_ref[s, tokens:, 64:] for s in here], axis=1)
        x = jnp.concatenate(main + [jnp.concatenate([low, high], axis=0)], axis=1)
        for g in range(groups):
            xs_ref[g * tokens:(g + 1) * tokens, c * span:(c + 1) * span] = x * pick_ref[g:g + 1, c * span:(c + 1) * span]

    for j in range(width // part):
        before(j)
        cols = slice(j * part, (j + 1) * part)
        acc = None
        for c in range(lev // SOURCES):
            here = range(c * SOURCES, (c + 1) * SOURCES)
            rows = [r for s in here for r in weight_rows(w_ref, s, 0, 128)]
            rows += [r for s in here for r in weight_rows(w_ref, s, 128, per)]
            w = jnp.concatenate([w_ref[s, quarter, low:high, cols] for s, quarter, low, high in rows], axis=0)
            term = jnp.dot(xs_ref[:, c * span:(c + 1) * span], w, preferred_element_type=jnp.float32)
            acc = term if acc is None else acc + term
        total = jnp.zeros((tokens, part), jnp.float32)
        for g in range(groups):
            v = acc[g * tokens:(g + 1) * tokens] + bias_ref[g:g + 1, cols]
            total += v / (1.0 + jnp.exp(-v)) * gain_ref[g:g + 1, cols]
        sum_ref[:, cols] = total

    emb = sum_ref[...].astype(jnp.bfloat16)
    wide = emb.astype(jnp.float32)
    inv = lax.rsqrt(jnp.mean(wide * wide, axis=-1, keepdims=True) + 1e-05)
    emb_ref[...] = emb.reshape(emb_ref.shape)
    normed_ref[...] = (wide * inv * norm_ref[...]).astype(jnp.bfloat16).reshape(normed_ref.shape)


def embed_first_kernel(place_ref, x_ref, pick_ref, bias_ref, gain_ref, norm_ref, *refs):
    pieces, (emb_ref, normed_ref, kept_ref, xs_ref, sum_ref, w_ref, sem) = refs[:10], refs[10:]
    lev, quarters, _, width = w_ref.shape
    half = width // 2
    plane, core = place_ref[0], place_ref[1]
    spots = ((0, 0, lev), (quarters - 1, 0, lev), (1, 0, lev), (2, 0, lev // 2), (2, lev // 2, lev))

    def loads(side, sibling):
        out = []
        for n, (ahead, first, last) in enumerate(spots):
            spot = w_ref.at[first:last, lax.rem(plane + ahead, quarters), :, side * half:(side + 1) * half]
            out.append(pltpu.make_async_copy(pieces[sibling * 5 + n], spot, sem.at[side * 5 + n]))
        return out

    for own_side in (0, 1):

        @pl.when(core == own_side)
        def _():
            for side in (0, 1):
                for load in loads(side, 0 if side == own_side else 1):
                    load.start()

    keep = pltpu.make_async_copy(w_ref, kept_ref, sem.at[10])

    def before(j):
        if j < 2:
            for load in loads(j, j):
                load.wait()
        if j == 1:
            keep.start()

    embed_body(x_ref, w_ref, pick_ref, bias_ref, gain_ref, norm_ref, emb_ref, normed_ref, xs_ref, sum_ref, before)
    keep.wait()


def embed_next_kernel(x_ref, pick_ref, bias_ref, gain_ref, norm_ref, kept_ref, emb_ref, normed_ref, xs_ref, sum_ref, w_ref, sem):
    loads = []
    for j in range(w_ref.shape[3] // PART):
        cols = slice(j * PART, (j + 1) * PART)
        loads.append(pltpu.make_async_copy(kept_ref.at[:, :, :, cols], w_ref.at[:, :, :, cols], sem.at[j]))
        loads[j].start()
    embed_body(
        x_ref, w_ref, pick_ref, bias_ref, gain_ref, norm_ref, emb_ref, normed_ref, xs_ref, sum_ref, lambda j: loads[j].wait()
    )


def embed(moved, place, w_all, pick, bias, gain, norm_gain):
    lev = moved.shape[0]
    tokens = moved.shape[1] * 2 // 3
    groups, width = bias.shape
    depth = pick.shape[1]
    cols = tokens // CHUNK
    out_shape = [jax.ShapeDtypeStruct((CHUNK, cols, width), jnp.bfloat16)] * 2
    size = w_all[0].shape[-2]
    kept = jax.ShapeDtypeStruct((lev, depth // lev // size, size, width), jnp.bfloat16)
    scratch = [
        pltpu.VMEM((groups * tokens, depth), jnp.bfloat16),
        pltpu.VMEM((tokens, width), jnp.float32),
        pltpu.VMEM(kept.shape, kept.dtype),
    ]
    far = pl.BlockSpec(memory_space=pl.ANY)
    common = dict(
        compiler_params=params(FIRST_LIMIT if len(w_all) > 1 else NEXT_LIMIT),
        cost_estimate=cost(FIRST_FLOPS if len(w_all) > 1 else 2 * tokens * depth * width * groups, depth * width * 2 + tokens * depth * 2),
    )
    shared = (moved, pick, bias, gain, norm_gain)
    if len(w_all) > 1:
        return pl.pallas_call(
            embed_first_kernel,
            in_specs=[smem()] + [vmem()] * 5 + [far] * 10,
            out_specs=[vmem()] * 2 + [far],
            out_shape=out_shape + [kept],
            scratch_shapes=scratch + [pltpu.SemaphoreType.DMA((11,))],
            name="embed_first",
            **common,
        )(place, *shared, *w_all)
    return (
        *pl.pallas_call(
            embed_next_kernel,
            in_specs=[vmem()] * 5 + [far],
            out_specs=[vmem()] * 2,
            out_shape=out_shape,
            scratch_shapes=scratch + [pltpu.SemaphoreType.DMA((width // PART,))],
            name="embed_next",
            **common,
        )(*shared, *w_all),
        w_all[0],
    )


def picks(level_group, lev, groups):
    row_groups = jnp.repeat(level_group, IN_LEV).reshape(lev // SOURCES, SOURCES, -1)
    steps = row_groups.shape[0]
    order = jnp.concatenate(
        [row_groups[:, :, :128].reshape(steps, -1), row_groups[:, :, 128:].reshape(steps, -1)], axis=1
    ).reshape(-1)
    return (order[None, :] == jnp.arange(groups, dtype=jnp.int32)[:, None]).astype(jnp.bfloat16)


def keys_values(x, w):
    n = x.shape[0] * x.shape[1]
    out = jnp.dot(x.reshape(n, x.shape[2]), w, preferred_element_type=jnp.float32).astype(jnp.bfloat16)
    return out.reshape(x.shape[0], x.shape[1], w.shape[1])


def queries_of(x, w):
    rows, cols, width = x.shape
    q = jnp.dot(x.reshape(rows * cols, width), w, preferred_element_type=jnp.float32).astype(jnp.bfloat16)
    return (q * jnp.bfloat16(DH ** (-0.5))).reshape(rows, cols, width)


def project_kernel(own0_ref, own1_ref, low_ref, high_ref, w_ref, q_ref, kv_ref):
    rows, cols, width = low_ref.shape
    inner = slice(STRIP, STRIP + cols)
    for c, ref in enumerate((own0_ref, own1_ref)):
        q = queries_of(ref[...], w_ref[:, :width])
        for b in range(cols // QCOLS):
            q_ref[b, c * rows * QCOLS:(c + 1) * rows * QCOLS, :] = q[:, b * QCOLS:(b + 1) * QCOLS, :].reshape(rows * QCOLS, width)
    for ref, at in ((own0_ref, 2), (own1_ref, 3), (low_ref, 0), (high_ref, 4)):
        kv_ref[at * rows:(at + 1) * rows, inner, :] = keys_values(ref[...], w_ref[:, width:])


def project(own0, own1, low, high, w_qkv):
    rows, cols, width = low.shape
    return pl.pallas_call(
        project_kernel,
        in_specs=[vmem()] * 5,
        out_specs=[vmem()] * 2,
        out_shape=[
            pltpu.VMEM((cols // QCOLS, 2 * rows * QCOLS, width), jnp.bfloat16),
            pltpu.VMEM((6 * rows, cols + 2 * STRIP, 2 * width), jnp.bfloat16),
        ],
        compiler_params=params(LIMIT),
        cost_estimate=cost(2 * low.size * 10 * width, w_qkv.size * 2 + low.size * 24),
        name="project",
    )(own0, own1, low, high, w_qkv)


def window_bias(start_ref, first_ref, rows):
    keys = 3 * rows * KCOLS
    key = lax.broadcasted_iota(jnp.int32, (QCOLS, keys), 1)
    key_row = key // KCOLS
    shift = key % KCOLS - lax.broadcasted_iota(jnp.int32, (QCOLS, keys), 0)
    near = STRIP - WIN // 2
    col_ok = (shift >= near) & (shift < near + WIN)
    first_row = first_ref[0]
    bias = []
    for r in range(rows):
        start = start_ref[first_row + r] - first_row + LAT_REACH
        ok = col_ok & (key_row >= start) & (key_row < start + WIN)
        bias.append(jnp.where(ok, 0.0, MASKED))
    return jnp.concatenate(bias + bias, axis=0)


def attend_block(b, bias, q_ref, kv_ref, att_ref):
    _, queries, width = q_ref.shape
    keys = bias.shape[1]
    lane = lax.broadcasted_iota(jnp.int32, (queries, 128), 1)
    is_first = lane < DH
    ones = jnp.ones((keys, 128), jnp.bfloat16)
    band = slice(b * QCOLS, b * QCOLS + KCOLS)
    for p in range(width // 128):
        here = slice(p * 128, (p + 1) * 128)
        here_v = slice(width + p * 128, width + (p + 1) * 128)
        q = q_ref[b, :, here]
        zero = jnp.zeros_like(q)
        qq = jnp.concatenate([jnp.where(is_first, q, zero), jnp.where(is_first, zero, q)], axis=0)
        k = kv_ref[:, band, here].reshape(keys, 128)
        v = kv_ref[:, band, here_v].reshape(keys, 128)
        s = lax.dot_general(qq, k, (((1,), (1,)), ((), ())), preferred_element_type=jnp.float32) + bias
        e = jnp.exp(s - jnp.max(s, axis=-1, keepdims=True)).astype(jnp.bfloat16)
        o = jnp.dot(e, jnp.concatenate([v, ones], axis=1), preferred_element_type=jnp.float32)
        o = o[:, :128] / o[:, 128:]
        att_ref[b, :, here] = jnp.where(is_first, o[:queries], o[queries:]).astype(jnp.bfloat16)


def finish_block(b, rows, att_ref, wout_ref, emb_refs, write):
    mixed = jnp.dot(att_ref[b], wout_ref[...], preferred_element_type=jnp.float32)
    mixed = mixed.reshape(rows, QCOLS, mixed.shape[1])
    half = rows // 2
    for c, ref in enumerate(emb_refs):
        wide = ref[:, b * QCOLS:(b + 1) * QCOLS, :].astype(jnp.float32)
        write(slice(c * half, (c + 1) * half), (wide + mixed[c * half:(c + 1) * half]).astype(jnp.bfloat16))


def middle_kernel(start_ref, first_ref, q_ref, _, low_ref, high_ref, left_ref, right_ref, w_ref, wout_ref, emb0_ref, emb1_ref,
                  kv_ref, out_ref, att_ref):
    half, cols, width = low_ref.shape
    rows = 2 * half
    wkv = w_ref[:, width:]
    inner = slice(STRIP, STRIP + cols)
    kv_ref[half:rows, inner, :] = keys_values(low_ref[...], wkv)
    kv_ref[2 * rows + half:, inner, :] = keys_values(high_ref[...], wkv)
    bias = window_bias(start_ref, first_ref, rows)
    attend_block(1, bias, q_ref, kv_ref, att_ref)

    def write(at, value):
        out_ref[at] = value

    finish_block(1, rows, att_ref, wout_ref, (emb0_ref, emb1_ref), write)
    for side, at in ((left_ref, slice(0, STRIP)), (right_ref, slice(STRIP + cols, None))):
        strip = keys_values(side[...], wkv)
        kv_ref[:half, at, :] = strip[:half]
        kv_ref[rows:2 * rows, at, :] = strip[half:3 * half]
        kv_ref[2 * rows:2 * rows + half, at, :] = strip[3 * half:]


def middle(lat_start, first_row, q, kv, low, high, left, right, w_qkv, w_out, emb0, emb1):
    half, cols, width = low.shape
    return pl.pallas_call(
        middle_kernel,
        in_specs=[smem(), smem()] + [vmem()] * 10,
        out_specs=[vmem()] * 2,
        out_shape=[pltpu.VMEM(kv.shape, kv.dtype), pltpu.VMEM((2 * half, QCOLS, width), jnp.bfloat16)],
        input_output_aliases={3: 0},
        scratch_shapes=[pltpu.VMEM(q.shape, jnp.bfloat16)],
        compiler_params=params(LIMIT),
        cost_estimate=cost(8e9, 10e6, 1e6),
        name="middle",
    )(lat_start, first_row, q, kv, low, high, left, right, w_qkv, w_out, emb0, emb1)


def sides_kernel(start_ref, first_ref, q_ref, _, left_ref, right_ref, w_ref, wout_ref, emb0_ref, emb1_ref, middle_ref,
                 out_ref, kv_ref, att_ref):
    rows, cols, width = out_ref.shape
    half = rows // 2
    blocks = q_ref.shape[0]
    wkv = w_ref[:, width:]
    for side, at in ((left_ref, slice(0, STRIP)), (right_ref, slice(STRIP + cols, None))):
        strip = keys_values(side[...], wkv)
        kv_ref[half:rows, at, :] = strip[:half]
        kv_ref[2 * rows + half:, at, :] = strip[half:]
    bias = window_bias(start_ref, first_ref, rows)
    out_ref[:, QCOLS:2 * QCOLS, :] = middle_ref[...]
    for b in (0, blocks - 1):
        attend_block(b, bias, q_ref, kv_ref, att_ref)

        def write(at, value):
            out_ref[at, b * QCOLS:(b + 1) * QCOLS, :] = value

        finish_block(b, rows, att_ref, wout_ref, (emb0_ref, emb1_ref), write)


def sides(lat_start, first_row, q, kv, left, right, w_qkv, w_out, emb0, emb1, centre):
    half, cols, width = emb0.shape
    return pl.pallas_call(
        sides_kernel,
        in_specs=[smem(), smem()] + [vmem()] * 9,
        out_specs=[vmem()] * 2,
        out_shape=[jax.ShapeDtypeStruct((2 * half, cols, width), jnp.bfloat16), pltpu.VMEM(kv.shape, kv.dtype)],
        input_output_aliases={3: 1},
        scratch_shapes=[pltpu.VMEM(q.shape, jnp.bfloat16)],
        compiler_params=params(LIMIT),
        cost_estimate=cost(9e9, 10e6, 2e6),
        name="sides",
    )(lat_start, first_row, q, kv, left, right, w_qkv, w_out, emb0, emb1, centre)[0]


def ring(count, stride, step):
    return [
        (base + i * stride, base + (i + step) % count * stride)
        for base in range(stride)
        for i in range(count)
    ]


def spread_kernel(plane_ref, w_ref, o_ref):
    size, half = o_ref.shape[1:]
    rows = pl.ds(pl.multiple_of(plane_ref[0] * size, size), size)
    for core in (0, 1):
        mine = w_ref[rows, core * half:(core + 1) * half]
        for chip in range(o_ref.shape[0] // 2):
            o_ref[2 * chip + core] = mine


def quarter_of_weights(w_embed, place, lev):
    size, width = w_embed.shape[0] // PLANES, w_embed.shape[1]
    sent = pl.pallas_call(
        spread_kernel,
        in_specs=[smem(), vmem()],
        out_specs=vmem(),
        out_shape=jax.ShapeDtypeStruct((lev, size, width // 2), w_embed.dtype),
        compiler_params=params(60),
        name="spread",
    )(place, w_embed)
    return lax.all_to_all(sent, "lev", split_axis=0, concat_axis=0, tiled=True)


def split_kernel(up_ref, down_ref, first_ref, second_ref):
    first_ref[...] = up_ref[...]
    second_ref[...] = down_ref[...]


def split(from_up, from_down):
    lev, size, half = from_up.shape
    block = (lev // 2, size, half)
    return pl.pallas_call(
        split_kernel,
        grid=(1,),
        in_specs=[pl.BlockSpec(block, lambda i: (0, 0, 0)), pl.BlockSpec(block, lambda i: (1, 0, 0))],
        out_specs=[pl.BlockSpec(block, lambda i: (0, 0, 0))] * 2,
        out_shape=[jax.ShapeDtypeStruct(block, from_up.dtype)] * 2,
        compiler_params=params(LIMIT),
        cost_estimate=cost(SPLIT_FLOPS, 4 * from_up.size),
        name="split",
    )(from_up, from_down)


def weight_pieces(own, lat):
    stride = lat // PLANES
    up, down = ring(PLANES, stride, 1), ring(PLANES, stride, -1)
    near = [lax.ppermute(own, "lat", up), lax.ppermute(own, "lat", down)]
    first, second = split(*near)
    far = [lax.ppermute(first, "lat", up), lax.ppermute(second, "lat", down)]
    pieces = [own] + near + far
    swap = [(i, i ^ 1) for i in range(own.shape[0])]
    return pieces + [lax.ppermute(piece, "lev", swap) for piece in pieces]


def per_device(
    fields, level_group, lat_start, w_embed, group_bias, group_gain, norm_gain, w_qkv, w_out
):
    rows = fields.shape[0]
    lev = lax.axis_size("lev")
    lat = lax.axis_size("lat")
    plane = lax.axis_index("lat") // (lat // PLANES)
    place = jnp.stack([plane, lax.axis_index("lev") % 2]).astype(jnp.int32)
    own = quarter_of_weights(w_embed, plane.astype(jnp.int32).reshape(1), lev)
    turned = jnp.transpose(fields, (0, 2, 1))
    pick = picks(level_group, lev, group_bias.shape[0])
    first_row = (lax.axis_index("lat") * rows).astype(jnp.int32).reshape(1)
    up = [(i, i + 1) for i in range(lat - 1)]
    down = [(b, a) for a, b in up]
    right_way = [(i, (i + 1) % lev) for i in range(lev)]
    left_way = [(b, a) for a, b in right_way]

    packed = [pack(turned, lev, c) for c in range(rows // CHUNK)]
    norm_gain = norm_gain[None, :]
    *packed, own, pick, place, norm_gain = lax.optimization_barrier((*packed, own, pick, place, norm_gain))
    w_all = weight_pieces(own, lat)
    emb, normed, low, high = [], [], [], []
    for c in range(rows // CHUNK):
        if c > 0:
            packed[c] = held
        moved = lax.all_to_all(packed[c], "lev", split_axis=0, concat_axis=0, tiled=True)
        if c == 0:
            held, *w_all[5:8] = lax.optimization_barrier((packed[1], *w_all[5:8]))
        e, n, kept = embed(moved, place, w_all, pick, group_bias, group_gain, norm_gain)
        w_all = [kept]
        emb.append(e)
        normed.append(n)
        if c % 2 == 0:
            low.append(lax.ppermute(n, "lat", up))
            high.append(lax.ppermute(n, "lat", down))
        else:
            high.append(lax.ppermute(n, "lat", down))
            low.append(lax.ppermute(n, "lat", up))

    def strips(tall):
        left = lax.ppermute(jnp.concatenate([t[:, -STRIP:] for t in tall], axis=0), "lev", right_way)
        right = lax.ppermute(jnp.concatenate([t[:, :STRIP] for t in tall], axis=0), "lev", left_way)
        return left, right

    low[0], high[0], normed[1] = lax.optimization_barrier((low[0], high[0], normed[1]))
    left, right = strips([low[0], normed[0], normed[1], high[0]])
    q, kv = project(normed[0], normed[1], low[0], high[0], w_qkv)
    high[1], low[1], q = lax.optimization_barrier((high[1], low[1], q))
    last_left, last_right = strips([low[1], high[1]])
    kv, centre = middle(
        lat_start, first_row, q, kv, low[1], high[1], left, right, w_qkv, w_out, emb[0], emb[1]
    )
    return sides(lat_start, first_row, q, kv, last_left, last_right, w_qkv, w_out, emb[0], emb[1], centre)


def solution(mesh):
    return jax.shard_map(
        per_device,
        mesh=mesh,
        in_specs=(P("lat", None, "lev"), P(), P(), P("lev", None), P(), P(), P(), P(), P()),
        out_specs=P("lat", "lev", None),
        check_vma=False,
    )
```
